32 devices in a mesh: dp: 4 (over y, core), mp: 8 (over z, x).
Axes of the slice: x: 2, y: 2, z: 4, core: 2. Of those that a mesh axis runs over, the one named last changes fastest.
Arguments:
- tokens_in: bfloat16 [80, 256, 1024], P('dp', 'mp'), may hold values from -6 to 6
- segment_ids: int32 [80, 256], P('dp'), may hold values from 0 to 64, as said below
- attn_gain: float32 [1024], replicated, may hold values from 0.1 to 1.9
- attn_shift: float32 [1024], replicated, may hold values from -4 to 4
- qkv_weight: bfloat16 [1024, 3072], P(None, 'mp'), may hold values from -0.1875 to 0.1875
- qkv_bias: float32 [2, 1024], P(None, 'mp'), may hold values from -4 to 4
- out_weight: bfloat16 [1024, 1024], P('mp'), may hold values from -0.5 to 0.5
- out_bias: float32 [1024], replicated, may hold values from -4 to 4
- mlp_gain: float32 [1024], replicated, may hold values from 0.1 to 1.9
- mlp_shift: float32 [1024], replicated, may hold values from -4 to 4
- up_weight: bfloat16 [1024, 4096], P(None, 'mp'), may hold values from -0.1875 to 0.1875
- up_bias: float32 [4096], P('mp'), may hold values from -4 to 4
- down_weight: bfloat16 [4096, 1024], P('mp'), may hold values from -0.125 to 0.125
- down_bias: float32 [1024], replicated, may hold values from -4 to 4
- cotangent: bfloat16 [80, 256, 1024], P('dp', 'mp'), may hold values from -6 to 6
Outputs:
- block_out: bfloat16 [80, 256, 1024], P('dp', 'mp')
- tokens_grad: float32 [80, 256, 1024], P('dp', 'mp')
- attn_gain_grad: float32 [1024], replicated
- attn_shift_grad: float32 [1024], replicated
- qkv_weight_grad: float32 [1024, 3072], P(None, 'mp')
- qkv_bias_grad: float32 [2, 1024], P(None, 'mp')
- out_weight_grad: float32 [1024, 1024], P('mp')
- out_bias_grad: float32 [1024], replicated
- mlp_gain_grad: float32 [1024], replicated
- mlp_shift_grad: float32 [1024], replicated
- up_weight_grad: float32 [1024, 4096], P(None, 'mp')
- up_bias_grad: float32 [4096], P('mp')
- down_weight_grad: float32 [4096, 1024], P('mp')
- down_bias_grad: float32 [1024], replicated
The draws below stay inside these ranges and needn't reach their ends.
Inputs may be any that keep to these rules, and one draw needn't show every extreme that they name: `segment_ids`: in each row, images occupy runs of positions with one nonzero id, the ids rising by one from 1 along the row; every row but the first ends in 1 to 32 padding positions with id 0. A token attends only to tokens with its own id.
All inputs are finite; a program needn't handle non-finite values.
Results may differ from the reference program's by a relative error of at most 0.012.
The reference program's roundings to bfloat16 on the way count: a program that leaves them out, or rounds other values in their place, can miss the bound.
Values may be sent and summed in bfloat16 or wider, within the bound.
A program may use at most 192 MiB of HBM per device.

```python
import math
import jax
import jax.numpy as jnp
from jax import lax

D = 1024
H = 16
HEAD_DIM = 64
FF = 4096
L = 256
ROWS = 80


def draw_segment_ids(key, part):
    key_breaks = jax.random.fold_in(key, 11)
    key_padding = jax.random.fold_in(key, 23)
    places = lax.broadcasted_iota(jnp.int32, (ROWS, L), 1)
    row_index = lax.broadcasted_iota(jnp.int32, (ROWS, L), 0)
    random_breaks = jax.random.randint(key_breaks, (ROWS, L), 0, max(2, L // 5)) == 0
    regular_breaks = places % 4 == 0
    breaks = jnp.where(row_index == 0, regular_breaks, random_breaks)
    breaks = jnp.logical_and(breaks, places > 0)
    labels = 1 + jnp.cumsum(breaks.astype(jnp.int32), axis=1)
    labels = jnp.minimum(labels, L // 4)
    padding = jax.random.randint(key_padding, (ROWS, 1), 1, L // 8 + 1)
    first_row = lax.broadcasted_iota(jnp.int32, (ROWS, 1), 0) == 0
    padding = jnp.where(first_row, 0, padding)
    return jnp.where(places >= L - padding, 0, labels).astype(jnp.int32)


def block_levels(stream_key, extent, shards, least, largest):
    loudness, own = 1.0, jax.random.fold_in(stream_key, 6)
    for axis_at, blocks in shards:
        heights = jnp.exp(jax.random.uniform(jax.random.fold_in(own, axis_at), (blocks,), jnp.float32, least / len(shards), largest / len(shards)))
        loudness = loudness * jnp.repeat(heights, extent[axis_at] // blocks).reshape([-1 if axis == axis_at else 1 for axis in range(len(extent))])
    return loudness


def gaussian(own_key, extent, width, most, pieces=(), dtype=jnp.bfloat16):
    drawn = jax.random.normal(own_key, extent, jnp.float32) * width
    if len(pieces) > 0:
        drawn = block_levels(own_key, extent, pieces, -0.22, 0.18) * drawn
    return jnp.clip(drawn, min=-most, max=most).astype(dtype)


def setup_inputs(seed: int = 0) -> dict:
    arg_keys = jax.random.split(jax.random.key(seed), 16)
    tokens_in = gaussian(arg_keys[0], (ROWS, L, D), 1.0, 6.0, ((0, 4), (1, 8)))
    segment_ids = draw_segment_ids(jax.random.fold_in(arg_keys[15], 71), 0)
    attn_gain = jnp.clip(1.0 + 0.18 * jax.random.normal(arg_keys[2], (D,), jnp.float32), 0.1, 1.9)
    attn_shift = gaussian(arg_keys[3], (D,), 0.3, 4.0, (), jnp.float32)
    qkv_weight = gaussian(arg_keys[4], (D, 3 * D), D ** -0.5, 0.1875, ((1, 8),))
    qkv_bias = gaussian(arg_keys[5], (2, D), 0.5, 4.0, ((1, 8),), jnp.float32)
    out_weight = gaussian(arg_keys[6], (D, D), (D // 8) ** -0.5, 0.5, ((0, 8),))
    out_bias = gaussian(arg_keys[7], (D,), 0.5, 4.0, (), jnp.float32)
    mlp_gain = jnp.clip(1.0 + 0.18 * jax.random.normal(arg_keys[8], (D,), jnp.float32), 0.1, 1.9)
    mlp_shift = gaussian(arg_keys[9], (D,), 0.3, 4.0, (), jnp.float32)
    up_weight = gaussian(arg_keys[10], (D, FF), D ** -0.5, 0.1875, ((1, 8),))
    up_bias = gaussian(arg_keys[11], (FF,), 0.5, 4.0, ((0, 8),), jnp.float32)
    down_weight = gaussian(arg_keys[12], (FF, D), (FF // 2) ** -0.5, 0.125, ((0, 8),))
    down_bias = gaussian(arg_keys[13], (D,), 0.5, 4.0, (), jnp.float32)
    cotangent = gaussian(arg_keys[14], (ROWS, L, D), 1.0, 6.0, ((0, 4), (1, 8)))
    return {"tokens_in": tokens_in, "segment_ids": segment_ids, "attn_gain": attn_gain, "attn_shift": attn_shift, "qkv_weight": qkv_weight, "qkv_bias": qkv_bias, "out_weight": out_weight, "out_bias": out_bias, "mlp_gain": mlp_gain, "mlp_shift": mlp_shift, "up_weight": up_weight, "up_bias": up_bias, "down_weight": down_weight, "down_bias": down_bias, "cotangent": cotangent}


EPS = 1e-06
MASKED = -1000000000.0

@jax.custom_vjp
def low(v):
    return lax.optimization_barrier(v.astype(jnp.bfloat16)).astype(jnp.float32)

@jax.custom_vjp
def low_back(v):
    return v

def low_keep(v):
    return (low(v), None)

def low_pass(kept, grad):
    return (grad,)

def back_keep(v):
    return (v, None)

def back_low(kept, grad):
    return (low(grad),)
low.defvjp(low_keep, low_pass)
low_back.defvjp(back_keep, back_low)

def layer_norm(values, gain_vec, shift_vec):
    row_mean = lax.optimization_barrier(jnp.mean(values, axis=-1, keepdims=True))
    centred = values - row_mean
    row_var = lax.optimization_barrier(jnp.mean(centred * centred, axis=-1, keepdims=True))
    return centred * lax.rsqrt(row_var + EPS) * gain_vec + shift_vec

def attend_rows(blocks):
    query_vecs, key_vecs, value_vecs, labels = blocks
    raw_scores = low_back(jnp.einsum('pqhe,pkhe->phqk', query_vecs, key_vecs, precision=lax.Precision.HIGHEST))
    allowed = (labels[:, :, None] == labels[:, None, :])[:, None]
    scores = jnp.where(allowed, raw_scores * HEAD_DIM ** (-0.5), MASKED)
    row_top = lax.optimization_barrier(jnp.max(scores, axis=-1, keepdims=True))
    raised = jnp.exp(scores - row_top)
    attn_probs = low(raised / lax.optimization_barrier(jnp.sum(raised, axis=-1, keepdims=True)))
    return jnp.einsum('phqk,pkhe->pqhe', attn_probs, value_vecs, precision=lax.Precision.HIGHEST)

def reference(tokens_in, segment_ids, attn_gain, attn_shift, qkv_weight, qkv_bias, out_weight, out_bias, mlp_gain, mlp_shift, up_weight, up_bias, down_weight, down_bias, cotangent):
    rows_per = math.gcd(ROWS, max(1, 4096 // L))
    label_blocks = segment_ids.reshape(ROWS // rows_per, rows_per, L)
    highest = lax.Precision.HIGHEST

    def forward(params):
        tokens_f, gain_one, shift_one, qkv_full, qkv_vec, out_full, out_vec, gain_two, shift_two, up_full, up_vec, down_full, down_vec = params
        normed_one = low(layer_norm(tokens_f, gain_one, shift_one)).reshape(ROWS * L, D)
        bias_parts = qkv_vec.reshape(2, H, HEAD_DIM)
        full_bias = jnp.stack([bias_parts[0], jnp.zeros((H, HEAD_DIM), jnp.float32), bias_parts[1]], axis=1).reshape(3 * D)
        projected = low(low_back(jnp.dot(normed_one, qkv_full, precision=highest) + full_bias))
        head_split = projected.reshape(ROWS // rows_per, rows_per, L, H, 3, HEAD_DIM)
        attn_blocks = lax.map(jax.checkpoint(attend_rows), (head_split[..., 0, :], head_split[..., 1, :], head_split[..., 2, :], label_blocks))
        attn_flat = low(low_back(attn_blocks.reshape(ROWS * L, D)))
        branch_one = low_back(jnp.dot(attn_flat, out_full, precision=highest)).reshape(ROWS, L, D)
        hidden = tokens_f + branch_one + out_vec
        normed_two = low(layer_norm(hidden, gain_two, shift_two)).reshape(ROWS * L, D)
        pre_act = low_back(jnp.dot(normed_two, up_full, precision=highest) + up_vec)
        act_low = low(jax.nn.gelu(pre_act, approximate=False))
        branch_two = low_back(jnp.dot(act_low, down_full, precision=highest)).reshape(ROWS, L, D)
        return hidden + branch_two + down_vec
    floats = (tokens_in.astype(jnp.float32), attn_gain, attn_shift, qkv_weight.astype(jnp.float32), qkv_bias, out_weight.astype(jnp.float32), out_bias, mlp_gain, mlp_shift, up_weight.astype(jnp.float32), up_bias, down_weight.astype(jnp.float32), down_bias)
    result, pullback = jax.vjp(forward, floats)
    gradients = pullback(cotangent.astype(jnp.float32))[0]
    return (result.astype(jnp.bfloat16), gradients[0], gradients[1], gradients[2], gradients[3], gradients[4], gradients[5], gradients[6], gradients[7], gradients[8], gradients[9], gradients[10], gradients[11], gradients[12])
```

```python
import functools
import math

import jax
import jax.numpy as jnp
from jax import lax
from jax.experimental import pallas as pl
from jax.experimental.pallas import tpu as pltpu
from jax.sharding import PartitionSpec as P

HEAD_DIM = 64
EPS = 1e-06
MASKED = -1000000000.0
MESH = pl.DeviceIdType.MESH
BF = jnp.bfloat16
F32 = jnp.float32


class Plan:
    def __init__(self, dp, mp, rows_dev, tok_local, seq_len):
        self.dp, self.mp, self.rows_dev, self.tok, self.seq = dp, mp, rows_dev, tok_local, seq_len
        self.share = mp // math.gcd(rows_dev, mp)
        self.group_rows = rows_dev * self.share // mp
        self.own = self.group_rows // self.share
        if self.share % 2 or dp % self.share or self.group_rows != self.own * self.share + 1:
            raise ValueError("unsupported sizes")
        self.groups = mp // self.share
        self.part = seq_len // self.share
        self.rows = self.own + 1

    def ring_at(self, p):
        p = lax.rem(p, self.mp)
        back = lax.div(p, self.mp // 2)
        return 2 * p * (1 - back) + (2 * self.mp - 1 - 2 * p) * back

    def place(self):
        d, m = lax.axis_index("dp"), lax.axis_index("mp")
        odd = lax.rem(m, 2)
        p = lax.div(m, 2) * (1 - odd) + (self.mp - 1 - lax.div(m, 2)) * odd
        return d, m, p


def greet(plan, d, m, others):
    barrier = pltpu.get_barrier_semaphore()
    base = lax.div(d, plan.share) * plan.share

    def one(i, carry):
        e, q = base + lax.div(i, plan.mp), lax.rem(i, plan.mp)

        @pl.when(jnp.logical_or(e != d, q != m))
        def _():
            pl.semaphore_signal(barrier, inc=1, device_id={"dp": e, "mp": q}, device_id_type=MESH)

        return carry

    lax.fori_loop(0, plan.share * plan.mp, one, 0)
    for e in others:
        pl.semaphore_signal(barrier, inc=1, device_id={"dp": e, "mp": m}, device_id_type=MESH)
    pl.semaphore_wait(barrier, plan.share * plan.mp - 1 + len(others))


def gather_kernel(
    plan, tok, cot, seg, w0, w1, w2, w3, tok3, cot3, seg3, g0, g1, g2, g3,
    tok_send, tok_recv, cot_send, cot_recv, seg_send, seg_recv, own_sem, ring_send, ring_recv, sib_send, sib_recv,
):
    n, share, own = plan.mp, plan.share, plan.own
    d, m, p = plan.place()
    core = lax.rem(d, 2)
    sib = d + 1 - 2 * core
    k = lax.rem(d, share)
    base = d - k
    shards, full = (w0, w1, w2, w3), (g0, g1, g2, g3)
    greet(plan, d, m, ())

    def quarter(w, c, way):
        rows = shards[w].shape[0] // 4
        return pl.ds(pl.multiple_of((2 * c + way) * rows, rows), rows)

    def ring(w, way, s, first=False):
        origin = m if first else plan.ring_at(p + n - s if way == 0 else p + s)
        rows = quarter(w, core, way)
        to = plan.ring_at(p + 1 if way == 0 else p + n - 1)
        return pltpu.make_async_remote_copy(
            shards[w].at[rows] if first else full[w].at[origin, rows],
            full[w].at[origin, rows],
            ring_send.at[w, way],
            ring_recv.at[w, way, s],
            device_id={"mp": to},
            device_id_type=MESH,
        )

    def sibling(w, way, s):
        origin = plan.ring_at(p + n - 1 - s if way == 0 else p + 1 + s)
        block = full[w].at[origin, quarter(w, core, way)]
        return pltpu.make_async_remote_copy(
            block, block, sib_send.at[w], sib_recv.at[w], device_id={"dp": sib}, device_id_type=MESH
        )

    for j in range(plan.groups):
        q = k * plan.groups + j
        for e in range(share):
            first = j * plan.group_rows
            at = lax.rem(m * plan.tok + plan.seq - e * plan.part, plan.seq)
            at = pl.multiple_of(at, plan.tok)
            mine = pl.ds(pl.multiple_of(m * plan.tok, plan.tok), plan.tok)
            pairs = (
                (tok.at[pl.ds(first + own * e, own)], tok3.at[pl.ds(0, own), mine], tok_send, tok_recv, 0),
                (tok.at[pl.ds(first + own * share, 1)], tok3.at[pl.ds(own, 1), pl.ds(at, plan.tok)], tok_send, tok_recv, 1),
                (cot.at[pl.ds(first + own * e, own)], cot3.at[pl.ds(0, own), mine], cot_send, cot_recv, 0),
                (cot.at[pl.ds(first + own * share, 1)], cot3.at[pl.ds(own, 1), pl.ds(at, plan.tok)], cot_send, cot_recv, 1),
            )
            here = jnp.logical_and(k == e, m == q)
            holds = lax.div(m * plan.tok, plan.part) == e
            for i, (src, dst, send, recv, what) in enumerate(pairs):
                wanted = holds if i == 3 else True

                @pl.when(jnp.logical_and(here, wanted))
                def _():
                    pltpu.make_async_copy(src, dst, recv.at[what]).start()

                @pl.when(jnp.logical_and(jnp.logical_not(here), wanted))
                def _():
                    pltpu.make_async_remote_copy(
                        src, dst, send.at[j, e, what], recv.at[what],
                        device_id={"dp": base + e, "mp": q}, device_id_type=MESH,
                    ).start()

    for e in range(share):

        @pl.when(k == e)
        def _():
            pltpu.make_async_copy(seg, seg3.at[e], seg_recv.at[e]).start()

        for f in range(share):

            @pl.when(jnp.logical_and(k == e, k != f))
            def _():
                pltpu.make_async_remote_copy(
                    seg, seg3.at[e], seg_send.at[f], seg_recv.at[e],
                    device_id={"dp": base + f}, device_id_type=MESH,
                ).start()

    for w in range(4):
        for way in range(2):
            ring(w, way, 0, True).start()
        pltpu.make_async_copy(shards[w], full[w].at[m], own_sem.at[w]).start()

    def step(s, carry):
        for w in range(4):
            for way in range(2):
                ring(w, way, s).wait_recv()

                @pl.when(s < n - 2)
                def _():
                    ring(w, way, s + 1).start()

                sibling(w, way, s).start()
        return carry

    lax.fori_loop(0, n - 1, step, 0)

    for w in range(4):
        rows = shards[w].shape[0]
        some = full[w].at[pl.ds(0, n - 1), pl.ds(0, rows // 2)]
        pltpu.make_async_copy(some, some, sib_recv.at[w]).wait()
        pltpu.make_async_copy(some, some, sib_send.at[w]).wait()
        some = full[w].at[pl.ds(0, n - 1), pl.ds(0, rows // 4)]
        for way in range(2):
            pltpu.make_async_copy(some, some, ring_send.at[w, way]).wait()
        pltpu.make_async_copy(shards[w], full[w].at[m], own_sem.at[w]).wait()
    for e in range(share):
        pltpu.make_async_copy(seg, seg3.at[e], seg_recv.at[e]).wait()

        @pl.when(k != e)
        def _():
            pltpu.make_async_copy(seg, seg3.at[e], seg_send.at[e]).wait()

    for ref, recv, extent in ((tok3, tok_recv, plan.seq), (cot3, cot_recv, plan.part)):
        some = ref.at[pl.ds(0, own)]
        pltpu.make_async_copy(some, some, recv.at[0]).wait()
        some = ref.at[pl.ds(own, 1), pl.ds(0, extent)]
        pltpu.make_async_copy(some, some, recv.at[1]).wait()
    for j in range(plan.groups):
        q = k * plan.groups + j
        for e in range(share):
            away = jnp.logical_not(jnp.logical_and(k == e, m == q))
            holds = lax.div(m * plan.tok, plan.part) == e
            for i, (ref, sem, rows) in enumerate(
                ((tok, tok_send, own), (tok, tok_send, 1), (cot, cot_send, own), (cot, cot_send, 1))
            ):
                some = ref.at[pl.ds(0, rows)]

                @pl.when(jnp.logical_and(away, holds if i == 3 else True))
                def _():
                    pltpu.make_async_copy(some, some, sem.at[j, e, i % 2]).wait()


def gather(plan, tokens_in, cotangent, segment_ids, weights):
    n, share = plan.mp, plan.share
    width = tokens_in.shape[2]
    any_space = pl.BlockSpec(memory_space=pl.ANY)
    dma = pltpu.SemaphoreType.DMA
    rows = jax.ShapeDtypeStruct((plan.rows, plan.seq, width), BF)
    return pl.pallas_call(
        functools.partial(gather_kernel, plan),
        out_shape=(
            rows,
            rows,
            jax.ShapeDtypeStruct((share,) + segment_ids.shape, jnp.int32),
            *[jax.ShapeDtypeStruct((n,) + w.shape, BF) for w in weights],
        ),
        in_specs=[any_space] * 7,
        out_specs=[any_space] * 7,
        scratch_shapes=[
            dma((plan.groups, share, 2)), dma((2,)), dma((plan.groups, share, 2)), dma((2,)),
            dma((share,)), dma((share,)), dma((4,)), dma((4, 2)), dma((4, 2, n - 1)), dma((4,)), dma((4,)),
        ],
        compiler_params=pltpu.CompilerParams(collective_id=0, has_side_effects=True),
        name="gather",
    )(tokens_in, cotangent, segment_ids, *weights)


def reduce_kernel(
    plan, n_y, x0, x1, x2, x3, out3, tg3, o0, o1, o2, o3, blk, tg,
    l0, l1, l2, l3, s0, s1, s2, s3, r0, r1, r2, r3, y0, y1, y2, y3, f0, f1, f2, f3, tgs, tgo, tgl,
    loc_sem, sib_send, sib_recv, ring_send, ring_recv, y_send, y_recv, fin_loc, fin_send, fin_recv,
    blk_send, blk_recv, tg_send, tg_recv, tgs_send, tgs_recv, tgl_sem,
):
    n, share, own, part = plan.mp, plan.share, plan.own, plan.part
    d, m, p = plan.place()
    core, yi = lax.rem(d, 2), lax.div(d, 2)
    sib = d + 1 - 2 * core
    k = lax.rem(d, share)
    base = d - k
    grads, outs = (x0, x1, x2, x3), (o0, o1, o2, o3)
    loc, sbl, slot = (l0, l1, l2, l3), (s0, s1, s2, s3), (r0, r1, r2, r3)
    ysl, fin = (y0, y1, y2, y3), (f0, f1, f2, f3)
    per_block = plan.share // 2
    block = lax.div(d, share)
    others = [lax.rem(yi + i, n_y) * 2 + core for i in range(1, n_y)]
    greet_all(plan, n_y, d, m)

    def quarter(w):
        return grads[w].shape[1] // 4

    def target(way, s):
        return plan.ring_at(p + n - 1 - s if way == 0 else p + 1 + s)

    def half_rows(w, way):
        return pl.ds(way * quarter(w), quarter(w))

    def full_rows(w, c, way):
        return pl.ds(pl.multiple_of((2 * c + way) * quarter(w), quarter(w)), quarter(w))

    def load(w, way, s):
        t = target(way, s)
        return pltpu.make_async_copy(
            grads[w].at[t, full_rows(w, core, way)], loc[w].at[t, half_rows(w, way)], loc_sem.at[w, way, s]
        )

    def give(w, way, s):
        t = target(way, s)
        return pltpu.make_async_remote_copy(
            grads[w].at[t, full_rows(w, 1 - core, way)], sbl[w].at[t, half_rows(w, way)],
            sib_send.at[w], sib_recv.at[w, way, s], device_id={"dp": sib}, device_id_type=MESH,
        )

    def hop(w, way, s):
        return pltpu.make_async_remote_copy(
            loc[w].at[target(way, s), half_rows(w, way)], slot[w].at[way, s], ring_send.at[w, way],
            ring_recv.at[w, way, s],
            device_id={"mp": plan.ring_at(p + 1 if way == 0 else p + n - 1)}, device_id_type=MESH,
        )

    for i in range(share):
        src = tg3.at[own, pl.ds(i * part, part)]
        if i == 0:
            pltpu.make_async_copy(src, tgs.at[0], tgl_sem.at[0]).start()
        else:
            pltpu.make_async_remote_copy(
                src, tgs.at[share - i], tgs_send.at[i], tgs_recv.at[share - i],
                device_id={"dp": base + lax.rem(k + i, share)}, device_id_type=MESH,
            ).start()

    j = lax.rem(m, plan.groups)
    home = base + lax.div(m, plan.groups)

    def send_rows(src3, shared, dst, send, recv, start):
        for q in range(n):
            toks = pl.ds(q * plan.tok, plan.tok)
            at = lax.rem(q * plan.tok, part)
            here = jnp.logical_and(home == d, m == q)
            first = j * plan.group_rows
            holds = (q * plan.tok) // part == k
            for what, (src, to, wanted) in enumerate(
                (
                    (src3.at[pl.ds(0, own), toks], dst.at[pl.ds(first + own * k, own)], True),
                    (shared.at[pl.ds(at, plan.tok)], dst.at[first + own * share], holds),
                )
            ):
                if not start[what]:
                    continue

                @pl.when(jnp.logical_and(here, wanted))
                def _():
                    pltpu.make_async_copy(src, to, recv.at[0]).start()

                @pl.when(jnp.logical_and(jnp.logical_not(here), wanted))
                def _():
                    pltpu.make_async_remote_copy(
                        src, to, send.at[q, what], recv.at[0], device_id={"dp": home, "mp": q}, device_id_type=MESH
                    ).start()

    def wait_rows(dst, send, recv):
        pltpu.make_async_copy(dst, dst, recv.at[0]).wait()
        for q in range(n):
            away = jnp.logical_not(jnp.logical_and(home == d, m == q))
            holds = (q * plan.tok) // part == k
            for what, rows in enumerate((own, 1)):
                some = dst.at[pl.ds(0, rows)]

                @pl.when(jnp.logical_and(away, True if what == 0 else holds))
                def _():
                    pltpu.make_async_copy(some, some, send.at[q, what]).wait()

    def begin(s, carry):
        for w in range(4):
            for way in range(2):
                load(w, way, s).start()
                give(w, way, s).start()
        return carry

    lax.fori_loop(0, n, begin, 0)
    send_rows(out3, out3.at[own], blk, blk_send, blk_recv, (True, True))
    send_rows(tg3, tgo, tg, tg_send, tg_recv, (True, False))

    def add(w, way, s, more, dst):
        t = target(way, s)
        rows = quarter(w)
        size = 16 if rows % 32 else 32

        @pl.loop(0, rows // size)
        def _(i):
            inner = pl.ds(pl.multiple_of(i * size, size), size)
            at = pl.ds(pl.multiple_of(way * rows + i * size, size), size)
            total = loc[w][t, at].astype(F32) + sbl[w][t, at].astype(F32)
            if more is not None:
                total = total + slot[w][way, more, inner].astype(F32)
            dst(t, at, total.astype(BF))

    def to_loc(w):
        def put(t, at, value):
            loc[w][t, at] = value

        return put

    def to_y(w):
        def put(t, at, value):
            ysl[w][yi, at] = value

        return put

    for w in range(4):
        for way in range(2):
            load(w, way, 0).wait()
            give(w, way, 0).wait_recv()
            add(w, way, 0, None, to_loc(w))
            hop(w, way, 0).start()

    for i in range(1, share):
        pltpu.make_async_copy(tgs.at[i], tgs.at[i], tgs_recv.at[i]).wait()
    pltpu.make_async_copy(tgs.at[0], tgs.at[0], tgl_sem.at[0]).wait()
    tgo[...] = sum(tgs[i].astype(F32) for i in range(share)).astype(BF)
    send_rows(tg3, tgo, tg, tg_send, tg_recv, (False, True))

    def step(s, carry):
        for w in range(4):
            for way in range(2):
                load(w, way, s).wait()
                give(w, way, s).wait_recv()
                hop(w, way, s - 1).wait_recv()
                add(w, way, s, s - 1, to_loc(w))
                hop(w, way, s).start()
        return carry

    lax.fori_loop(1, n - 1, step, 0)

    def to_others(w, i):
        return pltpu.make_async_remote_copy(
            ysl[w].at[yi], ysl[w].at[yi], y_send.at[w, i], y_recv.at[w, n_y - 2 - i],
            device_id={"dp": others[i]}, device_id_type=MESH,
        )

    for w in range(4):
        for way in range(2):
            load(w, way, n - 1).wait()
            give(w, way, n - 1).wait_recv()
            hop(w, way, n - 2).wait_recv()
            add(w, way, n - 1, n - 2, to_y(w))
        for i in range(n_y - 1):
            to_others(w, i).start()
    for w in range(4):
        rows = 2 * quarter(w)
        for i in range(n_y - 1):
            pltpu.make_async_copy(ysl[w].at[0], ysl[w].at[0], y_recv.at[w, i]).wait()
        size = 32

        @pl.loop(0, rows // size)
        def _(i):
            at = pl.ds(pl.multiple_of(i * size, size), size)
            total = ysl[w][0, at].astype(F32)
            for y in range(1, n_y):
                total = total + ysl[w][y, at].astype(F32)
            fin[w][at] = total

        there = outs[w].at[pl.ds(pl.multiple_of(core * rows, rows), rows)]
        pltpu.make_async_copy(fin[w], there, fin_loc.at[w]).start()
        pltpu.make_async_remote_copy(
            fin[w], there, fin_send.at[w], fin_recv.at[w], device_id={"dp": sib}, device_id_type=MESH
        ).start()

    for w in range(4):
        pltpu.make_async_copy(fin[w], fin[w], fin_loc.at[w]).wait()
        pltpu.make_async_copy(fin[w], fin[w], fin_send.at[w]).wait()
        pltpu.make_async_copy(fin[w], fin[w], fin_recv.at[w]).wait()
        for i in range(n_y - 1):
            pltpu.make_async_copy(ysl[w].at[0], ysl[w].at[0], y_send.at[w, i]).wait()
        for way in range(2):
            some = slot[w].at[0]
            pltpu.make_async_copy(some, some, ring_send.at[w, way]).wait()
        pltpu.make_async_copy(sbl[w], sbl[w], sib_send.at[w]).wait()
    for i in range(1, share):
        pltpu.make_async_copy(tgs.at[0], tgs.at[0], tgs_send.at[i]).wait()
    wait_rows(blk, blk_send, blk_recv)
    wait_rows(tg, tg_send, tg_recv)


def greet_all(plan, n_y, d, m):
    barrier = pltpu.get_barrier_semaphore()
    base = lax.div(d, plan.share) * plan.share

    def one(i, carry):
        e, q = base + lax.div(i, plan.mp), lax.rem(i, plan.mp)

        @pl.when(jnp.logical_or(e != d, q != m))
        def _():
            pl.semaphore_signal(barrier, inc=1, device_id={"dp": e, "mp": q}, device_id_type=MESH)

        return carry

    lax.fori_loop(0, plan.share * plan.mp, one, 0)

    def two(i, carry):
        e = 2 * i + lax.rem(d, 2)

        @pl.when(lax.div(e, plan.share) != lax.div(d, plan.share))
        def _():
            pl.semaphore_signal(barrier, inc=1, device_id={"dp": e}, device_id_type=MESH)

        return carry

    lax.fori_loop(0, n_y, two, 0)
    pl.semaphore_wait(barrier, plan.share * plan.mp - 1 + n_y - plan.share // 2)


def reduce_out(plan, grads, out3, tg3):
    n, share = plan.mp, plan.share
    n_y = plan.dp // 2
    width = out3.shape[2]
    any_space = pl.BlockSpec(memory_space=pl.ANY)
    dma = pltpu.SemaphoreType.DMA
    rows = jax.ShapeDtypeStruct((plan.rows_dev, plan.tok, width), BF)
    halves = [pltpu.VMEM((n, g.shape[1] // 2, g.shape[2]), BF) for g in grads]
    return pl.pallas_call(
        functools.partial(reduce_kernel, plan, n_y),
        out_shape=(*[jax.ShapeDtypeStruct(g.shape[1:], F32) for g in grads], rows, rows),
        in_specs=[any_space] * 6,
        out_specs=[any_space] * 6,
        scratch_shapes=[
            *halves,
            *halves,
            *[pltpu.VMEM((2, n - 1, g.shape[1] // 4, g.shape[2]), BF) for g in grads],
            *[pltpu.VMEM((n_y, g.shape[1] // 2, g.shape[2]), BF) for g in grads],
            *[pltpu.VMEM((g.shape[1] // 2, g.shape[2]), F32) for g in grads],
            pltpu.VMEM((share, plan.part, width), BF),
            pltpu.VMEM((plan.part, width), BF),
            pltpu.VMEM((8, 128), BF),
            dma((4, 2, n)), dma((4,)), dma((4, 2, n)), dma((4, 2)), dma((4, 2, n - 1)),
            dma((4, n_y - 1)), dma((4, n_y - 1)), dma((4,)), dma((4,)), dma((4,)),
            dma((n, 2)), dma((1,)), dma((n, 2)), dma((1,)), dma((share,)), dma((share,)), dma((1,)),
        ],
        compiler_params=pltpu.CompilerParams(
            collective_id=1, has_side_effects=True, vmem_limit_bytes=58 << 20
        ),
        name="reduce",
    )(*grads, out3, tg3)


def scores_of(query, key, allowed):
    raw = lax.dot_general(query, key, (((1,), (1,)), ((), ())), preferred_element_type=F32)
    scores = jnp.where(allowed, raw * HEAD_DIM ** (-0.5), MASKED)
    raised = jnp.exp(scores - jnp.max(scores, axis=-1, keepdims=True))
    return raised / jnp.sum(raised, axis=-1, keepdims=True)


def attend_kernel(heads, proj, seg_col, seg_row, out):
    allowed = seg_col[0] == seg_row[0]
    for h in range(heads):
        at = h * 3 * HEAD_DIM
        query, key, value = (proj[0, :, at + i * HEAD_DIM : at + (i + 1) * HEAD_DIM] for i in range(3))
        probs = scores_of(query, key, allowed).astype(BF)
        mixed = jnp.dot(probs, value, preferred_element_type=F32)
        out[0, :, h * HEAD_DIM : (h + 1) * HEAD_DIM] = mixed.astype(BF)


def attend(proj, seg):
    rows, seq, width3 = proj.shape
    heads = width3 // (3 * HEAD_DIM)
    return pl.pallas_call(
        functools.partial(attend_kernel, heads),
        out_shape=jax.ShapeDtypeStruct((rows, seq, width3 // 3), BF),
        grid=(rows,),
        in_specs=[
            pl.BlockSpec((1, seq, width3), lambda r: (r, 0, 0)),
            pl.BlockSpec((1, seq, 1), lambda r: (r, 0, 0)),
            pl.BlockSpec((1, 1, seq), lambda r: (r, 0, 0)),
        ],
        out_specs=pl.BlockSpec((1, seq, width3 // 3), lambda r: (r, 0, 0)),
        name="attend",
    )(proj, seg[:, :, None], seg[:, None, :])


def attend_back_kernel(heads, proj, grad, seg_col, seg_row, out):
    allowed = seg_col[0] == seg_row[0]
    across = (((1,), (1,)), ((), ()))
    down = (((0,), (0,)), ((), ()))
    for h in range(heads):
        at = h * 3 * HEAD_DIM
        query, key, value = (proj[0, :, at + i * HEAD_DIM : at + (i + 1) * HEAD_DIM] for i in range(3))
        head_grad = grad[0, :, h * HEAD_DIM : (h + 1) * HEAD_DIM]
        full = scores_of(query, key, allowed)
        value_grad = lax.dot_general(full.astype(BF), head_grad, down, preferred_element_type=F32)
        probs_grad = lax.dot_general(head_grad, value, across, preferred_element_type=F32)
        delta = jnp.sum(probs_grad * full, axis=-1, keepdims=True)
        low = (jnp.where(allowed, full * (probs_grad - delta), 0.0) * HEAD_DIM ** (-0.5)).astype(BF)
        query_grad = jnp.dot(low, key, preferred_element_type=F32)
        key_grad = lax.dot_general(low, query, down, preferred_element_type=F32)
        for i, part in enumerate((query_grad, key_grad, value_grad)):
            out[0, :, at + i * HEAD_DIM : at + (i + 1) * HEAD_DIM] = part.astype(BF)


def attend_back(proj, grad, seg):
    rows, seq, width3 = proj.shape
    heads = width3 // (3 * HEAD_DIM)
    return pl.pallas_call(
        functools.partial(attend_back_kernel, heads),
        out_shape=jax.ShapeDtypeStruct((rows, seq, width3), BF),
        grid=(rows,),
        in_specs=[
            pl.BlockSpec((1, seq, width3), lambda r: (r, 0, 0)),
            pl.BlockSpec((1, seq, width3 // 3), lambda r: (r, 0, 0)),
            pl.BlockSpec((1, seq, 1), lambda r: (r, 0, 0)),
            pl.BlockSpec((1, 1, seq), lambda r: (r, 0, 0)),
        ],
        out_specs=pl.BlockSpec((1, seq, width3), lambda r: (r, 0, 0)),
        name="attend_back",
    )(proj, grad, seg[:, :, None], seg[:, None, :])


def norm(values, gain_vec, shift_vec):
    centred = values - jnp.mean(values, axis=-1, keepdims=True)
    scale = lax.rsqrt(jnp.mean(centred * centred, axis=-1, keepdims=True) + EPS)
    unit = centred * scale
    return unit, scale, unit * gain_vec + shift_vec


def norm_back(unit, scale, gain_vec, grad):
    pulled = grad * gain_vec
    inner = jnp.mean(pulled * unit, axis=-1, keepdims=True)
    return scale * (pulled - jnp.mean(pulled, axis=-1, keepdims=True) - unit * inner)


def per_device(
    plan, tokens_in, segment_ids, attn_gain, attn_shift, qkv_weight, qkv_bias, out_weight, out_bias, mlp_gain, mlp_shift,
    up_weight, up_bias, down_weight, down_bias, cotangent,
):
    n, own, seq, part = plan.mp, plan.own, plan.seq, plan.part
    width = tokens_in.shape[2]
    held = own * seq + part
    every = plan.rows * seq
    ff_local = up_weight.shape[1]
    tok3, cot3, seg_all, wq, wo, wu, wd = gather(
        plan, tokens_in, cotangent, segment_ids, (qkv_weight, out_weight, up_weight, down_weight)
    )
    d, m = lax.axis_index("dp"), lax.axis_index("mp")
    k = lax.rem(d, plan.share)
    seg_flat = seg_all.reshape(plan.share * plan.rows_dev, seq)
    seg_own = lax.dynamic_slice(seg_flat, (m * plan.group_rows + own * k, 0), (own, seq))
    seg_last = lax.dynamic_slice(seg_flat, (m * plan.group_rows + own * plan.share, 0), (1, seq))
    seg_last = lax.dynamic_slice(jnp.concatenate([seg_last, seg_last], axis=1), (0, k * part), (1, seq))
    seg = jnp.concatenate([seg_own, seg_last], axis=0)

    bias_q = lax.all_gather(qkv_bias, "mp", axis=0)
    heads_local = qkv_bias.shape[1] // HEAD_DIM
    bias_q = bias_q.reshape(n, 2, heads_local, HEAD_DIM)
    full_bias = jnp.stack([bias_q[:, 0], jnp.zeros_like(bias_q[:, 0]), bias_q[:, 1]], axis=2).reshape(n, -1)
    bias_up = lax.all_gather(up_bias, "mp", axis=0)

    tokens_f = tok3.reshape(every, width).astype(F32)
    unit_one, scale_one, normed = norm(tokens_f, attn_gain, attn_shift)
    normed_one = normed.astype(BF)
    projected = (
        (jnp.einsum("td,sdf->tsf", normed_one, wq, preferred_element_type=F32) + full_bias)
        .astype(BF)
        .reshape(plan.rows, seq, 3 * width)
    )
    attn_out = attend(projected, seg)
    attn_flat = attn_out.reshape(every, width)[:held]
    wo_full = wo.reshape(width, width)
    hidden = tokens_f[:held] + jnp.dot(attn_flat, wo_full, preferred_element_type=F32) + out_bias
    unit_two, scale_two, normed = norm(hidden, mlp_gain, mlp_shift)
    normed_two = normed.astype(BF)
    pre_act = jnp.einsum("td,sdf->tsf", normed_two, wu, preferred_element_type=F32) + bias_up
    act_low = jax.nn.gelu(pre_act, approximate=False).astype(BF)
    down_full = wd.reshape(n * ff_local, width)
    act_flat = act_low.reshape(held, n * ff_local)
    block = (hidden + jnp.dot(act_flat, down_full, preferred_element_type=F32) + down_bias).astype(BF)

    cot = cot3.reshape(every, width)[:held]
    cot_f = cot.astype(F32)
    act_grad = jnp.einsum("td,sfd->tsf", cot, wd, preferred_element_type=F32)
    down_grad = jnp.einsum("tsf,td->sfd", act_low, cot, preferred_element_type=F32).astype(BF)
    phi = 0.5 * (1.0 + lax.erf(pre_act * math.sqrt(0.5)))
    density = jnp.exp(-0.5 * pre_act * pre_act) * (1.0 / math.sqrt(2.0 * math.pi))
    pre_grad = (act_grad * (phi + pre_act * density)).astype(BF)
    up_bias_part = jnp.sum(pre_grad, axis=0, dtype=F32)
    up_grad = jnp.einsum("td,tsf->sdf", normed_two, pre_grad, preferred_element_type=F32).astype(BF)
    normed_two_grad = jnp.einsum("tsf,sdf->td", pre_grad, wu, preferred_element_type=F32)
    mlp_gain_part = jnp.sum(normed_two_grad * unit_two, axis=0)
    mlp_shift_part = jnp.sum(normed_two_grad, axis=0)
    hidden_grad = cot_f + norm_back(unit_two, scale_two, mlp_gain, normed_two_grad)
    branch_grad = hidden_grad.astype(BF)
    out_grad = jnp.einsum("th,td->hd", attn_flat, branch_grad, preferred_element_type=F32).astype(BF)
    out_grad = out_grad.reshape(n, width // n, width)
    attn_grad = jnp.einsum("td,hd->th", branch_grad, wo_full, preferred_element_type=F32).astype(BF)
    attn_grad = jnp.concatenate([attn_grad, jnp.zeros((every - held, width), BF)], axis=0)
    qkv_grads = attend_back(projected, attn_grad.reshape(plan.rows, seq, width), seg)
    qkv_flat = qkv_grads.reshape(every, n, -1)
    qkv_grad = jnp.einsum("td,tsf->sdf", normed_one, qkv_flat, preferred_element_type=F32).astype(BF)
    bias_sums = jnp.sum(qkv_flat, axis=0, dtype=F32).reshape(n, heads_local, 3, HEAD_DIM)
    qkv_bias_part = jnp.stack([bias_sums[:, :, 0], bias_sums[:, :, 2]], axis=1)
    normed_one_grad = jnp.einsum("tsf,sdf->td", qkv_flat, wq, preferred_element_type=F32)
    attn_gain_part = jnp.sum(normed_one_grad * unit_one, axis=0)
    attn_shift_part = jnp.sum(normed_one_grad, axis=0)
    token_part = norm_back(unit_one, scale_one, attn_gain, normed_one_grad)
    tokens_part = jnp.concatenate([token_part[:held] + hidden_grad, token_part[held:]], axis=0).astype(BF)

    block3 = jnp.concatenate([block, jnp.zeros((every - held, width), BF)], axis=0).reshape(plan.rows, seq, width)
    sums = jnp.concatenate(
        [
            attn_gain_part, attn_shift_part, jnp.sum(hidden_grad, axis=0), mlp_gain_part, mlp_shift_part,
            jnp.sum(cot_f, axis=0), up_bias_part.reshape(-1), qkv_bias_part.reshape(-1),
        ]
    )
    sums = lax.psum(sums, ("dp", "mp"))
    six = sums[: 6 * width].reshape(6, width)
    up_sums = sums[6 * width : 6 * width + n * ff_local].reshape(n, ff_local)
    qkv_sums = sums[6 * width + n * ff_local :].reshape(n, 2, width // n)
    up_bias_grad = lax.dynamic_index_in_dim(up_sums, m, 0, keepdims=False)
    qkv_bias_grad = lax.dynamic_index_in_dim(qkv_sums, m, 0, keepdims=False)

    dq, do, du, dd, block_out, tokens_low = reduce_out(
        plan, (qkv_grad, out_grad, up_grad, down_grad), block3, tokens_part.reshape(plan.rows, seq, width)
    )
    tokens_grad = tokens_low.astype(F32)
    return (
        block_out, tokens_grad, six[0], six[1], dq, qkv_bias_grad, do, six[2], six[3], six[4], du, up_bias_grad, dd, six[5],
    )


def solution(mesh):
    dp, mp = mesh.shape["dp"], mesh.shape["mp"]
    rows_spec = P("dp", "mp", None)
    in_specs = (
        rows_spec, P("dp", None), P(), P(), P(None, "mp"), P(None, "mp"), P("mp", None), P(), P(), P(),
        P(None, "mp"), P("mp"), P("mp", None), P(), rows_spec,
    )
    out_specs = (
        rows_spec, rows_spec, P(), P(), P(None, "mp"), P(None, "mp"), P("mp", None), P(), P(), P(),
        P(None, "mp"), P("mp"), P("mp", None), P(),
    )

    def run(tokens_in, segment_ids, *rest):
        rows_all, seq_len, _ = tokens_in.shape
        plan = Plan(dp, mp, rows_all // dp, seq_len // mp, seq_len)
        return jax.shard_map(
            functools.partial(per_device, plan), mesh=mesh, in_specs=in_specs, out_specs=out_specs, check_vma=False
        )(tokens_in, segment_ids, *rest)

    return run
```

```python
import functools
import math

import jax
import jax.numpy as jnp
from jax import lax
from jax.experimental import pallas as pl
from jax.experimental.pallas import tpu as pltpu
from jax.sharding import PartitionSpec as P

HEAD_DIM = 64
EPS = 1e-06
MASKED = -1000000000.0
MESH = pl.DeviceIdType.MESH
BF = jnp.bfloat16
F32 = jnp.float32


class Plan:
    def __init__(self, dp, mp, rows_dev, tok_local, seq_len):
        self.dp, self.mp, self.rows_dev, self.tok, self.seq = dp, mp, rows_dev, tok_local, seq_len
        self.share = mp // math.gcd(rows_dev, mp)
        self.group_rows = rows_dev * self.share // mp
        self.own = self.group_rows // self.share
        if self.share % 2 or dp % self.share or dp % 4 or self.group_rows != self.own * self.share + 1:
            raise ValueError("unsupported sizes")
        self.groups = mp // self.share
        self.part = seq_len // self.share
        self.rows = self.own + 1
        self.hops = mp // 2
        self.all = dp * mp

    def ring_at(self, p):
        p = lax.rem(p, self.mp)
        back = lax.div(p, self.mp // 2)
        return 2 * p * (1 - back) + (2 * self.mp - 1 - 2 * p) * back


class Place:
    def __init__(self, plan):
        d, m = lax.axis_index("dp"), lax.axis_index("mp")
        odd = lax.rem(m, 2)
        self.d, self.m = d, m
        self.p = lax.div(m, 2) * (1 - odd) + (plan.mp - 1 - lax.div(m, 2)) * odd
        self.core = lax.rem(d, 2)
        self.sib = d + 1 - 2 * self.core
        self.y = lax.rem(lax.div(d, 2), 2)
        self.other = d + 2 - 4 * self.y
        self.k = lax.rem(d, plan.share)
        self.base = d - self.k
        self.quarter = 2 * self.y + self.core
        self.neighbour = (plan.ring_at(self.p + 1), plan.ring_at(self.p + plan.mp - 1))

    def away(self, plan, way, s):
        return plan.ring_at(self.p + plan.mp - s if way == 0 else self.p + s)


def greet(plan, at, everyone):
    barrier = pltpu.get_barrier_semaphore()
    span = plan.dp if everyone else max(plan.share, 4)
    base = lax.div(at.d, span) * span

    def one(i, carry):
        e, q = base + lax.div(i, plan.mp), lax.rem(i, plan.mp)

        @pl.when(jnp.logical_or(e != at.d, q != at.m))
        def _():
            pl.semaphore_signal(barrier, inc=1, device_id={"dp": e, "mp": q}, device_id_type=MESH)

        return carry

    lax.fori_loop(0, span * plan.mp, one, 0)
    pl.semaphore_wait(barrier, span * plan.mp - 1)


def remote(src, dst, send, recv, **to):
    return pltpu.make_async_remote_copy(src, dst, send, recv, device_id=to, device_id_type=MESH)


def settle(ref, sem):
    pltpu.make_async_copy(ref, ref, sem).wait()


def piece(ref, quarter, half=None):
    rows, cols = ref.shape[0] // 4, ref.shape[1]
    first = quarter * rows
    if half is None:
        return ref.at[pl.ds(pl.multiple_of(first, rows), rows)]
    if cols % 256 == 0:
        return ref.at[pl.ds(pl.multiple_of(first, rows), rows), pl.ds(half * (cols // 2), cols // 2)]
    return ref.at[pl.ds(pl.multiple_of(first + half * (rows // 2), rows // 2), rows // 2)]


def half_of(ref, half):
    rows, cols = ref.shape
    if cols % 256 == 0:
        return ref.at[:, pl.ds(half * (cols // 2), cols // 2)]
    return ref.at[pl.ds(half * (rows // 2), rows // 2)]


class Gatherer:
    def __init__(self, plan, at, shards, full, sems):
        self.plan, self.at, self.shards, self.full = plan, at, shards, full
        self.own_sem, self.ring_send, self.ring_recv, self.y_send, self.y_recv, self.sib_send, self.sib_recv = sems

    def _half(self, way, s):
        return way if s == self.plan.hops - 1 else None

    def ring(self, w, way, s):
        at, origin = self.at, self.at.away(self.plan, way, s)
        half = self._half(way, s)
        dst = piece(self.full[w].at[origin], at.quarter, half)
        src = piece(self.shards[w], at.quarter, half) if s == 0 else dst
        return remote(src, dst, self.ring_send.at[w, way], self.ring_recv.at[w, way, s], mp=at.neighbour[way])

    def cross(self, w, way, s):
        at, origin = self.at, self.at.away(self.plan, way, s + 1)
        block = piece(self.full[w].at[origin], at.quarter, self._half(way, s))
        return remote(block, block, self.y_send.at[w], self.y_recv.at[w, way, s], dp=at.other)

    def give(self, w, way, s, mine):
        at, origin = self.at, self.at.away(self.plan, way, s + 1)
        quarter = at.quarter if mine else 2 - 2 * at.y + at.core
        block = piece(self.full[w].at[origin], quarter, self._half(way, s))
        return remote(block, block, self.sib_send.at[w], self.sib_recv.at[w], dp=at.sib)

    def begin(self, w):
        for way in range(2):
            self.ring(w, way, 0).start()
        pltpu.make_async_copy(self.shards[w], self.full[w].at[self.at.m], self.own_sem.at[w]).start()

    def step(self, w, s):
        for way in range(2):
            self.ring(w, way, s).wait_recv()
            if s < self.plan.hops - 1:
                self.ring(w, way, s + 1).start()
            self.cross(w, way, s).start()
            self.give(w, way, s, True).start()

    def follow(self, w, s):
        for way in range(2):
            self.cross(w, way, s).wait_recv()
            self.give(w, way, s, False).start()

    def arrived(self, w):
        n, rows = self.plan.mp, self.shards[w].shape[0]
        settle(self.full[w].at[pl.ds(0, n - 1), pl.ds(0, rows // 2)], self.sib_recv.at[w])
        settle(self.shards[w], self.own_sem.at[w])

    def finish(self, w):
        n, rows = self.plan.mp, self.shards[w].shape[0]
        settle(self.full[w].at[pl.ds(0, n - 1), pl.ds(0, rows // 2)], self.sib_send.at[w])
        settle(self.full[w].at[pl.ds(0, n - 1), pl.ds(0, rows // 4)], self.y_send.at[w])
        for way in range(2):
            settle(self.full[w].at[pl.ds(0, self.plan.hops - 1), pl.ds(0, rows // 4)], self.ring_send.at[w, way])
            settle(piece(self.full[w].at[0], 0, way), self.ring_send.at[w, way])


def gatherer_sems(plan, count):
    dma = pltpu.SemaphoreType.DMA
    return [
        dma((count,)), dma((count, 2)), dma((count, 2, plan.hops)), dma((count,)), dma((count, 2, plan.hops)),
        dma((count,)), dma((count,)),
    ]


class RowsIn:
    def __init__(self, plan, at, src, dst, send, recv, whole_shared):
        self.plan, self.at, self.src, self.dst, self.send, self.recv = plan, at, src, dst, send, recv
        self.whole_shared = whole_shared

    def copies(self):
        plan, at = self.plan, self.at
        mine = pl.ds(pl.multiple_of(at.m * plan.tok, plan.tok), plan.tok)
        for j in range(plan.groups):
            q = at.k * plan.groups + j
            first = j * plan.group_rows
            for e in range(plan.share):
                here = jnp.logical_and(at.k == e, at.m == q)
                holds = True if self.whole_shared else lax.div(at.m * plan.tok, plan.part) == e
                to = lax.rem(at.m * plan.tok + plan.seq - e * plan.part, plan.seq)
                to = pl.ds(pl.multiple_of(to, plan.tok), plan.tok)
                yield here, True, q, e, j, 0, self.src.at[pl.ds(first + plan.own * e, plan.own)], self.dst.at[
                    pl.ds(0, plan.own), mine
                ]
                yield here, holds, q, e, j, 1, self.src.at[first + plan.own * plan.share], self.dst.at[plan.own, to]

    def start(self):
        for here, wanted, q, e, j, what, src, dst in self.copies():

            @pl.when(jnp.logical_and(here, wanted))
            def _():
                pltpu.make_async_copy(src, dst, self.recv.at[what]).start()

            @pl.when(jnp.logical_and(jnp.logical_not(here), wanted))
            def _():
                remote(src, dst, self.send.at[j, e, what], self.recv.at[what], dp=self.at.base + e, mp=q).start()

    def arrived(self):
        plan = self.plan
        settle(self.dst.at[pl.ds(0, plan.own)], self.recv.at[0])
        extent = plan.seq if self.whole_shared else plan.part
        settle(self.dst.at[plan.own, pl.ds(0, extent)], self.recv.at[1])

    def finish(self):
        for here, wanted, q, e, j, what, src, dst in self.copies():

            @pl.when(jnp.logical_and(jnp.logical_not(here), wanted))
            def _():
                settle(src, self.send.at[j, e, what])


def gather_kernel(
    plan, tok, cot, seg, bq, bu, w0, w1, w2, w3, tok3, cot3, seg3, gbq, gbu, g0, g1, g2, g3,
    tok_send, tok_recv, cot_send, cot_recv, seg_send, seg_recv, bias_send, bias_recv, *sems,
):
    n, share = plan.mp, plan.share
    at = Place(plan)
    gat = Gatherer(plan, at, (w0, w1, w2, w3), (g0, g1, g2, g3), sems)
    tokens = RowsIn(plan, at, tok, tok3, tok_send, tok_recv, True)
    cots = RowsIn(plan, at, cot, cot3, cot_send, cot_recv, False)
    greet(plan, at, False)

    gat.begin(0)
    tokens.start()
    biases = ((bq, gbq, 0), (bu, gbu, 1))
    for src, dst, i in biases:
        pltpu.make_async_copy(src, dst.at[at.m], bias_recv.at[i]).start()
        for s in range(1, n):
            remote(src, dst.at[at.m], bias_send.at[i], bias_recv.at[i], mp=lax.rem(at.m + s, n)).start()
    pltpu.make_async_copy(seg, seg3.at[at.k], seg_recv.at[0]).start()
    for e in range(1, share):
        remote(seg, seg3.at[at.k], seg_send.at[0], seg_recv.at[0], dp=at.base + lax.rem(at.k + e, share)).start()
    for w in (1, 2, 3):
        gat.begin(w)
    cots.start()
    for s in range(plan.hops):
        for w in range(4):
            gat.step(w, s)
            if s:
                gat.follow(w, s - 1)
    for w in range(4):
        gat.follow(w, plan.hops - 1)
    for w in range(4):
        gat.arrived(w)
        gat.finish(w)
    tokens.arrived()
    tokens.finish()
    cots.arrived()
    cots.finish()
    for src, dst, i in biases:
        settle(dst, bias_recv.at[i])
        settle(dst.at[pl.ds(0, n - 1)], bias_send.at[i])
    settle(seg3, seg_recv.at[0])
    settle(seg3.at[pl.ds(0, share - 1)], seg_send.at[0])


def gather(plan, tokens_in, cotangent, segment_ids, biases, weights):
    n, share = plan.mp, plan.share
    width = tokens_in.shape[2]
    any_space = pl.BlockSpec(memory_space=pl.ANY)
    dma = pltpu.SemaphoreType.DMA
    rows = jax.ShapeDtypeStruct((plan.rows, plan.seq, width), BF)
    return pl.pallas_call(
        functools.partial(gather_kernel, plan),
        out_shape=(
            rows,
            rows,
            jax.ShapeDtypeStruct((share,) + segment_ids.shape, jnp.int32),
            *[jax.ShapeDtypeStruct((n,) + b.shape, F32) for b in biases],
            *[jax.ShapeDtypeStruct((n,) + w.shape, BF) for w in weights],
        ),
        in_specs=[any_space] * 9,
        out_specs=[any_space] * 9,
        scratch_shapes=[
            dma((plan.groups, share, 2)), dma((2,)), dma((plan.groups, share, 2)), dma((2,)), dma((1,)), dma((1,)),
            dma((2,)), dma((2,)), *gatherer_sems(plan, 4),
        ],
        compiler_params=pltpu.CompilerParams(collective_id=0, has_side_effects=True),
        name="gather",
    )(tokens_in, cotangent, segment_ids, *biases, *weights)


class Reducer:
    def __init__(self, plan, at, grads, loc, sbl, yrc, slot, fin, grp, sems):
        self.plan, self.at, self.grads = plan, at, grads
        self.loc, self.sbl, self.yrc, self.slot, self.fin, self.grp = loc, sbl, yrc, slot, fin, grp
        (
            self.loc_sem, self.sib_send, self.sib_recv, self.y_send, self.y_recv, self.ring_send, self.ring_recv,
            self.grp_send, self.grp_recv, self.fin_send, self.fin_recv,
        ) = sems
        hops = plan.hops
        self.order = [(0, hops)] + [(way, dist) for dist in range(hops - 1, 0, -1) for way in range(2)] + [(0, 0)]

    def target(self, i):
        way, dist = self.order[i]
        return self.plan.ring_at(self.at.p + dist if way == 0 else self.at.p + self.plan.mp - dist)

    def load(self, w, yy, i):
        at, t = self.at, self.target(i)
        src = piece(self.grads[w].at[t], 2 * yy + at.core)
        return pltpu.make_async_copy(src, self.loc[w].at[yy, t], self.loc_sem.at[w, i, yy])

    def give(self, w, yy, i):
        at, t = self.at, self.target(i)
        src = piece(self.grads[w].at[t], 2 * yy + 1 - at.core)
        return remote(src, self.sbl[w].at[yy, t], self.sib_send.at[w], self.sib_recv.at[w, i, yy], dp=at.sib)

    def begin(self, w):
        for i in range(len(self.order)):
            for yy in range(2):
                self.load(w, yy, i).start()
                self.give(w, yy, i).start()
        if self.plan.hops > 0:
            for way in range(2):
                part = half_of(self.slot[w].at[way, 0], 1 - way)
                part[...] = jnp.zeros(part.shape, BF)

    def ready(self, w, yy, i):
        for v in range(2):

            @pl.when(yy == v)
            def _():
                self.load(w, v, i).wait()
                self.give(w, v, i).wait_recv()

    def add(self, w, yy, t, extra, put):
        rows, cols = self.loc[w].shape[2:]
        size = 32 if rows % 32 == 0 else rows

        def block(b):
            inner = pl.ds(pl.multiple_of(b * size, size), size)
            total = self.loc[w][yy, t, inner].astype(F32) + self.sbl[w][yy, t, inner].astype(F32)
            for ref in extra:
                total = total + ref[inner].astype(F32)
            put(inner, total)

        if rows == size:
            block(0)
        else:
            pl.loop(0, rows // size)(block)

    def cross(self, w, i):
        at, t = self.at, self.target(i)
        return remote(self.loc[w].at[1 - at.y, t], self.yrc[w].at[t], self.y_send.at[w], self.y_recv.at[w, i], dp=at.other)

    def first(self, w, i):
        at, t = self.at, self.target(i)
        self.ready(w, 1 - at.y, i)

        def put(inner, total):
            self.loc[w][1 - at.y, t, inner] = total.astype(BF)

        self.add(w, 1 - at.y, t, (), put)
        self.cross(w, i).start()

    def hop(self, w, way, s, t):
        src = self.loc[w].at[self.at.y, t]
        dst = self.slot[w].at[way, s]
        if s == 0:
            src, dst = half_of(src, way), half_of(dst, way)
        return remote(
            src, dst, self.ring_send.at[w, way], self.ring_recv.at[w, way, s], mp=self.at.neighbour[way]
        )

    def step(self, w, i):
        at, t = self.at, self.target(i)
        way, dist = self.order[i]
        s = self.plan.hops - dist
        self.ready(w, at.y, i)
        self.cross(w, i).wait_recv()
        extra = [self.yrc[w].at[t]]
        ways = (0, 1) if dist in (0, self.plan.hops) else (way,)
        if s > 0:
            for v in ways:
                self.hop(w, v, s - 1, t).wait_recv()
                extra.append(self.slot[w].at[v, s - 1])
        rows = self.loc[w].shape[2]
        if dist:

            def put(inner, total):
                self.loc[w][at.y, t, inner] = total.astype(BF)

            self.add(w, at.y, t, extra, put)
            for v in ways:
                self.hop(w, v, s, t).start()
        else:
            quads = self.plan.dp // 4
            mine = lax.div(at.d, 4)

            def put(inner, total):
                if quads > 1:
                    self.grp[w][mine, inner] = total.astype(BF)
                else:
                    to = pl.ds(pl.multiple_of(at.quarter * rows + inner.start, inner.size), inner.size)
                    self.fin[w][to] = total.astype(BF)

            self.add(w, at.y, t, extra, put)
            if quads > 1:
                for i in range(1, quads):
                    self.between(w, i, 0).start()

    def between(self, w, i, what):
        at, quads = self.at, self.plan.dp // 4
        to = lax.rem(at.d + 4 * i, self.plan.dp)
        block = self.grp[w].at[lax.div(at.d, 4)]
        return remote(block, block, self.grp_send.at[w], self.grp_recv.at[w], dp=to)

    def share_out(self, w, what):
        at = self.at
        quarter = at.quarter if what != 1 else 2 - 2 * at.y + at.core
        block = piece(self.fin[w], quarter)
        to = at.other if what == 2 else at.sib
        return remote(block, block, self.fin_send.at[w, what], self.fin_recv.at[w, what], dp=to)

    def last(self, w):
        quads = self.plan.dp // 4
        if quads > 1:
            rows = self.loc[w].shape[2]
            settle(self.grp[w].at[pl.ds(0, quads - 1)], self.grp_recv.at[w])
            total = self.grp[w][0].astype(F32)
            for i in range(1, quads):
                total = total + self.grp[w][i].astype(F32)
            self.fin[w][pl.ds(pl.multiple_of(self.at.quarter * rows, rows), rows)] = total.astype(BF)
        self.share_out(w, 2).start()
        self.share_out(w, 0).start()

    def spread(self, w):
        self.share_out(w, 2).wait_recv()
        self.share_out(w, 1).start()

    def arrived(self, w):
        self.share_out(w, 0).wait_recv()
        self.share_out(w, 1).wait_recv()

    def finish(self, w):
        hops = self.plan.hops
        quads = self.plan.dp // 4
        for what in range(3):
            self.share_out(w, what).wait_send()
        for i in range(1, quads):
            self.between(w, i, 0).wait_send()
        settle(self.loc[w].at[0], self.y_send.at[w])
        settle(self.sbl[w], self.sib_send.at[w])
        for way in range(2):
            settle(self.slot[w].at[way, pl.ds(0, hops - 1)], self.ring_send.at[w, way])
            settle(half_of(self.slot[w].at[way, 0], way), self.ring_send.at[w, way])


def reducer_scratch(plan, grads):
    n, quads = plan.mp, plan.dp // 4
    dma = pltpu.SemaphoreType.DMA
    count = len(grads)
    quarter = [(g.shape[1] // 4, g.shape[2]) for g in grads]
    scratch = [pltpu.VMEM((2, n) + q, BF) for q in quarter]
    scratch += [pltpu.VMEM((2, n) + q, BF) for q in quarter]
    scratch += [pltpu.VMEM((n,) + q, BF) for q in quarter]
    scratch += [pltpu.VMEM((2, plan.hops) + q, BF) for q in quarter]
    scratch += [pltpu.VMEM(g.shape[1:], BF) for g in grads]
    scratch += [pltpu.VMEM((quads,) + (q if quads > 1 else (8, 128)), BF) for q in quarter]
    scratch += [
        dma((count, n, 2)), dma((count,)), dma((count, n, 2)), dma((count,)), dma((count, n)), dma((count, 2)),
        dma((count, 2, plan.hops)), dma((count,)), dma((count,)), dma((count, 3)), dma((count, 3)),
    ]
    return scratch


class RowsOut:
    def __init__(self, plan, at, src, shared, dst, send, recv):
        self.plan, self.at, self.src, self.shared, self.dst, self.send, self.recv = plan, at, src, shared, dst, send, recv
        self.home = at.base + lax.div(at.m, plan.groups)
        self.first = lax.rem(at.m, plan.groups) * plan.group_rows

    def copies(self, what):
        plan, at = self.plan, self.at
        for q in range(plan.mp):
            here = jnp.logical_and(self.home == at.d, at.m == q)
            toks = pl.ds(q * plan.tok, plan.tok)
            if what == 0:
                yield q, here, True, self.src.at[pl.ds(0, plan.own), toks], self.dst.at[
                    pl.ds(self.first + plan.own * at.k, plan.own)
                ]
            else:
                holds = at.k == (q * plan.tok) // plan.part
                yield q, here, holds, self.shared.at[pl.ds((q * plan.tok) % plan.part, plan.tok)], self.dst.at[
                    self.first + plan.own * plan.share
                ]

    def start(self, what):
        for q, here, wanted, src, dst in self.copies(what):

            @pl.when(jnp.logical_and(here, wanted))
            def _():
                pltpu.make_async_copy(src, dst, self.recv.at[0]).start()

            @pl.when(jnp.logical_and(jnp.logical_not(here), wanted))
            def _():
                remote(src, dst, self.send.at[q, what], self.recv.at[0], dp=self.home, mp=q).start()

    def finish(self):
        settle(self.dst, self.recv.at[0])
        for what in range(2):
            for q, here, wanted, src, dst in self.copies(what):

                @pl.when(jnp.logical_and(jnp.logical_not(here), wanted))
                def _():
                    settle(src, self.send.at[q, what])


def reduce_kernel(plan, x0, x1, x2, x3, out3, tg3, vec, o0, o1, o2, o3, blk, tg, vout, *rest):
    share, own, part = plan.share, plan.own, plan.part
    grads, outs = (x0, x1, x2, x3), (o0, o1, o2, o3)
    groups = [rest[4 * i : 4 * i + 4] for i in range(6)]
    sems, rest = rest[24:35], rest[35:]
    fout, rest = rest[:4], rest[4:]
    (
        tgs, tgo, vrc, vsum, out_sem, blk_send, blk_recv, tg_send, tg_recv, tgs_send, tgs_recv, tgl_sem,
        v_send, v_recv,
    ) = rest
    at = Place(plan)
    red = Reducer(plan, at, grads, *groups, sems)
    blocks = RowsOut(plan, at, out3, out3.at[own], blk, blk_send, blk_recv)
    tokens = RowsOut(plan, at, tg3, tgo, tg, tg_send, tg_recv)
    greet(plan, at, True)
    me = at.d * plan.mp + at.m

    for w in range(4):
        red.begin(w)
    for i in range(share):
        src = tg3.at[own, pl.ds(i * part, part)]
        if i == 0:
            pltpu.make_async_copy(src, tgs.at[0], tgl_sem.at[0]).start()
        else:
            to = at.base + lax.rem(at.k + i, share)
            remote(src, tgs.at[share - i], tgs_send.at[i], tgs_recv.at[share - i], dp=to).start()

    def vector(phase, src_of, dst):
        def one(i, carry):
            to = lax.rem(me + i, plan.all)
            remote(
                src_of(to), dst.at[me], v_send.at[phase], v_recv.at[phase], dp=lax.div(to, plan.mp), mp=lax.rem(to, plan.mp)
            ).start()
            return carry

        lax.fori_loop(1, plan.all, one, 0)
        pltpu.make_async_copy(src_of(me), dst.at[me], v_recv.at[phase]).start()

    vector(0, lambda to: vec.at[to], vrc)
    blocks.start(0)
    blocks.start(1)
    tokens.start(0)
    for w in range(4):
        red.first(w, 0)
    settle(vrc, v_recv.at[0])
    vsum[...] = jnp.sum(vrc[...], axis=0)
    vector(1, lambda to: vsum, vout)
    for i in range(1, share):
        settle(tgs.at[i], tgs_recv.at[i])
    settle(tgs.at[0], tgl_sem.at[0])
    tgo[...] = sum(tgs[i].astype(F32) for i in range(share)).astype(BF)
    tokens.start(1)
    count = len(red.order)
    for i in range(count):
        for w in range(4):
            if i + 1 < count:
                red.first(w, i + 1)
            red.step(w, i)
    for w in range(4):
        red.last(w)
    for w in range(4):
        red.spread(w)
    for w in range(4):
        red.arrived(w)
        fout[w][...] = red.fin[w][...].astype(F32)
        pltpu.make_async_copy(fout[w], outs[w], out_sem.at[w]).start()
    for w in range(4):
        red.finish(w)
        settle(fout[w], out_sem.at[w])
    for i in range(1, share):
        settle(tgs.at[0], tgs_send.at[i])
    blocks.finish()
    tokens.finish()
    settle(vout, v_recv.at[1])
    for phase in range(2):
        settle(vout.at[pl.ds(0, plan.all - 1)], v_send.at[phase])


def reduce_out(plan, grads, out3, tg3, vec):
    n, share = plan.mp, plan.share
    width = out3.shape[2]
    any_space = pl.BlockSpec(memory_space=pl.ANY)
    dma = pltpu.SemaphoreType.DMA
    rows = jax.ShapeDtypeStruct((plan.rows_dev, plan.tok, width), BF)
    return pl.pallas_call(
        functools.partial(reduce_kernel, plan),
        out_shape=(
            *[jax.ShapeDtypeStruct(g.shape[1:], F32) for g in grads],
            rows,
            rows,
            jax.ShapeDtypeStruct(vec.shape, F32),
        ),
        in_specs=[any_space] * 7,
        out_specs=[any_space] * 7,
        scratch_shapes=[
            *reducer_scratch(plan, grads),
            *[pltpu.VMEM(g.shape[1:], F32) for g in grads],
            pltpu.VMEM((share, plan.part, width), BF),
            pltpu.VMEM((plan.part, width), BF),
            pltpu.VMEM(vec.shape, F32),
            pltpu.VMEM(vec.shape[1:], F32),
            dma((4,)), dma((n, 2)), dma((1,)), dma((n, 2)), dma((1,)), dma((share,)), dma((share,)), dma((1,)),
            dma((2,)), dma((2,)),
        ],
        compiler_params=pltpu.CompilerParams(
            collective_id=1, has_side_effects=True, vmem_limit_bytes=60 << 20
        ),
        name="reduce",
    )(*grads, out3, tg3, vec)


def scores_of(query, key, allowed):
    raw = lax.dot_general(query, key, (((1,), (1,)), ((), ())), preferred_element_type=F32)
    scores = jnp.where(allowed, raw * HEAD_DIM ** (-0.5), MASKED)
    raised = jnp.exp(scores - jnp.max(scores, axis=-1, keepdims=True))
    return raised / jnp.sum(raised, axis=-1, keepdims=True)


def attend_kernel(heads, proj, seg_col, seg_row, out):
    allowed = seg_col[0] == seg_row[0]
    for h in range(heads):
        at = h * 3 * HEAD_DIM
        query, key, value = (proj[0, :, at + i * HEAD_DIM : at + (i + 1) * HEAD_DIM] for i in range(3))
        probs = scores_of(query, key, allowed).astype(BF)
        mixed = jnp.dot(probs, value, preferred_element_type=F32)
        out[0, :, h * HEAD_DIM : (h + 1) * HEAD_DIM] = mixed.astype(BF)


def attend(proj, seg):
    rows, seq, width3 = proj.shape
    heads = width3 // (3 * HEAD_DIM)
    return pl.pallas_call(
        functools.partial(attend_kernel, heads),
        out_shape=jax.ShapeDtypeStruct((rows, seq, width3 // 3), BF),
        grid=(rows,),
        in_specs=[
            pl.BlockSpec((1, seq, width3), lambda r: (r, 0, 0)),
            pl.BlockSpec((1, seq, 1), lambda r: (r, 0, 0)),
            pl.BlockSpec((1, 1, seq), lambda r: (r, 0, 0)),
        ],
        out_specs=pl.BlockSpec((1, seq, width3 // 3), lambda r: (r, 0, 0)),
        name="attend",
    )(proj, seg[:, :, None], seg[:, None, :])


def attend_back_kernel(heads, proj, grad, seg_col, seg_row, out):
    allowed = seg_col[0] == seg_row[0]
    across = (((1,), (1,)), ((), ()))
    down = (((0,), (0,)), ((), ()))
    for h in range(heads):
        at = h * 3 * HEAD_DIM
        query, key, value = (proj[0, :, at + i * HEAD_DIM : at + (i + 1) * HEAD_DIM] for i in range(3))
        head_grad = grad[0, :, h * HEAD_DIM : (h + 1) * HEAD_DIM]
        full = scores_of(query, key, allowed)
        value_grad = lax.dot_general(full.astype(BF), head_grad, down, preferred_element_type=F32)
        probs_grad = lax.dot_general(head_grad, value, across, preferred_element_type=F32)
        delta = jnp.sum(probs_grad * full, axis=-1, keepdims=True)
        low = (jnp.where(allowed, full * (probs_grad - delta), 0.0) * HEAD_DIM ** (-0.5)).astype(BF)
        query_grad = jnp.dot(low, key, preferred_element_type=F32)
        key_grad = lax.dot_general(low, query, down, preferred_element_type=F32)
        for i, part in enumerate((query_grad, key_grad, value_grad)):
            out[0, :, at + i * HEAD_DIM : at + (i + 1) * HEAD_DIM] = part.astype(BF)


def attend_back(proj, grad, seg):
    rows, seq, width3 = proj.shape
    heads = width3 // (3 * HEAD_DIM)
    return pl.pallas_call(
        functools.partial(attend_back_kernel, heads),
        out_shape=jax.ShapeDtypeStruct((rows, seq, width3), BF),
        grid=(rows,),
        in_specs=[
            pl.BlockSpec((1, seq, width3), lambda r: (r, 0, 0)),
            pl.BlockSpec((1, seq, width3 // 3), lambda r: (r, 0, 0)),
            pl.BlockSpec((1, seq, 1), lambda r: (r, 0, 0)),
            pl.BlockSpec((1, 1, seq), lambda r: (r, 0, 0)),
        ],
        out_specs=pl.BlockSpec((1, seq, width3), lambda r: (r, 0, 0)),
        name="attend_back",
    )(proj, grad, seg[:, :, None], seg[:, None, :])


def norm(values, gain_vec, shift_vec):
    centred = values - jnp.mean(values, axis=-1, keepdims=True)
    scale = lax.rsqrt(jnp.mean(centred * centred, axis=-1, keepdims=True) + EPS)
    unit = centred * scale
    return unit, scale, unit * gain_vec + shift_vec


def norm_back(unit, scale, gain_vec, grad):
    pulled = grad * gain_vec
    inner = jnp.mean(pulled * unit, axis=-1, keepdims=True)
    return scale * (pulled - jnp.mean(pulled, axis=-1, keepdims=True) - unit * inner)


def per_device(
    plan, tokens_in, segment_ids, attn_gain, attn_shift, qkv_weight, qkv_bias, out_weight, out_bias, mlp_gain, mlp_shift,
    up_weight, up_bias, down_weight, down_bias, cotangent,
):
    n, own, seq, part = plan.mp, plan.own, plan.seq, plan.part
    width = tokens_in.shape[2]
    held = own * seq + part
    every = plan.rows * seq
    ff_local = up_weight.shape[1]
    tok3, cot3, seg_all, bias_q, bias_up, wq, wo, wu, wd = gather(
        plan, tokens_in, cotangent, segment_ids, (qkv_bias, up_bias.reshape(1, ff_local)),
        (qkv_weight, out_weight, up_weight, down_weight),
    )
    d, m = lax.axis_index("dp"), lax.axis_index("mp")
    k = lax.rem(d, plan.share)
    seg_flat = seg_all.reshape(plan.share * plan.rows_dev, seq)
    seg_own = lax.dynamic_slice(seg_flat, (m * plan.group_rows + own * k, 0), (own, seq))
    seg_last = lax.dynamic_slice(seg_flat, (m * plan.group_rows + own * plan.share, 0), (1, seq))
    seg_last = lax.dynamic_slice(jnp.concatenate([seg_last, seg_last], axis=1), (0, k * part), (1, seq))
    seg = jnp.concatenate([seg_own, seg_last], axis=0)

    heads_local = qkv_bias.shape[1] // HEAD_DIM
    bias_q = bias_q.reshape(n, 2, heads_local, HEAD_DIM)
    full_bias = jnp.stack([bias_q[:, 0], jnp.zeros_like(bias_q[:, 0]), bias_q[:, 1]], axis=2).reshape(n, -1)
    bias_up = bias_up.reshape(n, ff_local)

    tokens_f = tok3.reshape(every, width).astype(F32)
    unit_one, scale_one, normed = norm(tokens_f, attn_gain, attn_shift)
    normed_one = normed.astype(BF)
    projected = (
        (jnp.einsum("td,sdf->tsf", normed_one, wq, preferred_element_type=F32) + full_bias)
        .astype(BF)
        .reshape(plan.rows, seq, 3 * width)
    )
    attn_out = attend(projected, seg)
    attn_flat = attn_out.reshape(every, width)[:held]
    wo_full = wo.reshape(width, width)
    hidden = tokens_f[:held] + jnp.dot(attn_flat, wo_full, preferred_element_type=F32) + out_bias
    unit_two, scale_two, normed = norm(hidden, mlp_gain, mlp_shift)
    normed_two = normed.astype(BF)
    pre_act = jnp.einsum("td,sdf->tsf", normed_two, wu, preferred_element_type=F32) + bias_up
    act_low = jax.nn.gelu(pre_act, approximate=False).astype(BF)
    down_full = wd.reshape(n * ff_local, width)
    act_flat = act_low.reshape(held, n * ff_local)
    block = (hidden + jnp.dot(act_flat, down_full, preferred_element_type=F32) + down_bias).astype(BF)

    cot = cot3.reshape(every, width)[:held]
    cot_f = cot.astype(F32)
    act_grad = jnp.einsum("td,sfd->tsf", cot, wd, preferred_element_type=F32)
    down_grad = jnp.einsum("tsf,td->sfd", act_low, cot, preferred_element_type=F32).astype(BF)
    phi = 0.5 * (1.0 + lax.erf(pre_act * math.sqrt(0.5)))
    density = jnp.exp(-0.5 * pre_act * pre_act) * (1.0 / math.sqrt(2.0 * math.pi))
    pre_grad = (act_grad * (phi + pre_act * density)).astype(BF)
    up_bias_part = jnp.sum(pre_grad, axis=0, dtype=F32)
    up_grad = jnp.einsum("td,tsf->sdf", normed_two, pre_grad, preferred_element_type=F32).astype(BF)
    normed_two_grad = jnp.einsum("tsf,sdf->td", pre_grad, wu, preferred_element_type=F32)
    mlp_gain_part = jnp.sum(normed_two_grad * unit_two, axis=0)
    mlp_shift_part = jnp.sum(normed_two_grad, axis=0)
    hidden_grad = cot_f + norm_back(unit_two, scale_two, mlp_gain, normed_two_grad)
    branch_grad = hidden_grad.astype(BF)
    out_grad = jnp.einsum("th,td->hd", attn_flat, branch_grad, preferred_element_type=F32).astype(BF)
    out_grad = out_grad.reshape(n, width // n, width)
    attn_grad = jnp.einsum("td,hd->th", branch_grad, wo_full, preferred_element_type=F32).astype(BF)
    attn_grad = jnp.concatenate([attn_grad, jnp.zeros((every - held, width), BF)], axis=0)
    qkv_grads = attend_back(projected, attn_grad.reshape(plan.rows, seq, width), seg)
    qkv_flat = qkv_grads.reshape(every, n, -1)
    qkv_grad = jnp.einsum("td,tsf->sdf", normed_one, qkv_flat, preferred_element_type=F32).astype(BF)
    bias_sums = jnp.sum(qkv_flat, axis=0, dtype=F32).reshape(n, heads_local, 3, HEAD_DIM)
    qkv_bias_part = jnp.stack([bias_sums[:, :, 0], bias_sums[:, :, 2]], axis=1)
    normed_one_grad = jnp.einsum("tsf,sdf->td", qkv_flat, wq, preferred_element_type=F32)
    attn_gain_part = jnp.sum(normed_one_grad * unit_one, axis=0)
    attn_shift_part = jnp.sum(normed_one_grad, axis=0)
    token_part = norm_back(unit_one, scale_one, attn_gain, normed_one_grad)
    tokens_part = jnp.concatenate([token_part[:held] + hidden_grad, token_part[held:]], axis=0).astype(BF)

    block3 = jnp.concatenate([block, jnp.zeros((every - held, width), BF)], axis=0).reshape(plan.rows, seq, width)
    six = jnp.stack(
        [
            attn_gain_part, attn_shift_part, jnp.sum(hidden_grad, axis=0), mlp_gain_part, mlp_shift_part,
            jnp.sum(cot_f, axis=0),
        ]
    )
    six_size, up_size, qkv_size = 6 * width // plan.all, ff_local // plan.dp, 2 * width // plan.all
    up_rows = up_bias_part.reshape(n, plan.dp, up_size).swapaxes(0, 1).reshape(plan.all, up_size)
    qkv_rows = qkv_bias_part.reshape(n, plan.dp, qkv_size).swapaxes(0, 1).reshape(plan.all, qkv_size)
    vec = jnp.concatenate([six.reshape(plan.all, six_size), up_rows, qkv_rows], axis=1)
    size = vec.shape[1]
    padded = -(-size // 128) * 128
    vec = jnp.pad(vec, ((0, 0), (0, padded - size))).reshape(plan.all, padded // 128, 128)

    dq, do, du, dd, block_out, tokens_low, sums = reduce_out(
        plan, (qkv_grad, out_grad, up_grad, down_grad), block3, tokens_part.reshape(plan.rows, seq, width), vec
    )
    sums = sums.reshape(plan.all, padded)
    six = sums[:, :six_size].reshape(6, width)
    mine = lax.dynamic_index_in_dim(sums.reshape(plan.dp, n, padded), m, 1, keepdims=False)
    up_bias_grad = mine[:, six_size : six_size + up_size].reshape(ff_local)
    qkv_bias_grad = mine[:, six_size + up_size : size].reshape(2, width // n)
    tokens_grad = tokens_low.astype(F32)
    return (
        block_out, tokens_grad, six[0], six[1], dq, qkv_bias_grad, do, six[2], six[3], six[4], du, up_bias_grad, dd, six[5],
    )


def solution(mesh):
    dp, mp = mesh.shape["dp"], mesh.shape["mp"]
    rows_spec = P("dp", "mp", None)
    in_specs = (
        rows_spec, P("dp", None), P(), P(), P(None, "mp"), P(None, "mp"), P("mp", None), P(), P(), P(),
        P(None, "mp"), P("mp"), P("mp", None), P(), rows_spec,
    )
    out_specs = (
        rows_spec, rows_spec, P(), P(), P(None, "mp"), P(None, "mp"), P("mp", None), P(), P(), P(),
        P(None, "mp"), P("mp"), P("mp", None), P(),
    )

    def run(tokens_in, segment_ids, *rest):
        rows_all, seq_len, _ = tokens_in.shape
        plan = Plan(dp, mp, rows_all // dp, seq_len // mp, seq_len)
        return jax.shard_map(
            functools.partial(per_device, plan), mesh=mesh, in_specs=in_specs, out_specs=out_specs, check_vma=False
        )(tokens_in, segment_ids, *rest)

    return run
```

```python
import functools
import math

import jax
import jax.numpy as jnp
from jax import lax
from jax.experimental import pallas as pl
from jax.experimental.pallas import tpu as pltpu
from jax.sharding import PartitionSpec as P

HEAD_DIM = 64
EPS = 1e-06
MASKED = -1000000000.0
MESH = pl.DeviceIdType.MESH
BF = jnp.bfloat16
F32 = jnp.float32


class Plan:
    def __init__(self, dp, mp, rows_dev, tok_local, seq_len):
        self.dp, self.mp, self.rows_dev, self.tok, self.seq = dp, mp, rows_dev, tok_local, seq_len
        self.share = mp // math.gcd(rows_dev, mp)
        self.group_rows = rows_dev * self.share // mp
        self.own = self.group_rows // self.share
        if self.share % 2 or dp % self.share or dp % 4 or self.group_rows != self.own * self.share + 1:
            raise ValueError("unsupported sizes")
        self.groups = mp // self.share
        self.part = seq_len // self.share
        self.rows = self.own + 1
        self.hops = mp // 2
        self.all = dp * mp

    def ring_at(self, p):
        p = lax.rem(p, self.mp)
        back = lax.div(p, self.mp // 2)
        return 2 * p * (1 - back) + (2 * self.mp - 1 - 2 * p) * back


class Place:
    def __init__(self, plan):
        d, m = lax.axis_index("dp"), lax.axis_index("mp")
        odd = lax.rem(m, 2)
        self.d, self.m = d, m
        self.p = lax.div(m, 2) * (1 - odd) + (plan.mp - 1 - lax.div(m, 2)) * odd
        self.core = lax.rem(d, 2)
        self.sib = d + 1 - 2 * self.core
        self.y = lax.rem(lax.div(d, 2), 2)
        self.other = d + 2 - 4 * self.y
        self.k = lax.rem(d, plan.share)
        self.base = d - self.k
        self.quarter = 2 * self.y + self.core
        self.neighbour = (plan.ring_at(self.p + 1), plan.ring_at(self.p + plan.mp - 1))

    def away(self, plan, way, s):
        return plan.ring_at(self.p + plan.mp - s if way == 0 else self.p + s)


def greet(plan, at, everyone):
    barrier = pltpu.get_barrier_semaphore()
    span = plan.dp if everyone else max(plan.share, 4)
    base = lax.div(at.d, span) * span

    def one(i, carry):
        e, q = base + lax.div(i, plan.mp), lax.rem(i, plan.mp)

        @pl.when(jnp.logical_or(e != at.d, q != at.m))
        def _():
            pl.semaphore_signal(barrier, inc=1, device_id={"dp": e, "mp": q}, device_id_type=MESH)

        return carry

    lax.fori_loop(0, span * plan.mp, one, 0)
    pl.semaphore_wait(barrier, span * plan.mp - 1)


def remote(src, dst, send, recv, **to):
    return pltpu.make_async_remote_copy(src, dst, send, recv, device_id=to, device_id_type=MESH)


def settle(ref, sem):
    pltpu.make_async_copy(ref, ref, sem).wait()


def piece(ref, quarter, half=None):
    rows, cols = ref.shape[0] // 4, ref.shape[1]
    first = quarter * rows
    if half is None:
        return ref.at[pl.ds(pl.multiple_of(first, rows), rows)]
    if cols % 256 == 0:
        return ref.at[pl.ds(pl.multiple_of(first, rows), rows), pl.ds(half * (cols // 2), cols // 2)]
    return ref.at[pl.ds(pl.multiple_of(first + half * (rows // 2), rows // 2), rows // 2)]


def half_of(ref, half):
    rows, cols = ref.shape
    if cols % 256 == 0:
        return ref.at[:, pl.ds(half * (cols // 2), cols // 2)]
    return ref.at[pl.ds(half * (rows // 2), rows // 2)]


class Gatherer:
    def __init__(self, plan, at, shards, full, sems):
        self.plan, self.at, self.shards, self.full = plan, at, shards, full
        self.own_sem, self.ring_send, self.ring_recv, self.y_send, self.y_recv, self.sib_send, self.sib_recv = sems

    def _half(self, way, s):
        return way if s == self.plan.hops - 1 else None

    def ring(self, w, way, s):
        at, origin = self.at, self.at.away(self.plan, way, s)
        half = self._half(way, s)
        dst = piece(self.full[w].at[origin], at.quarter, half)
        src = piece(self.shards[w], at.quarter, half) if s == 0 else dst
        return remote(src, dst, self.ring_send.at[w, way], self.ring_recv.at[w, way, s], mp=at.neighbour[way])

    def cross(self, w, way, s):
        at, origin = self.at, self.at.away(self.plan, way, s + 1)
        block = piece(self.full[w].at[origin], at.quarter, self._half(way, s))
        return remote(block, block, self.y_send.at[w], self.y_recv.at[w, way, s], dp=at.other)

    def give(self, w, way, s, mine):
        at, origin = self.at, self.at.away(self.plan, way, s + 1)
        quarter = at.quarter if mine else 2 - 2 * at.y + at.core
        block = piece(self.full[w].at[origin], quarter, self._half(way, s))
        return remote(block, block, self.sib_send.at[w], self.sib_recv.at[w], dp=at.sib)

    def begin(self, w):
        for way in range(2):
            self.ring(w, way, 0).start()
        pltpu.make_async_copy(self.shards[w], self.full[w].at[self.at.m], self.own_sem.at[w]).start()

    def step(self, w, s):
        for way in range(2):
            self.ring(w, way, s).wait_recv()
            if s < self.plan.hops - 1:
                self.ring(w, way, s + 1).start()
            self.cross(w, way, s).start()
            self.give(w, way, s, True).start()

    def follow(self, w, s):
        for way in range(2):
            self.cross(w, way, s).wait_recv()
            self.give(w, way, s, False).start()

    def arrived(self, w):
        n, rows = self.plan.mp, self.shards[w].shape[0]
        settle(self.full[w].at[pl.ds(0, n - 1), pl.ds(0, rows // 2)], self.sib_recv.at[w])
        settle(self.shards[w], self.own_sem.at[w])

    def finish(self, w):
        n, rows = self.plan.mp, self.shards[w].shape[0]
        settle(self.full[w].at[pl.ds(0, n - 1), pl.ds(0, rows // 2)], self.sib_send.at[w])
        settle(self.full[w].at[pl.ds(0, n - 1), pl.ds(0, rows // 4)], self.y_send.at[w])
        for way in range(2):
            settle(self.full[w].at[pl.ds(0, self.plan.hops - 1), pl.ds(0, rows // 4)], self.ring_send.at[w, way])
            settle(piece(self.full[w].at[0], 0, way), self.ring_send.at[w, way])


def gatherer_sems(plan, count):
    dma = pltpu.SemaphoreType.DMA
    return [
        dma((count,)), dma((count, 2)), dma((count, 2, plan.hops)), dma((count,)), dma((count, 2, plan.hops)),
        dma((count,)), dma((count,)),
    ]


class RowsIn:
    def __init__(self, plan, at, src, dst, send, recv, whole_shared):
        self.plan, self.at, self.src, self.dst, self.send, self.recv = plan, at, src, dst, send, recv
        self.whole_shared = whole_shared

    def copies(self):
        plan, at = self.plan, self.at
        mine = pl.ds(pl.multiple_of(at.m * plan.tok, plan.tok), plan.tok)
        for j in range(plan.groups):
            q = at.k * plan.groups + j
            first = j * plan.group_rows
            for e in range(plan.share):
                here = jnp.logical_and(at.k == e, at.m == q)
                holds = True if self.whole_shared else lax.div(at.m * plan.tok, plan.part) == e
                to = lax.rem(at.m * plan.tok + plan.seq - e * plan.part, plan.seq)
                to = pl.ds(pl.multiple_of(to, plan.tok), plan.tok)
                yield here, True, q, e, j, 0, self.src.at[pl.ds(first + plan.own * e, plan.own)], self.dst.at[
                    pl.ds(0, plan.own), mine
                ]
                yield here, holds, q, e, j, 1, self.src.at[first + plan.own * plan.share], self.dst.at[plan.own, to]

    def start(self, only=None):
        for here, wanted, q, e, j, what, src, dst in self.copies():
            if only is not None and only != j:
                continue

            @pl.when(jnp.logical_and(here, wanted))
            def _():
                pltpu.make_async_copy(src, dst, self.recv.at[what]).start()

            @pl.when(jnp.logical_and(jnp.logical_not(here), wanted))
            def _():
                remote(src, dst, self.send.at[j, e, what], self.recv.at[what], dp=self.at.base + e, mp=q).start()

    def arrived(self):
        plan = self.plan
        settle(self.dst.at[pl.ds(0, plan.own)], self.recv.at[0])
        extent = plan.seq if self.whole_shared else plan.part
        settle(self.dst.at[plan.own, pl.ds(0, extent)], self.recv.at[1])

    def finish(self):
        for here, wanted, q, e, j, what, src, dst in self.copies():

            @pl.when(jnp.logical_and(jnp.logical_not(here), wanted))
            def _():
                settle(src, self.send.at[j, e, what])


def run(count, body, table):
    def one(j, carry):
        for when, thunks in sorted(table.items()):

            @pl.when(j == when)
            def _():
                for thunk in thunks:
                    thunk()

        body(j)
        return carry

    lax.fori_loop(0, count, one, 0)


def spread_over(count, thunks, first=0):
    table = {}
    for i, thunk in enumerate(thunks):
        table.setdefault(first + i * (count - first) // len(thunks), []).append(thunk)
    return table


def norm_rows(values, gain_vec, shift_vec):
    unit, _, normed = norm(values, gain_vec, shift_vec)
    return normed


def forward_kernel(
    plan, heads, tok, cot, seg, bq, bu, w0, w1, w2, w3, gain_one, shift_one, out_bias, gain_two, shift_two,
    tok_o, cot3, seg_o, g0, g1, g2, g3, proj_o, attn_o, hid_o, two_o, act_o, der_o,
    tok_v, one_v, wq_v, proj_v, attn_v, wo_v, hid_v, two_v, wu_v, act_v, der_v, seg_v, bq_v, bu_v,
    tok_send, tok_recv, cot_send, cot_recv, seg_send, seg_recv, bias_send, bias_recv, load_sem, save_sem, act_sem, *sems,
):
    n, share, own, part, seq = plan.mp, plan.share, plan.own, plan.part, plan.seq
    held = own * seq + part
    at = Place(plan)
    gat = Gatherer(plan, at, (w0, w1, w2, w3), (g0, g1, g2, g3), sems)
    tokens = RowsIn(plan, at, tok, tok_v, tok_send, tok_recv, True)
    cots = RowsIn(plan, at, cot, cot3, cot_send, cot_recv, False)
    hops = plan.hops
    greet(plan, at, False)

    gat.begin(0)
    tokens.start()
    biases = ((bq, bq_v, 0), (bu, bu_v, 1))
    for src, dst, i in biases:
        pltpu.make_async_copy(src, dst.at[at.m], bias_recv.at[i]).start()
        for s in range(1, n):
            remote(src, dst.at[at.m], bias_send.at[i], bias_recv.at[i], mp=lax.rem(at.m + s, n)).start()
    pltpu.make_async_copy(seg, seg_v.at[at.k], seg_recv.at[0]).start()
    for e in range(1, share):
        remote(seg, seg_v.at[at.k], seg_send.at[0], seg_recv.at[0], dp=at.base + lax.rem(at.k + e, share)).start()
    part_of = functools.partial
    hop = [[part_of(gat.step, w, s) for s in range(hops)] for w in range(4)]
    after = [[part_of(gat.follow, w, s) for s in range(hops)] for w in range(4)]
    gat.begin(1)
    gat.begin(2)
    hop[0][0]()
    for s in range(1, hops):
        hop[0][s]()
        after[0][s - 1]()
        if s == 1:
            hop[2][0]()
        if s == 2:
            hop[1][0]()
            after[2][0]()
            gat.begin(3)
    after[1][0]()
    after[0][hops - 1]()
    tokens.arrived()
    save_tok = pltpu.make_async_copy(tok_v, tok_o, save_sem.at[0])
    save_tok.start()
    gain, shift = gain_one[...], shift_one[...]

    @pl.loop(0, plan.rows * share)
    def _(b):
        r, first = lax.div(b, share), pl.multiple_of(lax.rem(b, share) * part, part)
        values = tok_v[r, pl.ds(first, part)].astype(F32)
        one_v[pl.ds(pl.multiple_of(b * part, part), part)] = norm_rows(values, gain, shift).astype(BF)

    settle(seg_v, seg_recv.at[0])
    labels = []
    for r in range(plan.rows):
        row = at.m * plan.group_rows + (own * at.k + r if r < own else own * share)
        line = seg_v[lax.div(row, plan.rows_dev), pl.ds(lax.rem(row, plan.rows_dev), 1)]
        if r == own:
            turned = line
            for e in range(1, share):
                moved = jnp.concatenate([line[:, e * part :], line[:, : e * part]], axis=1)
                turned = jnp.where(at.k == e, moved, turned)
            line = turned
        seg_o[pl.ds(r, 1)] = line
    for src, dst, i in biases:
        settle(dst, bias_recv.at[i])

    gat.arrived(0)
    load_q = pltpu.make_async_copy(g0, wq_v, load_sem.at[0])
    load_q.start()
    load_q.wait()

    def attend_shard(s):
        @pl.loop(0, plan.rows)
        def _(r):
            rows = pl.ds(pl.multiple_of(r * seq, seq), seq)
            projected = jnp.dot(one_v[rows], wq_v[s], preferred_element_type=F32) + bq_v[s]
            proj_v[s, rows] = projected.astype(BF)

        def head(r, first, count, h):
            col = h * 3 * HEAD_DIM
            query = proj_v[s, pl.ds(first, count), col : col + HEAD_DIM]
            keys = pl.ds(pl.multiple_of(r * seq, seq), seq)
            key = proj_v[s, keys, col + HEAD_DIM : col + 2 * HEAD_DIM]
            value = proj_v[s, keys, col + 2 * HEAD_DIM : col + 3 * HEAD_DIM]
            line = seg_o[pl.ds(r, 1)].astype(F32)
            column = jnp.transpose(jnp.broadcast_to(line, (128, seq)))[:count, :1]
            probs = scores_of(query, key, column == line).astype(BF)
            mixed = jnp.dot(probs, value, preferred_element_type=F32)
            attn_v[s, pl.ds(first, count), h * HEAD_DIM : (h + 1) * HEAD_DIM] = mixed.astype(BF)

        @pl.loop(0, own)
        def _(r):
            for h in range(heads):
                head(r, pl.multiple_of(r * seq, seq), seq, h)

        for h in range(heads):
            head(own, own * seq, part, h)

    moves = []
    for s in range(1, hops):
        moves += [hop[2][s], hop[1][s], part_of(cots.start, s - 1)]
        moves += [hop[3][s - 1], after[2][s], after[1][s]]
        moves += [after[3][s - 2]] if s > 1 else []
    for j in range(hops - 1, plan.groups):
        moves.append(part_of(cots.start, j))
    comm = spread_over(n, moves)
    run(n, attend_shard, comm)
    save_proj = pltpu.make_async_copy(proj_v, proj_o, save_sem.at[1])
    save_proj.start()
    save_attn = pltpu.make_async_copy(attn_v, attn_o, save_sem.at[2])
    save_attn.start()

    gat.arrived(1)
    load_o = pltpu.make_async_copy(g1, wo_v, load_sem.at[0])
    load_o.start()
    load_o.wait()
    bias, gain, shift = out_bias[...], gain_two[...], shift_two[...]

    @pl.loop(0, own * share + 1)
    def _(b):
        r, first = lax.div(b, share), pl.multiple_of(lax.rem(b, share) * part, part)
        rows = pl.ds(pl.multiple_of(b * part, part), part)
        total = tok_v[r, pl.ds(first, part)].astype(F32) + bias
        for s in range(n):
            total = total + jnp.dot(attn_v[s, rows], wo_v[s], preferred_element_type=F32)
        hid_v[rows] = total
        two_v[rows] = norm_rows(total, gain, shift).astype(BF)

    save_hid = pltpu.make_async_copy(hid_v, hid_o, save_sem.at[3])
    save_hid.start()
    save_two = pltpu.make_async_copy(two_v, two_o, save_sem.at[4])
    save_two.start()
    after[3][hops - 2]()
    hop[3][hops - 1]()
    gat.arrived(2)
    load_u = pltpu.make_async_copy(g2, wu_v, load_sem.at[0])
    load_u.start()
    load_u.wait()

    def feed_shard(s):
        @pl.loop(0, own * share + 1)
        def _(b):
            rows = pl.ds(pl.multiple_of(b * part, part), part)
            pre = jnp.dot(two_v[rows], wu_v[s], preferred_element_type=F32) + bu_v[s]
            below = 0.5 * (1.0 + lax.erf(pre * math.sqrt(0.5)))
            density = jnp.exp(-0.5 * pre * pre) * (1.0 / math.sqrt(2.0 * math.pi))
            act_v[s, rows] = (pre * below).astype(BF)
            der_v[s, rows] = below + pre * density

        pltpu.make_async_copy(act_v.at[s], act_o.at[s], act_sem.at[0]).start()
        pltpu.make_async_copy(der_v.at[s], der_o.at[s], act_sem.at[1]).start()

    run(n, feed_shard, {})
    after[3][hops - 1]()
    gat.arrived(3)
    for w in range(4):
        gat.finish(w)
    tokens.finish()
    cots.arrived()
    cots.finish()
    for src, dst, i in biases:
        settle(dst.at[pl.ds(0, n - 1)], bias_send.at[i])
    settle(seg_v.at[pl.ds(0, share - 1)], seg_send.at[0])
    for save in (save_tok, save_proj, save_attn, save_hid, save_two):
        save.wait()
    settle(act_v, act_sem.at[0])
    settle(der_v, act_sem.at[1])


def forward(plan, tokens_in, cotangent, segment_ids, biases, weights, vectors):
    n, share = plan.mp, plan.share
    width = tokens_in.shape[2]
    held, every = plan.own * plan.seq + plan.part, plan.rows * plan.seq
    any_space = pl.BlockSpec(memory_space=pl.ANY)
    in_vmem = pl.BlockSpec(memory_space=pltpu.VMEM)
    dma = pltpu.SemaphoreType.DMA
    rows = ((plan.rows, plan.seq, width), BF)
    heads = weights[1].shape[0] // HEAD_DIM
    local, three, ff = weights[1].shape[0], weights[0].shape[1], weights[2].shape[1]
    full = [((n,) + w.shape, BF) for w in weights]
    proj, attn = ((n, every, three), BF), ((n, held, local), BF)
    hid, two = ((held, width), F32), ((held, width), BF)
    act, der = ((n, held, ff), BF), ((n, held, ff), F32)
    outs = [rows, rows, ((plan.rows, plan.seq), jnp.int32), *full, proj, attn, hid, two, act, der]
    return pl.pallas_call(
        functools.partial(forward_kernel, plan, heads),
        out_shape=[jax.ShapeDtypeStruct(*o) for o in outs],
        in_specs=[any_space] * 9 + [in_vmem] * 5,
        out_specs=[any_space] * 2 + [in_vmem] + [any_space] * 10,
        scratch_shapes=[
            pltpu.VMEM(*rows), pltpu.VMEM((every, width), BF), pltpu.VMEM(*full[0]), pltpu.VMEM(*proj),
            pltpu.VMEM(*attn), pltpu.VMEM(*full[1]), pltpu.VMEM(*hid), pltpu.VMEM(*two), pltpu.VMEM(*full[2]),
            pltpu.VMEM(*act), pltpu.VMEM(*der), pltpu.VMEM((share,) + segment_ids.shape, jnp.int32),
            *[pltpu.VMEM((n,) + b.shape, F32) for b in biases],
            dma((plan.groups, share, 2)), dma((2,)), dma((plan.groups, share, 2)), dma((2,)), dma((1,)), dma((1,)),
            dma((2,)), dma((2,)), dma((1,)), dma((5,)), dma((2,)), *gatherer_sems(plan, 4),
        ],
        compiler_params=pltpu.CompilerParams(
            collective_id=0, has_side_effects=True, vmem_limit_bytes=58 << 20
        ),
        name="forward",
    )(tokens_in, cotangent, segment_ids, *biases, *weights, *vectors)


class Reducer:
    def __init__(self, plan, at, stage, loc, sbl, yrc, slot, fin, grp, out, sems):
        self.plan, self.at, self.stage = plan, at, stage
        self.loc, self.sbl, self.yrc, self.slot, self.fin, self.grp, self.out = loc, sbl, yrc, slot, fin, grp, out
        (
            self.sib_send, self.sib_recv, self.y_send, self.y_recv, self.ring_send, self.ring_recv,
            self.grp_send, self.grp_recv, self.fin_send, self.fin_recv, self.out_sem, self.credit,
        ) = sems
        hops = plan.hops
        self.order = [(0, hops)] + [(way, dist) for dist in range(hops - 1, 0, -1) for way in range(2)] + [(0, 0)]

    def target(self, i):
        n, hops = self.plan.mp, self.plan.hops
        dist = hops - lax.div(i + 1, 2)
        up = jnp.where(i == 0, 1, lax.rem(i, 2))
        return self.plan.ring_at(self.at.p + dist * up + (n - dist) * (1 - up))

    def give(self, u, yy, i):
        at, t = self.at, self.target(i)
        src = self.stage[u].at[2 * yy + 1 - at.core]
        return remote(src, self.sbl[u].at[yy, t], self.sib_send.at[u], self.sib_recv.at[u, i, yy], dp=at.sib)

    def begin(self, u, i):
        at, t = self.at, self.target(i)
        rows = self.stage[u].shape[1]
        for yy in range(2):
            self.give(u, yy, i).start()
        size = 32 if rows % 32 == 0 else rows
        for yy in range(2):

            @pl.loop(0, rows // size)
            def _(b):
                inner = pl.ds(pl.multiple_of(b * size, size), size)
                self.loc[u][yy, t, inner] = self.stage[u][2 * yy + at.core, inner]

    def given(self, u):
        settle(self.stage[u].at[pl.ds(0, 2)], self.sib_send.at[u])

    def clear(self, u):
        for way in range(2):
            part = half_of(self.slot[u].at[way, 0], 1 - way)
            part[...] = jnp.zeros(part.shape, BF)

    def add(self, u, yy, t, extra, put):
        rows = self.loc[u].shape[2]
        size = 32 if rows % 32 == 0 else rows

        def block(b):
            inner = pl.ds(pl.multiple_of(b * size, size), size)
            total = self.loc[u][yy, t, inner].astype(F32) + self.sbl[u][yy, t, inner].astype(F32)
            for ref in extra:
                total = total + ref[inner].astype(F32)
            put(inner, total)

        pl.loop(0, rows // size)(block)

    def cross(self, u, i):
        at, t = self.at, self.target(i)
        return remote(self.loc[u].at[1 - at.y, t], self.yrc[u].at[t], self.y_send.at[u], self.y_recv.at[u, i], dp=at.other)

    def first(self, u, i):
        at, t = self.at, self.target(i)
        self.give(u, 1 - at.y, i).wait_recv()

        def put(inner, total):
            self.loc[u][1 - at.y, t, inner] = total.astype(BF)

        self.add(u, 1 - at.y, t, (), put)
        self.cross(u, i).start()

    def hop(self, u, way, s, t):
        src = self.loc[u].at[self.at.y, t]
        dst = self.slot[u].at[way, s]
        if s == 0:
            src, dst = half_of(src, way), half_of(dst, way)
        return remote(
            src, dst, self.ring_send.at[u, way], self.ring_recv.at[u, way, s], mp=self.at.neighbour[way]
        )

    def step(self, u, i):
        at, t = self.at, self.target(i)
        way, dist = self.order[i]
        s = self.plan.hops - dist
        self.give(u, at.y, i).wait_recv()
        self.cross(u, i).wait_recv()
        extra = [self.yrc[u].at[t]]
        ways = (0, 1) if dist in (0, self.plan.hops) else (way,)
        if s > 0:
            for v in ways:
                self.hop(u, v, s - 1, t).wait_recv()
                extra.append(self.slot[u].at[v, s - 1])
        rows = self.loc[u].shape[2]
        quads = self.plan.dp // 4

        def put(inner, total):
            if dist:
                self.loc[u][at.y, t, inner] = total.astype(BF)
            elif quads > 1:
                self.grp[u][lax.div(at.d, 4), inner] = total.astype(BF)
            else:
                to = pl.ds(pl.multiple_of(at.quarter * rows + inner.start, inner.size), inner.size)
                self.fin[u][to] = total.astype(BF)

        self.add(u, at.y, t, extra, put)
        if dist:
            for v in ways:
                self.hop(u, v, s, t).start()
        else:
            for other in range(1, quads):
                self.between(u, other).start()

    def between(self, u, other):
        at = self.at
        to = lax.rem(at.d + 4 * other, self.plan.dp)
        block = self.grp[u].at[lax.div(at.d, 4)]
        return remote(block, block, self.grp_send.at[u], self.grp_recv.at[u], dp=to)

    def share_out(self, u, what):
        at = self.at
        quarter = at.quarter if what != 1 else 2 - 2 * at.y + at.core
        block = piece(self.fin[u], quarter)
        to = at.other if what == 2 else at.sib
        return remote(block, block, self.fin_send.at[u, what], self.fin_recv.at[u, what], dp=to)

    def last(self, u):
        quads = self.plan.dp // 4
        if quads > 1:
            rows = self.loc[u].shape[2]
            settle(self.grp[u].at[pl.ds(0, quads - 1)], self.grp_recv.at[u])
            total = self.grp[u][0].astype(F32)
            for other in range(1, quads):
                total = total + self.grp[u][other].astype(F32)
            self.fin[u][pl.ds(pl.multiple_of(self.at.quarter * rows, rows), rows)] = total.astype(BF)
        self.share_out(u, 2).start()
        self.share_out(u, 0).start()

    def spread(self, u):
        self.share_out(u, 2).wait_recv()
        self.share_out(u, 1).start()

    def write(self, u, dst):
        self.share_out(u, 0).wait_recv()
        self.share_out(u, 1).wait_recv()
        rows = self.loc[u].shape[2]

        @pl.loop(0, 4)
        def _(q):
            at = pl.ds(pl.multiple_of(q * rows, rows), rows)
            slot = lax.rem(q, 2)

            @pl.when(q > 1)
            def _():
                settle(self.out.at[slot], self.out_sem.at[slot])

            self.out[slot] = self.fin[u][at].astype(F32)
            pltpu.make_async_copy(self.out.at[slot], dst.at[at], self.out_sem.at[slot]).start()

        for slot in range(2):
            settle(self.out.at[slot], self.out_sem.at[slot])

    def sent(self, u):
        hops = self.plan.hops
        settle(self.loc[u].at[0], self.y_send.at[u])
        for way in range(2):
            settle(self.slot[u].at[way, pl.ds(0, hops - 1)], self.ring_send.at[u, way])
            settle(half_of(self.slot[u].at[way, 0], way), self.ring_send.at[u, way])

    def release(self, u):
        at = self.at
        self.sent(u)
        for to in ({"dp": at.sib}, {"dp": at.other}, {"mp": at.neighbour[0]}, {"mp": at.neighbour[1]}):
            pl.semaphore_signal(self.credit, inc=1, device_id=to, device_id_type=MESH)

    def claim(self):
        pl.semaphore_wait(self.credit, 4)

    def finish(self, u):
        for what in range(3):
            self.share_out(u, what).wait_send()
        for other in range(1, self.plan.dp // 4):
            self.between(u, other).wait_send()


class RowsOut:
    def __init__(self, plan, at, src, shared, dst, send, recv):
        self.plan, self.at, self.src, self.shared, self.dst, self.send, self.recv = plan, at, src, shared, dst, send, recv
        self.home = at.base + lax.div(at.m, plan.groups)
        self.first = lax.rem(at.m, plan.groups) * plan.group_rows

    def copies(self, what):
        plan, at = self.plan, self.at
        for q in range(plan.mp):
            here = jnp.logical_and(self.home == at.d, at.m == q)
            toks = pl.ds(q * plan.tok, plan.tok)
            if what == 0:
                yield q, here, True, self.src.at[pl.ds(0, plan.own), toks], self.dst.at[
                    pl.ds(self.first + plan.own * at.k, plan.own)
                ]
            else:
                holds = at.k == (q * plan.tok) // plan.part
                yield q, here, holds, self.shared.at[pl.ds((q * plan.tok) % plan.part, plan.tok)], self.dst.at[
                    self.first + plan.own * plan.share
                ]

    def start(self, what):
        for q, here, wanted, src, dst in self.copies(what):

            @pl.when(jnp.logical_and(here, wanted))
            def _():
                pltpu.make_async_copy(src, dst, self.recv.at[0]).start()

            @pl.when(jnp.logical_and(jnp.logical_not(here), wanted))
            def _():
                remote(src, dst, self.send.at[q, what], self.recv.at[0], dp=self.home, mp=q).start()

    def finish(self):
        settle(self.dst, self.recv.at[0])
        for what in range(2):
            for q, here, wanted, src, dst in self.copies(what):

                @pl.when(jnp.logical_and(jnp.logical_not(here), wanted))
                def _():
                    settle(src, self.send.at[q, what])


ACROSS = (((1,), (1,)), ((), ()))
DOWN = (((0,), (0,)), ((), ()))


def backward_kernel(
    plan, heads, g0, g1, g2, g3, tok, cot, seg, proj, attn, hid, two, act, der, gain_one, shift_one, gain_two, down_bias,
    blk, tg, o0, o1, o2, vout, *rest,
):
    n, share, own, part, seq = plan.mp, plan.share, plan.own, plan.part, plan.seq
    hops = plan.hops
    held, every = own * seq + part, plan.rows * seq
    width, ff, three, local = hid.shape[1], act.shape[2], proj.shape[2], attn.shape[2]
    (
        stage_a, stage_b, loc_a, loc_b, sbl_a, sbl_b, yrc_a, yrc_b, slot_a, slot_b, fin_a, fin_b, fin_c,
        grp_a, grp_b, grp_c, out_v,
    ) = rest[:17]
    sems, rest = rest[17:29], rest[29:]
    (
        grad_v, low_v, block_v, tgs, tgo, sums, ups, qbs, msg, vrc, vsum,
        load_sem, wgt_sem, blk_send, blk_recv, tg_send, tg_recv, tgs_send, tgs_recv, tgl_sem, v_send, v_recv,
    ) = rest
    at = Place(plan)
    red = Reducer(
        plan, at, (stage_a, stage_b, stage_a), (loc_a, loc_b, loc_a), (sbl_a, sbl_b, sbl_a), (yrc_a, yrc_b, yrc_a),
        (slot_a, slot_b, slot_a), (fin_a, fin_b, fin_c), (grp_a, grp_b, grp_c), out_v, sems,
    )
    blocks = RowsOut(plan, at, block_v, block_v.at[own], blk, blk_send, blk_recv)
    greet(plan, at, True)
    part_of = functools.partial
    count = len(red.order)
    first = [[part_of(red.first, u, i) for i in range(count)] for u in range(3)]
    step = [[part_of(red.step, u, i) for i in range(count)] for u in range(3)]
    red.clear(0)
    red.clear(1)
    sums[...] = jnp.zeros(sums.shape, F32)
    blocks_held = own * share + 1

    def stream(loads, i):
        def copies(j, slot):
            t = red.target(j)
            for what, (src, dst) in enumerate(loads):
                yield pltpu.make_async_copy(src.at[t], dst.at[slot], wgt_sem.at[what, slot])

        if isinstance(i, int):
            for copy in copies(i, i % 2):
                copy.start()
            return

        @pl.when(i + 1 < n)
        def _():
            for copy in copies(i + 1, lax.rem(i + 1, 2)):
                copy.start()

        for copy in copies(i, lax.rem(i, 2)):
            copy.wait()

    def feed_forward(wd_v, wu_v, act_v, der_v, low_pre, two_v, cot_v, hid_v, sum_v):
        loads = ((g3, wd_v), (g2, wu_v), (act, act_v), (der, der_v))
        stream(loads, 0)
        small = [pltpu.make_async_copy(two, two_v, load_sem.at[0]), pltpu.make_async_copy(hid, hid_v, load_sem.at[1])]
        for r in range(plan.rows):
            extent = seq if r < own else part
            small.append(
                pltpu.make_async_copy(
                    cot.at[r, pl.ds(0, extent)], cot_v.at[pl.ds(r * seq, extent)], load_sem.at[2 + r]
                )
            )
        for copy in small:
            copy.start()
        for copy in small:
            copy.wait()

        @pl.loop(0, blocks_held)
        def _(b):
            rows = pl.ds(pl.multiple_of(b * part, part), part)
            sum_v[rows] = hid_v[rows] + down_bias[...]
            grad_v[rows] = jnp.zeros((part, width), F32)

        def body(i):
            stream(loads, i)
            slot = lax.rem(i, 2)
            rows = ff // 4

            @pl.when(i > 0)
            def _():
                red.given(0)
                red.given(1)

            for q in range(4):
                lhs = act_v[slot, :, q * rows : (q + 1) * rows]
                stage_a[q] = lax.dot_general(lhs, cot_v[...], DOWN, preferred_element_type=F32).astype(BF)
            red.begin(0, i)

            def block(b, total):
                at_rows = pl.ds(pl.multiple_of(b * part, part), part)
                act_grad = lax.dot_general(cot_v[at_rows], wd_v[slot], ACROSS, preferred_element_type=F32)
                low = (act_grad * der_v[slot, at_rows]).astype(BF)
                low_pre[at_rows] = low
                grad_v[at_rows] += lax.dot_general(low, wu_v[slot], ACROSS, preferred_element_type=F32)
                sum_v[at_rows] += jnp.dot(act_v[slot, at_rows], wd_v[slot], preferred_element_type=F32)
                return total + jnp.sum(low.astype(F32), axis=0, keepdims=True)

            total = lax.fori_loop(0, blocks_held, block, jnp.zeros((1, ff), F32))
            ups[red.target(i)] = total
            for q in range(4):
                lhs = low_pre[:, q * rows : (q + 1) * rows]
                stage_b[q] = lax.dot_general(lhs, two_v[...], DOWN, preferred_element_type=F32).astype(BF)
            red.begin(1, i)

        table = {}
        for i in range(count - 1):
            table.setdefault(i + 1, []).append(first[0][i])
        for i in range(count - 2):
            table.setdefault(i + 2, []).append(step[0][i])
        run(n, body, table)
        red.given(0)
        red.given(1)
        first[0][count - 1]()
        first[1][0]()
        step[0][count - 2]()
        first[1][1]()

        @pl.loop(0, blocks_held)
        def _(b):
            r, start = lax.div(b, share), pl.multiple_of(lax.rem(b, share) * part, part)
            rows = pl.ds(pl.multiple_of(b * part, part), part)
            block_v[r, pl.ds(start, part)] = sum_v[rows].astype(BF)
            hidden, grad, cot_f = hid_v[rows], grad_v[rows], cot_v[rows].astype(F32)
            unit, scale, _ = norm(hidden, gain_two[...], 0.0)
            hidden_grad = cot_f + norm_back(unit, scale, gain_two[...], grad)
            grad_v[rows] = hidden_grad
            low_v[rows] = hidden_grad.astype(BF)
            for line, value in ((2, hidden_grad), (3, grad * unit), (4, grad), (5, cot_f)):
                sums[pl.ds(line, 1)] += jnp.sum(value, axis=0, keepdims=True)

        blocks.start(0)
        blocks.start(1)

    pl.run_scoped(
        feed_forward,
        pltpu.VMEM((2,) + g3.shape[1:], BF), pltpu.VMEM((2,) + g2.shape[1:], BF), pltpu.VMEM((2, held, ff), BF),
        pltpu.VMEM((2, held, ff), F32), pltpu.VMEM((held, ff), BF), pltpu.VMEM((held, width), BF),
        pltpu.VMEM((held, width), BF), pltpu.VMEM((held, width), F32), pltpu.VMEM((held, width), F32),
    )

    def attention(wq_v, wo_v, proj_v, attn_v, head_v, three_v, tok_v, one_v, back_v, out3):
        loads = ((g0, wq_v), (g1, wo_v), (proj, proj_v), (attn, attn_v))
        stream(loads, 0)
        load = pltpu.make_async_copy(tok, tok_v, load_sem.at[0])
        load.start()
        step[0][count - 1]()
        red.last(0)
        for i in range(2, count):
            first[1][i]()
        red.spread(0)
        red.release(0)
        load.wait()

        @pl.loop(0, plan.rows * share)
        def _(b):
            r, start = lax.div(b, share), pl.multiple_of(lax.rem(b, share) * part, part)
            rows = pl.ds(pl.multiple_of(b * part, part), part)
            values = tok_v[r, pl.ds(start, part)].astype(F32)
            one_v[rows] = norm_rows(values, gain_one[...], shift_one[...]).astype(BF)
            back_v[rows] = jnp.zeros((part, width), F32)

        three_v[...] = jnp.zeros(three_v.shape, BF)
        red.claim()

        def body(i):
            stream(loads, i)
            slot = lax.rem(i, 2)

            @pl.loop(0, blocks_held)
            def _(b):
                rows = pl.ds(pl.multiple_of(b * part, part), part)
                grad = lax.dot_general(low_v[rows], wo_v[slot], ACROSS, preferred_element_type=F32)
                head_v[rows] = grad.astype(BF)

            def head(r, queries, amount, h):
                col = h * 3 * HEAD_DIM
                keys = pl.ds(pl.multiple_of(r * seq, seq), seq)
                query = proj_v[slot, pl.ds(queries, amount), col : col + HEAD_DIM]
                key = proj_v[slot, keys, col + HEAD_DIM : col + 2 * HEAD_DIM]
                value = proj_v[slot, keys, col + 2 * HEAD_DIM : col + 3 * HEAD_DIM]
                head_grad = head_v[pl.ds(queries, amount), h * HEAD_DIM : (h + 1) * HEAD_DIM]
                line = seg[pl.ds(r, 1)].astype(F32)
                column = jnp.transpose(jnp.broadcast_to(line, (128, seq)))[:amount, :1]
                allowed = column == line
                full = scores_of(query, key, allowed)
                value_grad = lax.dot_general(full.astype(BF), head_grad, DOWN, preferred_element_type=F32)
                probs_grad = lax.dot_general(head_grad, value, ACROSS, preferred_element_type=F32)
                delta = jnp.sum(probs_grad * full, axis=-1, keepdims=True)
                low = (jnp.where(allowed, full * (probs_grad - delta), 0.0) * HEAD_DIM ** (-0.5)).astype(BF)
                query_grad = jnp.dot(low, key, preferred_element_type=F32)
                key_grad = lax.dot_general(low, query, DOWN, preferred_element_type=F32)
                three_v[pl.ds(queries, amount), col : col + HEAD_DIM] = query_grad.astype(BF)
                three_v[keys, col + HEAD_DIM : col + 2 * HEAD_DIM] = key_grad.astype(BF)
                three_v[keys, col + 2 * HEAD_DIM : col + 3 * HEAD_DIM] = value_grad.astype(BF)

            @pl.loop(0, own)
            def _(r):
                for h in range(heads):
                    head(r, pl.multiple_of(r * seq, seq), seq, h)

            for h in range(heads):
                head(own, own * seq, part, h)

            @pl.when(i > 0)
            def _():
                red.given(2)

            wide, narrow = three // 4, local // 4
            weight = lax.dot_general(three_v[...], one_v[...], DOWN, preferred_element_type=F32).astype(BF)
            out_weight = lax.dot_general(attn_v[slot], low_v[...], DOWN, preferred_element_type=F32).astype(BF)
            for q in range(4):
                stage_a[q, :wide] = weight[q * wide : (q + 1) * wide]
                stage_a[q, wide:] = out_weight[q * narrow : (q + 1) * narrow]
            red.begin(2, i)

            def block(b, total):
                rows = pl.ds(pl.multiple_of(b * part, part), part)
                low = three_v[rows]
                back_v[rows] += lax.dot_general(low, wq_v[slot], ACROSS, preferred_element_type=F32)
                return total + jnp.sum(low.astype(F32), axis=0, keepdims=True)

            qbs[red.target(i)] = lax.fori_loop(0, plan.rows * share, block, jnp.zeros((1, three), F32))

        table = {}
        for i in range(count):
            table.setdefault(i, []).append(step[1][i])
            if i + 1 < count:
                table.setdefault(i + 1, []).append(first[2][i])
        run(n, body, table)
        red.last(1)
        red.given(2)
        first[2][count - 1]()

        @pl.loop(0, plan.rows * share)
        def _(b):
            r, start = lax.div(b, share), pl.multiple_of(lax.rem(b, share) * part, part)
            rows = pl.ds(pl.multiple_of(b * part, part), part)
            unit, scale, _ = norm(tok_v[r, pl.ds(start, part)].astype(F32), gain_one[...], 0.0)
            grad = back_v[rows]
            for line, value in ((0, grad * unit), (1, grad)):
                sums[pl.ds(line, 1)] += jnp.sum(value, axis=0, keepdims=True)
            grad = norm_back(unit, scale, gain_one[...], grad)

            @pl.when(b < blocks_held)
            def _():
                mine = pl.ds(pl.multiple_of(jnp.minimum(b, blocks_held - 1) * part, part), part)
                out3[r, pl.ds(start, part)] = (grad + grad_v[mine]).astype(BF)

            @pl.when(b >= blocks_held)
            def _():
                out3[r, pl.ds(start, part)] = grad.astype(BF)

        tokens = RowsOut(plan, at, out3, tgo, tg, tg_send, tg_recv)
        for e in range(share):
            src = out3.at[own, pl.ds(e * part, part)]
            if e == 0:
                pltpu.make_async_copy(src, tgs.at[0], tgl_sem.at[0]).start()
            else:
                to = at.base + lax.rem(at.k + e, share)
                remote(src, tgs.at[share - e], tgs_send.at[e], tgs_recv.at[share - e], dp=to).start()
        tokens.start(0)

        lines = [-(-size // 128) for size in (ff, three)]
        msg[...] = jnp.zeros(msg.shape, F32)
        for q in range(n):
            msg[q, :8, : width // n] = sums[:, q * (width // n) : (q + 1) * (width // n)]
            line = 8
            for ref, size in ((ups, ff), (qbs, three)):
                for first_col in range(0, size, 128):
                    cols = min(128, size - first_col)
                    msg[q, line : line + 1, :cols] = ref[q, :, first_col : first_col + cols]
                    line += 1
        me = at.d * n + at.m

        def one(i, carry):
            to = lax.rem(me + i, plan.all)
            e, q = lax.div(to, n), lax.rem(to, n)
            remote(msg.at[q], vrc.at[me], v_send.at[0], v_recv.at[0], dp=e, mp=q).start()
            return carry

        lax.fori_loop(1, plan.all, one, 0)
        pltpu.make_async_copy(msg.at[at.m], vrc.at[me], v_recv.at[0]).start()
        step[2][0]()
        for e in range(1, share):
            settle(tgs.at[e], tgs_recv.at[e])
        settle(tgs.at[0], tgl_sem.at[0])
        tgo[...] = sum(tgs[e].astype(F32) for e in range(share)).astype(BF)
        tokens.start(1)
        step[2][1]()
        red.spread(1)
        settle(vrc, v_recv.at[0])
        vsum[...] = jnp.sum(vrc[...], axis=0)
        for e in range(1, n):
            remote(vsum, vout.at[at.m], v_send.at[1], v_recv.at[1], mp=lax.rem(at.m + e, n)).start()
        pltpu.make_async_copy(vsum, vout.at[at.m], v_recv.at[1]).start()
        red.write(0, o0)
        for i in range(2, count):
            step[2][i]()
            if i == 3:
                red.write(1, o1)
        red.last(2)
        red.spread(2)
        red.write(2, o2)
        for u in range(3):
            red.finish(u)
        red.sent(1)
        red.sent(2)
        for e in range(1, share):
            settle(tgs.at[0], tgs_send.at[e])
        blocks.finish()
        tokens.finish()
        settle(vout, v_recv.at[1])
        settle(vrc.at[pl.ds(0, plan.all - 1)], v_send.at[0])
        settle(vout.at[pl.ds(0, n - 1)], v_send.at[1])

    pl.run_scoped(
        attention,
        pltpu.VMEM((2,) + g0.shape[1:], BF), pltpu.VMEM((2,) + g1.shape[1:], BF), pltpu.VMEM((2, every, three), BF),
        pltpu.VMEM((2, held, local), BF), pltpu.VMEM((held, local), BF), pltpu.VMEM((every, three), BF),
        pltpu.VMEM((plan.rows, seq, width), BF), pltpu.VMEM((every, width), BF), pltpu.VMEM((every, width), F32),
        pltpu.VMEM((plan.rows, seq, width), BF),
    )


def backward(plan, weights, tok3, cot3, seg, proj, attn, hid, two, act, der, vectors):
    n, share = plan.mp, plan.share
    held, width = hid.shape
    ff, three, local = act.shape[2], proj.shape[2], attn.shape[2]
    heads = local // HEAD_DIM
    quads, quarter = plan.dp // 4, ff // 4
    if local + three != ff:
        raise ValueError("unsupported sizes")
    any_space = pl.BlockSpec(memory_space=pl.ANY)
    in_vmem = pl.BlockSpec(memory_space=pltpu.VMEM)
    dma = pltpu.SemaphoreType.DMA
    rows = jax.ShapeDtypeStruct((plan.rows_dev, plan.tok, width), BF)
    shard = jax.ShapeDtypeStruct((ff, width), F32)
    size = 8 + -(-ff // 128) + -(-three // 128)
    size = -(-size // 8) * 8
    vec = (size, 128)
    return pl.pallas_call(
        functools.partial(backward_kernel, plan, heads),
        out_shape=[rows, rows, shard, shard, shard, jax.ShapeDtypeStruct((n,) + vec, F32)],
        in_specs=[any_space] * 6 + [in_vmem] + [any_space] * 6 + [in_vmem] * 4,
        out_specs=[any_space] * 6,
        scratch_shapes=[
            *[pltpu.VMEM((4, quarter, width), BF)] * 2,
            *[pltpu.VMEM((2, n, quarter, width), BF)] * 4,
            *[pltpu.VMEM((n, quarter, width), BF)] * 2,
            *[pltpu.VMEM((2, plan.hops, quarter, width), BF)] * 2,
            *[pltpu.VMEM((ff, width), BF)] * 3,
            *[pltpu.VMEM((quads,) + ((quarter, width) if quads > 1 else (8, 128)), BF)] * 3,
            pltpu.VMEM((2, quarter, width), F32),
            dma((3,)), dma((3, n, 2)), dma((3,)), dma((3, n)), dma((3, 2)), dma((3, 2, plan.hops)), dma((3,)), dma((3,)),
            dma((3, 3)), dma((3, 3)), dma((2,)), pltpu.SemaphoreType.REGULAR,
            pltpu.VMEM((held, width), F32), pltpu.VMEM((held, width), BF), pltpu.VMEM((plan.rows, plan.seq, width), BF),
            pltpu.VMEM((share, plan.part, width), BF), pltpu.VMEM((plan.part, width), BF), pltpu.VMEM((8, width), F32),
            pltpu.VMEM((n, 1, ff), F32), pltpu.VMEM((n, 1, three), F32), pltpu.VMEM((n,) + vec, F32),
            pltpu.VMEM((plan.all,) + vec, F32), pltpu.VMEM(vec, F32),
            dma((2 + plan.rows,)), dma((4, 2)), dma((n, 2)), dma((1,)), dma((n, 2)), dma((1,)), dma((share,)),
            dma((share,)), dma((1,)), dma((2,)), dma((2,)),
        ],
        compiler_params=pltpu.CompilerParams(
            collective_id=1, has_side_effects=True, vmem_limit_bytes=61 << 20
        ),
        name="backward",
    )(*weights, tok3, cot3, seg, proj, attn, hid, two, act, der, *vectors)


def scores_of(query, key, allowed):
    raw = lax.dot_general(query, key, (((1,), (1,)), ((), ())), preferred_element_type=F32)
    scores = jnp.where(allowed, raw * HEAD_DIM ** (-0.5), MASKED)
    raised = jnp.exp(scores - jnp.max(scores, axis=-1, keepdims=True))
    return raised / jnp.sum(raised, axis=-1, keepdims=True)


def norm(values, gain_vec, shift_vec):
    centred = values - jnp.mean(values, axis=-1, keepdims=True)
    scale = lax.rsqrt(jnp.mean(centred * centred, axis=-1, keepdims=True) + EPS)
    unit = centred * scale
    return unit, scale, unit * gain_vec + shift_vec


def norm_back(unit, scale, gain_vec, grad):
    pulled = grad * gain_vec
    inner = jnp.mean(pulled * unit, axis=-1, keepdims=True)
    return scale * (pulled - jnp.mean(pulled, axis=-1, keepdims=True) - unit * inner)


def per_device(
    plan, tokens_in, segment_ids, attn_gain, attn_shift, qkv_weight, qkv_bias, out_weight, out_bias, mlp_gain, mlp_shift,
    up_weight, up_bias, down_weight, down_bias, cotangent,
):
    n, width = plan.mp, tokens_in.shape[2]
    ff_local = up_weight.shape[1]
    heads_local = qkv_bias.shape[1] // HEAD_DIM
    parts = qkv_bias.reshape(2, heads_local, HEAD_DIM)
    bias_three = jnp.stack([parts[0], jnp.zeros_like(parts[0]), parts[1]], axis=1).reshape(1, -1)
    vectors = [v.reshape(1, width) for v in (attn_gain, attn_shift, out_bias, mlp_gain, mlp_shift)]
    tok3, cot3, seg, wq, wo, wu, wd, proj, attn, hidden, normed_two, act_low, gelu_slope = forward(
        plan, tokens_in, cotangent, segment_ids, (bias_three, up_bias.reshape(1, ff_local)),
        (qkv_weight, out_weight, up_weight, down_weight), vectors,
    )
    block_out, tokens_low, down_grad, up_grad, rest_grad, sums = backward(
        plan, (wq, wo, wu, wd), tok3, cot3, seg, proj, attn, hidden, normed_two, act_low, gelu_slope,
        [v.reshape(1, width) for v in (attn_gain, attn_shift, mlp_gain, down_bias)],
    )
    local, three = out_weight.shape[0], qkv_weight.shape[1]
    rest_grad = rest_grad.reshape(4, (local + three) // 4, width)
    qkv_grad = rest_grad[:, : three // 4].reshape(three, width).T
    out_grad = rest_grad[:, three // 4 :].reshape(local, width)
    six = jnp.swapaxes(sums[:, :6, : width // n], 0, 1).reshape(6, width)
    mine = lax.dynamic_index_in_dim(sums, lax.axis_index("mp"), 0, keepdims=False)
    lines = [-(-size // 128) for size in (ff_local, three)]
    up_bias_grad = mine[8 : 8 + lines[0]].reshape(-1)[:ff_local]
    bias_sums = mine[8 + lines[0] : 8 + sum(lines)].reshape(-1)[:three].reshape(heads_local, 3, HEAD_DIM)
    qkv_bias_grad = jnp.stack([bias_sums[:, 0], bias_sums[:, 2]]).reshape(2, local)
    return (
        block_out, tokens_low.astype(F32), six[0], six[1], qkv_grad, qkv_bias_grad, out_grad, six[2], six[3], six[4],
        up_grad.T, up_bias_grad, down_grad, six[5],
    )


def solution(mesh):
    dp, mp = mesh.shape["dp"], mesh.shape["mp"]
    rows_spec = P("dp", "mp", None)
    in_specs = (
        rows_spec, P("dp", None), P(), P(), P(None, "mp"), P(None, "mp"), P("mp", None), P(), P(), P(),
        P(None, "mp"), P("mp"), P("mp", None), P(), rows_spec,
    )
    out_specs = (
        rows_spec, rows_spec, P(), P(), P(None, "mp"), P(None, "mp"), P("mp", None), P(), P(), P(),
        P(None, "mp"), P("mp"), P("mp", None), P(),
    )

    def run(tokens_in, segment_ids, *rest):
        rows_all, seq_len, _ = tokens_in.shape
        plan = Plan(dp, mp, rows_all // dp, seq_len // mp, seq_len)
        return jax.shard_map(
            functools.partial(per_device, plan), mesh=mesh, in_specs=in_specs, out_specs=out_specs, check_vma=False
        )(tokens_in, segment_ids, *rest)

    return run
```

```python
import functools
import math

import jax
import jax.numpy as jnp
from jax import lax
from jax.experimental import pallas as pl
from jax.experimental.pallas import tpu as pltpu
from jax.sharding import PartitionSpec as P

HEAD_DIM = 64
EPS = 1e-06
MASKED = -1000000000.0
MESH = pl.DeviceIdType.MESH
BF = jnp.bfloat16
F32 = jnp.float32
ACROSS = (((1,), (1,)), ((), ()))
DOWN = (((0,), (0,)), ((), ()))


class Plan:
    def __init__(self, dp, mp, rows_dev, tok_local, seq_len):
        self.dp, self.mp, self.rows_dev, self.tok, self.seq = dp, mp, rows_dev, tok_local, seq_len
        self.share = mp // math.gcd(rows_dev, mp)
        self.group_rows = rows_dev * self.share // mp
        self.own = self.group_rows // self.share
        if self.share % 2 or dp % self.share or dp % 4 or self.group_rows != self.own * self.share + 1:
            raise ValueError("unsupported sizes")
        self.groups = mp // self.share
        self.part = seq_len // self.share
        self.rows = self.own + 1
        self.hops = mp // 2
        self.all = dp * mp

    def ring_at(self, p):
        p = lax.rem(p, self.mp)
        back = lax.div(p, self.mp // 2)
        return 2 * p * (1 - back) + (2 * self.mp - 1 - 2 * p) * back


class Place:
    def __init__(self, plan):
        d, m = lax.axis_index("dp"), lax.axis_index("mp")
        odd = lax.rem(m, 2)
        self.d, self.m = d, m
        self.p = lax.div(m, 2) * (1 - odd) + (plan.mp - 1 - lax.div(m, 2)) * odd
        self.core = lax.rem(d, 2)
        self.sib = d + 1 - 2 * self.core
        self.y = lax.rem(lax.div(d, 2), 2)
        self.other = d + 2 - 4 * self.y
        self.k = lax.rem(d, plan.share)
        self.base = d - self.k
        self.quarter = 2 * self.y + self.core
        self.neighbour = (plan.ring_at(self.p + 1), plan.ring_at(self.p + plan.mp - 1))

    def away(self, plan, way, s):
        return plan.ring_at(self.p + plan.mp - s if way == 0 else self.p + s)


def greet(plan, at, everyone):
    barrier = pltpu.get_barrier_semaphore()
    span = plan.dp if everyone else max(plan.share, 4)
    base = lax.div(at.d, span) * span

    def one(i, carry):
        e, q = base + lax.div(i, plan.mp), lax.rem(i, plan.mp)

        @pl.when(jnp.logical_or(e != at.d, q != at.m))
        def _():
            pl.semaphore_signal(barrier, inc=1, device_id={"dp": e, "mp": q}, device_id_type=MESH)

        return carry

    lax.fori_loop(0, span * plan.mp, one, 0)
    pl.semaphore_wait(barrier, span * plan.mp - 1)


def remote(src, dst, send, recv, **to):
    return pltpu.make_async_remote_copy(src, dst, send, recv, device_id=to, device_id_type=MESH)


def settle(ref, sem):
    pltpu.make_async_copy(ref, ref, sem).wait()


def piece(ref, quarter, half=None):
    rows, cols = ref.shape[0] // 4, ref.shape[1]
    first = quarter * rows
    if half is None:
        return ref.at[pl.ds(pl.multiple_of(first, rows), rows)]
    if cols % 256 == 0:
        return ref.at[pl.ds(pl.multiple_of(first, rows), rows), pl.ds(half * (cols // 2), cols // 2)]
    return ref.at[pl.ds(pl.multiple_of(first + half * (rows // 2), rows // 2), rows // 2)]


def half_of(ref, half):
    rows, cols = ref.shape
    if cols % 256 == 0:
        return ref.at[:, pl.ds(half * (cols // 2), cols // 2)]
    return ref.at[pl.ds(half * (rows // 2), rows // 2)]


class Gatherer:
    def __init__(self, plan, at, shards, full, sems):
        self.plan, self.at, self.shards, self.full = plan, at, shards, full
        self.own_sem, self.ring_send, self.ring_recv, self.y_send, self.y_recv, self.sib_send, self.sib_recv = sems

    def _half(self, way, s):
        return way if s == self.plan.hops - 1 else None

    def ring(self, w, way, s):
        at, origin = self.at, self.at.away(self.plan, way, s)
        half = self._half(way, s)
        dst = piece(self.full[w].at[origin], at.quarter, half)
        src = piece(self.shards[w], at.quarter, half) if s == 0 else dst
        return remote(src, dst, self.ring_send.at[w, way], self.ring_recv.at[w, way, s], mp=at.neighbour[way])

    def cross(self, w, way, s):
        at, origin = self.at, self.at.away(self.plan, way, s + 1)
        block = piece(self.full[w].at[origin], at.quarter, self._half(way, s))
        return remote(block, block, self.y_send.at[w], self.y_recv.at[w, way, s], dp=at.other)

    def give(self, w, way, s, mine):
        at, origin = self.at, self.at.away(self.plan, way, s + 1)
        quarter = at.quarter if mine else 2 - 2 * at.y + at.core
        block = piece(self.full[w].at[origin], quarter, self._half(way, s))
        return remote(block, block, self.sib_send.at[w], self.sib_recv.at[w], dp=at.sib)

    def begin(self, w):
        for way in range(2):
            self.ring(w, way, 0).start()
        pltpu.make_async_copy(self.shards[w], self.full[w].at[self.at.m], self.own_sem.at[w]).start()

    def step(self, w, s):
        for way in range(2):
            self.ring(w, way, s).wait_recv()
            if s < self.plan.hops - 1:
                self.ring(w, way, s + 1).start()
            self.cross(w, way, s).start()
            self.give(w, way, s, True).start()

    def follow(self, w, s):
        for way in range(2):
            self.cross(w, way, s).wait_recv()
            self.give(w, way, s, False).start()

    def arrived(self, w):
        n, rows = self.plan.mp, self.shards[w].shape[0]
        settle(self.full[w].at[pl.ds(0, n - 1), pl.ds(0, rows // 2)], self.sib_recv.at[w])
        settle(self.shards[w], self.own_sem.at[w])

    def finish(self, w):
        n, rows = self.plan.mp, self.shards[w].shape[0]
        settle(self.full[w].at[pl.ds(0, n - 1), pl.ds(0, rows // 2)], self.sib_send.at[w])
        settle(self.full[w].at[pl.ds(0, n - 1), pl.ds(0, rows // 4)], self.y_send.at[w])
        for way in range(2):
            settle(self.full[w].at[pl.ds(0, self.plan.hops - 1), pl.ds(0, rows // 4)], self.ring_send.at[w, way])
            settle(piece(self.full[w].at[0], 0, way), self.ring_send.at[w, way])


def gatherer_sems(plan, count):
    dma = pltpu.SemaphoreType.DMA
    return [
        dma((count,)), dma((count, 2)), dma((count, 2, plan.hops)), dma((count,)), dma((count, 2, plan.hops)),
        dma((count,)), dma((count,)),
    ]


class RowsIn:
    def __init__(self, plan, at, src, dst, send, recv, whole_shared):
        self.plan, self.at, self.src, self.dst, self.send, self.recv = plan, at, src, dst, send, recv
        self.whole_shared = whole_shared

    def copies(self):
        plan, at = self.plan, self.at
        mine = pl.ds(pl.multiple_of(at.m * plan.tok, plan.tok), plan.tok)
        for j in range(plan.groups):
            q = at.k * plan.groups + j
            first = j * plan.group_rows
            for e in range(plan.share):
                here = jnp.logical_and(at.k == e, at.m == q)
                holds = True if self.whole_shared else lax.div(at.m * plan.tok, plan.part) == e
                to = lax.rem(at.m * plan.tok + plan.seq - e * plan.part, plan.seq)
                to = pl.ds(pl.multiple_of(to, plan.tok), plan.tok)
                yield here, True, q, e, j, 0, self.src.at[pl.ds(first + plan.own * e, plan.own)], self.dst.at[
                    pl.ds(0, plan.own), mine
                ]
                yield here, holds, q, e, j, 1, self.src.at[first + plan.own * plan.share], self.dst.at[plan.own, to]

    def start(self, only=None):
        for here, wanted, q, e, j, what, src, dst in self.copies():
            if only is not None and only != j:
                continue

            @pl.when(jnp.logical_and(here, wanted))
            def _():
                pltpu.make_async_copy(src, dst, self.recv.at[what]).start()

            @pl.when(jnp.logical_and(jnp.logical_not(here), wanted))
            def _():
                remote(src, dst, self.send.at[j, e, what], self.recv.at[what], dp=self.at.base + e, mp=q).start()

    def arrived(self):
        plan = self.plan
        settle(self.dst.at[pl.ds(0, plan.own)], self.recv.at[0])
        extent = plan.seq if self.whole_shared else plan.part
        settle(self.dst.at[plan.own, pl.ds(0, extent)], self.recv.at[1])

    def finish(self):
        for here, wanted, q, e, j, what, src, dst in self.copies():

            @pl.when(jnp.logical_and(jnp.logical_not(here), wanted))
            def _():
                settle(src, self.send.at[j, e, what])


def run(count, body, table):
    def one(j, carry):
        for when, thunks in sorted(table.items()):

            @pl.when(j == when)
            def _():
                for thunk in thunks:
                    thunk()

        body(j)
        return carry

    lax.fori_loop(0, count, one, 0)


def spread_over(count, thunks, first=0):
    table = {}
    for i, thunk in enumerate(thunks):
        table.setdefault(first + i * (count - first) // len(thunks), []).append(thunk)
    return table


def norm_rows(values, gain_vec, shift_vec):
    unit, _, normed = norm(values, gain_vec, shift_vec)
    return normed


def forward_kernel(
    plan, heads, tok, cot, seg, bq, bu, w0, w1, w2, w3, gain_one, shift_one, out_bias, gain_two, shift_two,
    tok_o, cot3, seg_o, g0, g1, g2, g3, proj_o, attn_o, hid_o, two_o, act_o, der_o,
    tok_v, one_v, wq_v, proj_v, attn_v, wo_v, hid_v, two_v, wu_v, act_v, der_v, seg_v, columns, bq_v, bu_v,
    tok_send, tok_recv, cot_send, cot_recv, seg_send, seg_recv, bias_send, bias_recv, load_sem, save_sem, act_sem, *sems,
):
    n, share, own, part, seq = plan.mp, plan.share, plan.own, plan.part, plan.seq
    held = own * seq + part
    at = Place(plan)
    gat = Gatherer(plan, at, (w0, w1, w2, w3), (g0, g1, g2, g3), sems)
    tokens = RowsIn(plan, at, tok, tok_v, tok_send, tok_recv, True)
    cots = RowsIn(plan, at, cot, cot3, cot_send, cot_recv, False)
    hops = plan.hops
    greet(plan, at, False)

    gat.begin(0)
    tokens.start()
    biases = ((bq, bq_v, 0), (bu, bu_v, 1))
    for src, dst, i in biases:
        pltpu.make_async_copy(src, dst.at[at.m], bias_recv.at[i]).start()
        for s in range(1, n):
            remote(src, dst.at[at.m], bias_send.at[i], bias_recv.at[i], mp=lax.rem(at.m + s, n)).start()
    pltpu.make_async_copy(seg, seg_v.at[at.k], seg_recv.at[0]).start()
    for e in range(1, share):
        remote(seg, seg_v.at[at.k], seg_send.at[0], seg_recv.at[0], dp=at.base + lax.rem(at.k + e, share)).start()
    part_of = functools.partial
    hop = [[part_of(gat.step, w, s) for s in range(hops)] for w in range(4)]
    after = [[part_of(gat.follow, w, s) for s in range(hops)] for w in range(4)]
    gat.begin(1)
    gat.begin(2)
    hop[0][0]()
    for s in range(1, hops):
        hop[0][s]()
        after[0][s - 1]()
        if s == 1:
            hop[2][0]()
        if s == 2:
            hop[1][0]()
            after[2][0]()
            gat.begin(3)
    after[1][0]()
    after[0][hops - 1]()
    tokens.arrived()
    save_tok = pltpu.make_async_copy(tok_v, tok_o, save_sem.at[0])
    save_tok.start()
    gain, shift = gain_one[...], shift_one[...]

    @pl.loop(0, plan.rows * share)
    def _(b):
        r, first = lax.div(b, share), pl.multiple_of(lax.rem(b, share) * part, part)
        values = tok_v[r, pl.ds(first, part)].astype(F32)
        one_v[pl.ds(pl.multiple_of(b * part, part), part)] = norm_rows(values, gain, shift).astype(BF)

    settle(seg_v, seg_recv.at[0])
    labels = []
    for r in range(plan.rows):
        row = at.m * plan.group_rows + (own * at.k + r if r < own else own * share)
        line = seg_v[lax.div(row, plan.rows_dev), pl.ds(lax.rem(row, plan.rows_dev), 1)]
        if r == own:
            turned = line
            for e in range(1, share):
                moved = jnp.concatenate([line[:, e * part :], line[:, : e * part]], axis=1)
                turned = jnp.where(at.k == e, moved, turned)
            line = turned
        seg_o[pl.ds(r, 1)] = line
    label_columns(seg_o, plan.rows, columns)
    for src, dst, i in biases:
        settle(dst, bias_recv.at[i])

    gat.arrived(0)
    load_q = pltpu.make_async_copy(g0, wq_v, load_sem.at[0])
    load_q.start()
    load_q.wait()

    def attend_shard(s):
        projected = jnp.dot(one_v[...], wq_v[s], preferred_element_type=F32) + bq_v[s]
        proj_v[s] = projected.astype(BF)

        def attend(r, first, amount):
            allowed = same_image(seg_o, columns, r, amount)
            keys = pl.ds(pl.multiple_of(r * seq, seq), seq)
            for h in range(heads):
                col = h * 3 * HEAD_DIM
                query = proj_v[s, pl.ds(first, amount), col : col + HEAD_DIM]
                key = proj_v[s, keys, col + HEAD_DIM : col + 2 * HEAD_DIM]
                value = proj_v[s, keys, col + 2 * HEAD_DIM : col + 3 * HEAD_DIM]
                probs = probs_of(key, query, allowed).astype(BF)
                mixed = lax.dot_general(probs, value, DOWN, preferred_element_type=F32)
                attn_v[s, pl.ds(first, amount), h * HEAD_DIM : (h + 1) * HEAD_DIM] = mixed.astype(BF)

        @pl.loop(0, own)
        def _(r):
            attend(r, pl.multiple_of(r * seq, seq), seq)

        attend(own, own * seq, part)

    moves = []
    for s in range(1, hops):
        moves += [hop[2][s], hop[1][s], part_of(cots.start, s - 1)]
        moves += [hop[3][s - 1], after[2][s], after[1][s]]
        moves += [after[3][s - 2]] if s > 1 else []
    for j in range(hops - 1, plan.groups):
        moves.append(part_of(cots.start, j))
    comm = spread_over(n, moves)
    run(n, attend_shard, comm)
    save_proj = pltpu.make_async_copy(proj_v, proj_o, save_sem.at[1])
    save_proj.start()
    save_attn = pltpu.make_async_copy(attn_v, attn_o, save_sem.at[2])
    save_attn.start()

    gat.arrived(1)
    load_o = pltpu.make_async_copy(g1, wo_v, load_sem.at[0])
    load_o.start()
    load_o.wait()
    bias, gain, shift = out_bias[...], gain_two[...], shift_two[...]

    def branch(first, amount, values):
        rows = pl.ds(first, amount)
        total = values.astype(F32) + bias
        for s in range(n):
            total = total + jnp.dot(attn_v[s, rows], wo_v[s], preferred_element_type=F32)
        hid_v[rows] = total
        two_v[rows] = norm_rows(total, gain, shift).astype(BF)

    @pl.loop(0, own)
    def _(r):
        branch(pl.multiple_of(r * seq, seq), seq, tok_v[r])

    branch(own * seq, part, tok_v[own, :part])

    save_hid = pltpu.make_async_copy(hid_v, hid_o, save_sem.at[3])
    save_hid.start()
    save_two = pltpu.make_async_copy(two_v, two_o, save_sem.at[4])
    save_two.start()
    after[3][hops - 2]()
    hop[3][hops - 1]()
    gat.arrived(2)
    load_u = pltpu.make_async_copy(g2, wu_v, load_sem.at[0])
    load_u.start()
    load_u.wait()

    def feed_shard(s):
        pre = jnp.dot(two_v[...], wu_v[s], preferred_element_type=F32) + bu_v[s]
        below = 0.5 * (1.0 + lax.erf(pre * math.sqrt(0.5)))
        density = jnp.exp(-0.5 * pre * pre) * (1.0 / math.sqrt(2.0 * math.pi))
        act_v[s] = (pre * below).astype(BF)
        der_v[s] = below + pre * density

        pltpu.make_async_copy(act_v.at[s], act_o.at[s], act_sem.at[0]).start()
        pltpu.make_async_copy(der_v.at[s], der_o.at[s], act_sem.at[1]).start()

    run(n, feed_shard, {})
    after[3][hops - 1]()
    gat.arrived(3)
    for w in range(4):
        gat.finish(w)
    tokens.finish()
    cots.arrived()
    cots.finish()
    for src, dst, i in biases:
        settle(dst.at[pl.ds(0, n - 1)], bias_send.at[i])
    settle(seg_v.at[pl.ds(0, share - 1)], seg_send.at[0])
    for save in (save_tok, save_proj, save_attn, save_hid, save_two):
        save.wait()
    settle(act_v, act_sem.at[0])
    settle(der_v, act_sem.at[1])


def forward(plan, tokens_in, cotangent, segment_ids, biases, weights, vectors):
    n, share = plan.mp, plan.share
    width = tokens_in.shape[2]
    held, every = plan.own * plan.seq + plan.part, plan.rows * plan.seq
    any_space = pl.BlockSpec(memory_space=pl.ANY)
    in_vmem = pl.BlockSpec(memory_space=pltpu.VMEM)
    dma = pltpu.SemaphoreType.DMA
    rows = ((plan.rows, plan.seq, width), BF)
    heads = weights[1].shape[0] // HEAD_DIM
    local, three, ff = weights[1].shape[0], weights[0].shape[1], weights[2].shape[1]
    full = [((n,) + w.shape, BF) for w in weights]
    proj, attn = ((n, every, three), BF), ((n, held, local), BF)
    hid, two = ((held, width), F32), ((held, width), BF)
    act, der = ((n, held, ff), BF), ((n, held, ff), F32)
    outs = [rows, rows, ((plan.rows, plan.seq), jnp.int32), *full, proj, attn, hid, two, act, der]
    return pl.pallas_call(
        functools.partial(forward_kernel, plan, heads),
        out_shape=[jax.ShapeDtypeStruct(*o) for o in outs],
        in_specs=[any_space] * 9 + [in_vmem] * 5,
        out_specs=[any_space] * 2 + [in_vmem] + [any_space] * 10,
        scratch_shapes=[
            pltpu.VMEM(*rows), pltpu.VMEM((every, width), BF), pltpu.VMEM(*full[0]), pltpu.VMEM(*proj),
            pltpu.VMEM(*attn), pltpu.VMEM(*full[1]), pltpu.VMEM(*hid), pltpu.VMEM(*two), pltpu.VMEM(*full[2]),
            pltpu.VMEM(*act), pltpu.VMEM(*der), pltpu.VMEM((share,) + segment_ids.shape, jnp.int32),
            pltpu.VMEM((plan.rows, plan.seq, 128), F32),
            *[pltpu.VMEM((n,) + b.shape, F32) for b in biases],
            dma((plan.groups, share, 2)), dma((2,)), dma((plan.groups, share, 2)), dma((2,)), dma((1,)), dma((1,)),
            dma((2,)), dma((2,)), dma((1,)), dma((5,)), dma((2,)), *gatherer_sems(plan, 4),
        ],
        compiler_params=pltpu.CompilerParams(
            collective_id=0, has_side_effects=True, vmem_limit_bytes=58 << 20
        ),
        name="forward",
    )(tokens_in, cotangent, segment_ids, *biases, *weights, *vectors)


class Reducer:
    def __init__(self, plan, at, stage, loc, sbl, yrc, slot, wide, fin, grp, out, sems):
        self.plan, self.at, self.stage, self.wide = plan, at, stage, wide
        self.loc, self.sbl, self.yrc, self.slot, self.fin, self.grp, self.out = loc, sbl, yrc, slot, fin, grp, out
        (
            self.sib_send, self.sib_recv, self.y_send, self.y_recv, self.ring_send, self.ring_recv,
            self.grp_send, self.grp_recv, self.fin_send, self.fin_recv, self.out_sem, self.credit,
        ) = sems
        hops = plan.hops
        self.order = [(0, hops)] + [(way, dist) for dist in range(hops - 1, 0, -1) for way in range(2)] + [(0, 0)]

    def target(self, i):
        n, hops = self.plan.mp, self.plan.hops
        dist = hops - lax.div(i + 1, 2)
        up = jnp.where(i == 0, 1, lax.rem(i, 2))
        return self.plan.ring_at(self.at.p + dist * up + (n - dist) * (1 - up))

    def give(self, u, yy, i):
        at, t = self.at, self.target(i)
        src = self.stage[u].at[2 * yy + 1 - at.core]
        return remote(src, self.sbl[u].at[yy, t], self.sib_send.at[u], self.sib_recv.at[u, i, yy], dp=at.sib)

    def begin(self, u, i):
        at, t = self.at, self.target(i)
        rows = self.stage[u].shape[1]
        for yy in range(2):
            self.give(u, yy, i).start()
        size = 32 if rows % 32 == 0 else rows
        for yy in range(2):

            @pl.loop(0, rows // size)
            def _(b):
                inner = pl.ds(pl.multiple_of(b * size, size), size)
                self.loc[u][yy, t, inner] = self.stage[u][2 * yy + at.core, inner]

    def given(self, u):
        settle(self.stage[u].at[pl.ds(0, 2)], self.sib_send.at[u])

    def clear(self, u):
        for way in range(2):
            part = half_of(self.slot[u].at[way, 0], 1 - way)
            part[...] = jnp.zeros(part.shape, BF)
            for yy in range(2):
                part = half_of(self.wide.at[way, 0, yy], 1 - way)
                part[...] = jnp.zeros(part.shape, BF)

    def add(self, u, yy, t, extra, put):
        rows = self.loc[u].shape[2]
        size = 32 if rows % 32 == 0 else rows

        def block(b):
            inner = pl.ds(pl.multiple_of(b * size, size), size)
            total = self.loc[u][yy, t, inner].astype(F32) + self.sbl[u][yy, t, inner].astype(F32)
            for ref in extra:
                total = total + ref[inner].astype(F32)
            put(inner, total)

        pl.loop(0, rows // size)(block)

    def cross(self, u, i):
        at, t = self.at, self.target(i)
        return remote(self.loc[u].at[1 - at.y, t], self.yrc[u].at[t], self.y_send.at[u], self.y_recv.at[u, i], dp=at.other)

    def first(self, u, i):
        at, t = self.at, self.target(i)
        self.give(u, 1 - at.y, i).wait_recv()

        def put(inner, total):
            self.loc[u][1 - at.y, t, inner] = total.astype(BF)

        self.add(u, 1 - at.y, t, (), put)
        self.cross(u, i).start()

    def hop(self, u, way, s, t):
        src = self.loc[u].at[self.at.y, t]
        dst = self.slot[u].at[way, s]
        if s == 0:
            src, dst = half_of(src, way), half_of(dst, way)
        return remote(
            src, dst, self.ring_send.at[u, way], self.ring_recv.at[u, way, s], mp=self.at.neighbour[way]
        )

    def step(self, u, i):
        at, t = self.at, self.target(i)
        way, dist = self.order[i]
        s = self.plan.hops - dist
        self.give(u, at.y, i).wait_recv()
        self.cross(u, i).wait_recv()
        extra = [self.yrc[u].at[t]]
        ways = (0, 1) if dist in (0, self.plan.hops) else (way,)
        if s > 0:
            for v in ways:
                self.hop(u, v, s - 1, t).wait_recv()
                extra.append(self.slot[u].at[v, s - 1])
        rows = self.loc[u].shape[2]
        quads = self.plan.dp // 4

        def put(inner, total):
            if dist:
                self.loc[u][at.y, t, inner] = total.astype(BF)
            elif quads > 1:
                self.grp[u][lax.div(at.d, 4), inner] = total.astype(BF)
            else:
                to = pl.ds(pl.multiple_of(at.quarter * rows + inner.start, inner.size), inner.size)
                self.fin[u][to] = total.astype(BF)

        self.add(u, at.y, t, extra, put)
        if dist:
            for v in ways:
                self.hop(u, v, s, t).start()
        else:
            for other in range(1, quads):
                self.between(u, other).start()

    def wide_hop(self, u, way, s, t):
        src, dst = self.loc[u].at[:, t], self.wide.at[way, s]
        if s == 0:
            half = self.wide.shape[-1] // 2
            src, dst = (ref.at[:, :, pl.ds(way * half, half)] for ref in (src, dst))
        return remote(
            src, dst, self.ring_send.at[u, way], self.ring_recv.at[u, way, s], mp=self.at.neighbour[way]
        )

    def wide_cross(self, u):
        mine, theirs = self.yrc[u].at[pl.ds(2, 2)], self.yrc[u].at[pl.ds(0, 2)]
        return remote(mine, theirs, self.y_send.at[u], self.y_recv.at[u, 0], dp=self.at.other)

    def wide_step(self, u, i):
        at, t = self.at, self.target(i)
        way, dist = self.order[i]
        s = self.plan.hops - dist
        ways = (0, 1) if dist in (0, self.plan.hops) else (way,)
        for yy in range(2):
            self.give(u, yy, i).wait_recv()
        if s > 0:
            for v in ways:
                self.wide_hop(u, v, s - 1, t).wait_recv()
        for yy in range(2):
            extra = [self.wide.at[v, s - 1, yy] for v in ways] if s > 0 else []

            def put(inner, total):
                if dist:
                    self.loc[u][yy, t, inner] = total.astype(BF)
                else:
                    self.yrc[u][2 + yy, inner] = total.astype(BF)

            self.add(u, yy, t, extra, put)
        if dist:
            for v in ways:
                self.wide_hop(u, v, s, t).start()
        else:
            self.wide_cross(u).start()

    def wide_last(self, u):
        at, quads = self.at, self.plan.dp // 4
        rows = self.loc[u].shape[2]
        self.wide_cross(u).wait_recv()
        for yy in range(2):
            to = pl.ds(pl.multiple_of((2 * yy + at.core) * rows, rows), rows)
            total = self.yrc[u][yy].astype(F32) + self.yrc[u][2 + yy].astype(F32)
            if quads > 1:
                self.grp[u][lax.div(at.d, 4), yy] = total.astype(BF)
            else:
                self.fin[u][to] = total.astype(BF)
        if quads > 1:
            for other in range(1, quads):
                self.between(u, other).start()
            settle(self.grp[u].at[pl.ds(0, quads - 1)], self.grp_recv.at[u])
            for yy in range(2):
                to = pl.ds(pl.multiple_of((2 * yy + at.core) * rows, rows), rows)
                total = self.grp[u][0, yy].astype(F32)
                for other in range(1, quads):
                    total = total + self.grp[u][other, yy].astype(F32)
                self.fin[u][to] = total.astype(BF)
        for what in range(2):
            self.wide_out(u, what).start()

    def wide_out(self, u, what):
        block = piece(self.fin[u], 2 * what + self.at.core)
        return remote(block, block, self.fin_send.at[u, what], self.fin_recv.at[u, what], dp=self.at.sib)

    def wide_sent(self, u):
        hops = self.plan.hops
        settle(self.yrc[u].at[pl.ds(0, 2)], self.y_send.at[u])
        for way in range(2):
            settle(self.wide.at[way, pl.ds(0, hops - 1)], self.ring_send.at[u, way])
            half = self.wide.shape[-1] // 2
            settle(self.wide.at[way, 0, :, :, pl.ds(0, half)], self.ring_send.at[u, way])

    def between(self, u, other):
        at = self.at
        to = lax.rem(at.d + 4 * other, self.plan.dp)
        block = self.grp[u].at[lax.div(at.d, 4)]
        return remote(block, block, self.grp_send.at[u], self.grp_recv.at[u], dp=to)

    def share_out(self, u, what):
        at = self.at
        quarter = at.quarter if what != 1 else 2 - 2 * at.y + at.core
        block = piece(self.fin[u], quarter)
        to = at.other if what == 2 else at.sib
        return remote(block, block, self.fin_send.at[u, what], self.fin_recv.at[u, what], dp=to)

    def last(self, u):
        quads = self.plan.dp // 4
        if quads > 1:
            rows = self.loc[u].shape[2]
            settle(self.grp[u].at[pl.ds(0, quads - 1)], self.grp_recv.at[u])
            total = self.grp[u][0].astype(F32)
            for other in range(1, quads):
                total = total + self.grp[u][other].astype(F32)
            self.fin[u][pl.ds(pl.multiple_of(self.at.quarter * rows, rows), rows)] = total.astype(BF)
        self.share_out(u, 2).start()
        self.share_out(u, 0).start()

    def spread(self, u):
        self.share_out(u, 2).wait_recv()
        self.share_out(u, 1).start()

    def write(self, u, dst, wide=False):
        for what in range(2):
            (self.wide_out if wide else self.share_out)(u, what).wait_recv()
        rows = self.loc[u].shape[2]

        @pl.loop(0, 4)
        def _(q):
            at = pl.ds(pl.multiple_of(q * rows, rows), rows)
            slot = lax.rem(q, 2)

            @pl.when(q > 1)
            def _():
                settle(self.out.at[slot], self.out_sem.at[slot])

            self.out[slot] = self.fin[u][at].astype(F32)
            pltpu.make_async_copy(self.out.at[slot], dst.at[at], self.out_sem.at[slot]).start()

        for slot in range(2):
            settle(self.out.at[slot], self.out_sem.at[slot])

    def sent(self, u):
        hops = self.plan.hops
        settle(self.loc[u].at[0], self.y_send.at[u])
        for way in range(2):
            settle(self.slot[u].at[way, pl.ds(0, hops - 1)], self.ring_send.at[u, way])
            settle(half_of(self.slot[u].at[way, 0], way), self.ring_send.at[u, way])

    def release(self, u):
        at = self.at
        self.wide_sent(u)
        for to in ({"dp": at.sib}, {"dp": at.other}, {"mp": at.neighbour[0]}, {"mp": at.neighbour[1]}):
            pl.semaphore_signal(self.credit, inc=1, device_id=to, device_id_type=MESH)

    def claim(self):
        pl.semaphore_wait(self.credit, 4)

    def finish(self, u, wide=False):
        for what in range(2 if wide else 3):
            (self.wide_out if wide else self.share_out)(u, what).wait_send()
        for other in range(1, self.plan.dp // 4):
            self.between(u, other).wait_send()


class RowsOut:
    def __init__(self, plan, at, src, shared, dst, send, recv):
        self.plan, self.at, self.src, self.shared, self.dst, self.send, self.recv = plan, at, src, shared, dst, send, recv
        self.home = at.base + lax.div(at.m, plan.groups)
        self.first = lax.rem(at.m, plan.groups) * plan.group_rows

    def copies(self, what):
        plan, at = self.plan, self.at
        for q in range(plan.mp):
            here = jnp.logical_and(self.home == at.d, at.m == q)
            toks = pl.ds(q * plan.tok, plan.tok)
            if what == 0:
                yield q, here, True, self.src.at[pl.ds(0, plan.own), toks], self.dst.at[
                    pl.ds(self.first + plan.own * at.k, plan.own)
                ]
            else:
                holds = at.k == (q * plan.tok) // plan.part
                yield q, here, holds, self.shared.at[pl.ds((q * plan.tok) % plan.part, plan.tok)], self.dst.at[
                    self.first + plan.own * plan.share
                ]

    def start(self, what):
        for q, here, wanted, src, dst in self.copies(what):

            @pl.when(jnp.logical_and(here, wanted))
            def _():
                pltpu.make_async_copy(src, dst, self.recv.at[0]).start()

            @pl.when(jnp.logical_and(jnp.logical_not(here), wanted))
            def _():
                remote(src, dst, self.send.at[q, what], self.recv.at[0], dp=self.home, mp=q).start()

    def finish(self):
        settle(self.dst, self.recv.at[0])
        for what in range(2):
            for q, here, wanted, src, dst in self.copies(what):

                @pl.when(jnp.logical_and(jnp.logical_not(here), wanted))
                def _():
                    settle(src, self.send.at[q, what])


def backward_kernel(
    plan, heads, g0, g1, g2, g3, tok, cot, seg, proj, attn, hid, two, act, der, gain_one, shift_one, gain_two, down_bias,
    blk, tg, o0, o1, o2, vout, *rest,
):
    n, share, own, part, seq = plan.mp, plan.share, plan.own, plan.part, plan.seq
    hops = plan.hops
    held, every = own * seq + part, plan.rows * seq
    width, ff, three, local = hid.shape[1], act.shape[2], proj.shape[2], attn.shape[2]
    (
        stage_a, stage_b, loc_a, loc_b, sbl_a, sbl_b, yrc_a, yrc_b, slot_a, slot_b, wide_v, fin_a, fin_b, fin_c,
        grp_a, grp_b, grp_c, out_v,
    ) = rest[:18]
    sems, rest = rest[18:30], rest[30:]
    (
        grad_v, low_v, block_v, tgs, tgo, sums, ups, qbs, msg, vrc, vsum,
        load_sem, wgt_sem, blk_send, blk_recv, tg_send, tg_recv, tgs_send, tgs_recv, tgl_sem, v_send, v_recv,
    ) = rest
    at = Place(plan)
    red = Reducer(
        plan, at, (stage_a, stage_b, stage_a), (loc_a, loc_b, loc_a), (sbl_a, sbl_b, sbl_a), (yrc_a, yrc_b, yrc_a),
        (slot_a, slot_b, slot_a), wide_v, (fin_a, fin_b, fin_c), (grp_a, grp_b, grp_c), out_v, sems,
    )
    blocks = RowsOut(plan, at, block_v, block_v.at[own], blk, blk_send, blk_recv)
    greet(plan, at, True)
    part_of = functools.partial
    count = len(red.order)
    first = [[part_of(red.first, u, i) for i in range(count)] for u in range(3)]
    step = [[part_of(red.step, u, i) for i in range(count)] for u in range(3)]
    wide = [part_of(red.wide_step, 0, i) for i in range(count)]
    red.clear(0)
    red.clear(1)
    sums[...] = jnp.zeros(sums.shape, F32)
    blocks_held = own * share + 1

    def stream(loads, i):
        def copies(j, slot):
            t = red.target(j)
            for what, (src, dst) in enumerate(loads):
                yield pltpu.make_async_copy(src.at[t], dst.at[slot], wgt_sem.at[what, slot])

        if isinstance(i, int):
            for copy in copies(i, i % 2):
                copy.start()
            return

        @pl.when(i + 1 < n)
        def _():
            for copy in copies(i + 1, lax.rem(i + 1, 2)):
                copy.start()

        for copy in copies(i, lax.rem(i, 2)):
            copy.wait()

    def feed_forward(wd_v, wu_v, act_v, der_v, low_pre, two_v, cot_v, hid_v, sum_v):
        loads = ((g3, wd_v), (g2, wu_v), (act, act_v), (der, der_v))
        stream(loads, 0)
        small = [pltpu.make_async_copy(two, two_v, load_sem.at[0]), pltpu.make_async_copy(hid, hid_v, load_sem.at[1])]
        for r in range(plan.rows):
            extent = seq if r < own else part
            small.append(
                pltpu.make_async_copy(
                    cot.at[r, pl.ds(0, extent)], cot_v.at[pl.ds(r * seq, extent)], load_sem.at[2 + r]
                )
            )
        for copy in small:
            copy.start()
        for copy in small:
            copy.wait()

        @pl.loop(0, blocks_held)
        def _(b):
            rows = pl.ds(pl.multiple_of(b * part, part), part)
            sum_v[rows] = hid_v[rows] + down_bias[...]
            grad_v[rows] = jnp.zeros((part, width), F32)

        def body(i):
            stream(loads, i)
            slot = lax.rem(i, 2)
            rows = ff // 4

            @pl.when(i > 0)
            def _():
                red.given(0)
                red.given(1)

            for q in range(4):
                lhs = act_v[slot, :, q * rows : (q + 1) * rows]
                stage_a[q] = lax.dot_general(lhs, cot_v[...], DOWN, preferred_element_type=F32).astype(BF)
            red.begin(0, i)

            act_grad = lax.dot_general(cot_v[...], wd_v[slot], ACROSS, preferred_element_type=F32)
            low = (act_grad * der_v[slot]).astype(BF)
            low_pre[...] = low
            ups[red.target(i)] = jnp.sum(low.astype(F32), axis=0, keepdims=True)
            for q in range(4):
                lhs = low_pre[:, q * rows : (q + 1) * rows]
                stage_b[q] = lax.dot_general(lhs, two_v[...], DOWN, preferred_element_type=F32).astype(BF)
            red.begin(1, i)
            grad_v[...] += lax.dot_general(low_pre[...], wu_v[slot], ACROSS, preferred_element_type=F32)
            sum_v[...] += jnp.dot(act_v[slot], wd_v[slot], preferred_element_type=F32)

        table = {}
        for i in range(count - 1):
            table.setdefault(i + 1, []).extend([first[1][i], wide[i]])
        for i in range(count - 2):
            table.setdefault(i + 2, []).append(step[1][i])
        run(n, body, table)
        red.given(0)
        red.given(1)
        first[1][count - 1]()
        wide[count - 1]()
        step[1][count - 2]()

        @pl.loop(0, blocks_held)
        def _(b):
            r, start = lax.div(b, share), pl.multiple_of(lax.rem(b, share) * part, part)
            rows = pl.ds(pl.multiple_of(b * part, part), part)
            block_v[r, pl.ds(start, part)] = sum_v[rows].astype(BF)
            hidden, grad, cot_f = hid_v[rows], grad_v[rows], cot_v[rows].astype(F32)
            unit, scale, _ = norm(hidden, gain_two[...], 0.0)
            hidden_grad = cot_f + norm_back(unit, scale, gain_two[...], grad)
            grad_v[rows] = hidden_grad
            low_v[rows] = hidden_grad.astype(BF)
            for line, value in ((2, hidden_grad), (3, grad * unit), (4, grad), (5, cot_f)):
                sums[pl.ds(line, 1)] += jnp.sum(value, axis=0, keepdims=True)

        blocks.start(0)
        blocks.start(1)

    pl.run_scoped(
        feed_forward,
        pltpu.VMEM((2,) + g3.shape[1:], BF), pltpu.VMEM((2,) + g2.shape[1:], BF), pltpu.VMEM((2, held, ff), BF),
        pltpu.VMEM((2, held, ff), F32), pltpu.VMEM((held, ff), BF), pltpu.VMEM((held, width), BF),
        pltpu.VMEM((held, width), BF), pltpu.VMEM((held, width), F32), pltpu.VMEM((held, width), F32),
    )

    def attention(wq_v, wo_v, proj_v, attn_v, head_v, three_v, tok_v, one_v, back_v, out3, columns):
        loads = ((g0, wq_v), (g1, wo_v), (proj, proj_v), (attn, attn_v))
        stream(loads, 0)
        load = pltpu.make_async_copy(tok, tok_v, load_sem.at[0])
        load.start()
        step[1][count - 1]()
        red.last(1)
        red.wide_last(0)
        red.release(0)
        load.wait()

        @pl.loop(0, plan.rows * share)
        def _(b):
            r, start = lax.div(b, share), pl.multiple_of(lax.rem(b, share) * part, part)
            rows = pl.ds(pl.multiple_of(b * part, part), part)
            values = tok_v[r, pl.ds(start, part)].astype(F32)
            one_v[rows] = norm_rows(values, gain_one[...], shift_one[...]).astype(BF)
            back_v[rows] = jnp.zeros((part, width), F32)

        three_v[...] = jnp.zeros(three_v.shape, BF)
        label_columns(seg, plan.rows, columns)
        red.spread(1)
        red.claim()

        def body(i):
            stream(loads, i)
            slot = lax.rem(i, 2)

            head_v[...] = lax.dot_general(low_v[...], wo_v[slot], ACROSS, preferred_element_type=F32).astype(BF)

            def attend(r, first, amount):
                allowed = same_image(seg, columns, r, amount)
                keys, queries = pl.ds(pl.multiple_of(r * seq, seq), seq), pl.ds(first, amount)
                for h in range(heads):
                    col = h * 3 * HEAD_DIM
                    query = proj_v[slot, queries, col : col + HEAD_DIM]
                    key = proj_v[slot, keys, col + HEAD_DIM : col + 2 * HEAD_DIM]
                    value = proj_v[slot, keys, col + 2 * HEAD_DIM : col + 3 * HEAD_DIM]
                    head_grad = head_v[queries, h * HEAD_DIM : (h + 1) * HEAD_DIM]
                    full = probs_of(key, query, allowed)
                    value_grad = jnp.dot(full.astype(BF), head_grad, preferred_element_type=F32)
                    probs_grad = lax.dot_general(value, head_grad, ACROSS, preferred_element_type=F32)
                    delta = jnp.sum(probs_grad * full, axis=0, keepdims=True)
                    low = (jnp.where(allowed, full * (probs_grad - delta), 0.0) * HEAD_DIM ** (-0.5)).astype(BF)
                    query_grad = lax.dot_general(low, key, DOWN, preferred_element_type=F32)
                    key_grad = jnp.dot(low, query, preferred_element_type=F32)
                    three_v[queries, col : col + HEAD_DIM] = query_grad.astype(BF)
                    three_v[keys, col + HEAD_DIM : col + 2 * HEAD_DIM] = key_grad.astype(BF)
                    three_v[keys, col + 2 * HEAD_DIM : col + 3 * HEAD_DIM] = value_grad.astype(BF)

            @pl.loop(0, own)
            def _(r):
                attend(r, pl.multiple_of(r * seq, seq), seq)

            attend(own, own * seq, part)

            @pl.when(i > 0)
            def _():
                red.given(2)

            wide, narrow = three // 4, local // 4
            weight = lax.dot_general(three_v[...], one_v[...], DOWN, preferred_element_type=F32).astype(BF)
            out_weight = lax.dot_general(attn_v[slot], low_v[...], DOWN, preferred_element_type=F32).astype(BF)
            for q in range(4):
                stage_a[q, :wide] = weight[q * wide : (q + 1) * wide]
                stage_a[q, wide:] = out_weight[q * narrow : (q + 1) * narrow]
            red.begin(2, i)

            back_v[...] += lax.dot_general(three_v[...], wq_v[slot], ACROSS, preferred_element_type=F32)
            qbs[red.target(i)] = jnp.sum(three_v[...].astype(F32), axis=0, keepdims=True)

        table = {2: [part_of(red.write, 0, o0, True)], 3: [part_of(red.write, 1, o1)]}
        for i in range(count - 1):
            table.setdefault(i + 1, []).append(first[2][i])
        for i in range(count - 2):
            table.setdefault(i + 2, []).append(step[2][i])
        run(n, body, table)
        red.given(2)
        first[2][count - 1]()
        step[2][count - 2]()

        @pl.loop(0, plan.rows * share)
        def _(b):
            r, start = lax.div(b, share), pl.multiple_of(lax.rem(b, share) * part, part)
            rows = pl.ds(pl.multiple_of(b * part, part), part)
            unit, scale, _ = norm(tok_v[r, pl.ds(start, part)].astype(F32), gain_one[...], 0.0)
            grad = back_v[rows]
            for line, value in ((0, grad * unit), (1, grad)):
                sums[pl.ds(line, 1)] += jnp.sum(value, axis=0, keepdims=True)
            grad = norm_back(unit, scale, gain_one[...], grad)

            @pl.when(b < blocks_held)
            def _():
                mine = pl.ds(pl.multiple_of(jnp.minimum(b, blocks_held - 1) * part, part), part)
                out3[r, pl.ds(start, part)] = (grad + grad_v[mine]).astype(BF)

            @pl.when(b >= blocks_held)
            def _():
                out3[r, pl.ds(start, part)] = grad.astype(BF)

        tokens = RowsOut(plan, at, out3, tgo, tg, tg_send, tg_recv)
        for e in range(share):
            src = out3.at[own, pl.ds(e * part, part)]
            if e == 0:
                pltpu.make_async_copy(src, tgs.at[0], tgl_sem.at[0]).start()
            else:
                to = at.base + lax.rem(at.k + e, share)
                remote(src, tgs.at[share - e], tgs_send.at[e], tgs_recv.at[share - e], dp=to).start()
        tokens.start(0)

        lines = [-(-size // 128) for size in (ff, three)]
        msg[...] = jnp.zeros(msg.shape, F32)
        for q in range(n):
            msg[q, :8, : width // n] = sums[:, q * (width // n) : (q + 1) * (width // n)]
            line = 8
            for ref, size in ((ups, ff), (qbs, three)):
                for first_col in range(0, size, 128):
                    cols = min(128, size - first_col)
                    msg[q, line : line + 1, :cols] = ref[q, :, first_col : first_col + cols]
                    line += 1
        me = at.d * n + at.m

        def one(i, carry):
            to = lax.rem(me + i, plan.all)
            e, q = lax.div(to, n), lax.rem(to, n)
            remote(msg.at[q], vrc.at[me], v_send.at[0], v_recv.at[0], dp=e, mp=q).start()
            return carry

        lax.fori_loop(1, plan.all, one, 0)
        pltpu.make_async_copy(msg.at[at.m], vrc.at[me], v_recv.at[0]).start()
        for e in range(1, share):
            settle(tgs.at[e], tgs_recv.at[e])
        settle(tgs.at[0], tgl_sem.at[0])
        tgo[...] = sum(tgs[e].astype(F32) for e in range(share)).astype(BF)
        tokens.start(1)
        step[2][count - 1]()
        red.last(2)
        settle(vrc, v_recv.at[0])
        vsum[...] = jnp.sum(vrc[...], axis=0)
        for e in range(1, n):
            remote(vsum, vout.at[at.m], v_send.at[1], v_recv.at[1], mp=lax.rem(at.m + e, n)).start()
        pltpu.make_async_copy(vsum, vout.at[at.m], v_recv.at[1]).start()
        red.spread(2)
        red.write(2, o2)
        for u in range(3):
            red.finish(u, u == 0)
        red.sent(1)
        red.sent(2)
        for e in range(1, share):
            settle(tgs.at[0], tgs_send.at[e])
        blocks.finish()
        tokens.finish()
        settle(vout, v_recv.at[1])
        settle(vrc.at[pl.ds(0, plan.all - 1)], v_send.at[0])
        settle(vout.at[pl.ds(0, n - 1)], v_send.at[1])

    pl.run_scoped(
        attention,
        pltpu.VMEM((2,) + g0.shape[1:], BF), pltpu.VMEM((2,) + g1.shape[1:], BF), pltpu.VMEM((2, every, three), BF),
        pltpu.VMEM((2, held, local), BF), pltpu.VMEM((held, local), BF), pltpu.VMEM((every, three), BF),
        pltpu.VMEM((plan.rows, seq, width), BF), pltpu.VMEM((every, width), BF), pltpu.VMEM((every, width), F32),
        pltpu.VMEM((plan.rows, seq, width), BF), pltpu.VMEM((plan.rows, seq, 128), F32),
    )


def backward(plan, weights, tok3, cot3, seg, proj, attn, hid, two, act, der, vectors):
    n, share = plan.mp, plan.share
    held, width = hid.shape
    ff, three, local = act.shape[2], proj.shape[2], attn.shape[2]
    heads = local // HEAD_DIM
    quads, quarter = plan.dp // 4, ff // 4
    if local + three != ff:
        raise ValueError("unsupported sizes")
    any_space = pl.BlockSpec(memory_space=pl.ANY)
    in_vmem = pl.BlockSpec(memory_space=pltpu.VMEM)
    dma = pltpu.SemaphoreType.DMA
    rows = jax.ShapeDtypeStruct((plan.rows_dev, plan.tok, width), BF)
    shard = jax.ShapeDtypeStruct((ff, width), F32)
    size = 8 + -(-ff // 128) + -(-three // 128)
    size = -(-size // 8) * 8
    vec = (size, 128)
    return pl.pallas_call(
        functools.partial(backward_kernel, plan, heads),
        out_shape=[rows, rows, shard, shard, shard, jax.ShapeDtypeStruct((n,) + vec, F32)],
        in_specs=[any_space] * 6 + [in_vmem] + [any_space] * 6 + [in_vmem] * 4,
        out_specs=[any_space] * 6,
        scratch_shapes=[
            *[pltpu.VMEM((4, quarter, width), BF)] * 2,
            *[pltpu.VMEM((2, n, quarter, width), BF)] * 4,
            *[pltpu.VMEM((n, quarter, width), BF)] * 2,
            *[pltpu.VMEM((2, plan.hops, quarter, width), BF)] * 2,
            pltpu.VMEM((2, plan.hops, 2, quarter, width), BF),
            *[pltpu.VMEM((ff, width), BF)] * 3,
            pltpu.VMEM((quads, 2) + ((quarter, width) if quads > 1 else (8, 128)), BF),
            *[pltpu.VMEM((quads,) + ((quarter, width) if quads > 1 else (8, 128)), BF)] * 2,
            pltpu.VMEM((2, quarter, width), F32),
            dma((3,)), dma((3, n, 2)), dma((3,)), dma((3, n)), dma((3, 2)), dma((3, 2, plan.hops)), dma((3,)), dma((3,)),
            dma((3, 3)), dma((3, 3)), dma((2,)), pltpu.SemaphoreType.REGULAR,
            pltpu.VMEM((held, width), F32), pltpu.VMEM((held, width), BF), pltpu.VMEM((plan.rows, plan.seq, width), BF),
            pltpu.VMEM((share, plan.part, width), BF), pltpu.VMEM((plan.part, width), BF), pltpu.VMEM((8, width), F32),
            pltpu.VMEM((n, 1, ff), F32), pltpu.VMEM((n, 1, three), F32), pltpu.VMEM((n,) + vec, F32),
            pltpu.VMEM((plan.all,) + vec, F32), pltpu.VMEM(vec, F32),
            dma((2 + plan.rows,)), dma((4, 2)), dma((n, 2)), dma((1,)), dma((n, 2)), dma((1,)), dma((share,)),
            dma((share,)), dma((1,)), dma((2,)), dma((2,)),
        ],
        compiler_params=pltpu.CompilerParams(
            collective_id=1, has_side_effects=True, vmem_limit_bytes=61 << 20
        ),
        name="backward",
    )(*weights, tok3, cot3, seg, proj, attn, hid, two, act, der, *vectors)


def probs_of(key, query, allowed):
    raw = lax.dot_general(key, query, ACROSS, preferred_element_type=F32)
    scores = jnp.where(allowed, raw * HEAD_DIM ** (-0.5), MASKED)
    raised = jnp.exp(scores - jnp.max(scores, axis=0, keepdims=True))
    return raised * (1.0 / jnp.sum(raised, axis=0, keepdims=True))


def label_columns(labels, rows, columns):
    for r in range(rows):
        line = labels[pl.ds(r, 1)].astype(F32)
        columns[r] = jnp.transpose(jnp.broadcast_to(line, (128, line.shape[1])))


def same_image(labels, columns, r, amount):
    line = labels[pl.ds(r, 1)].astype(F32)[:, :amount]
    down = columns[r]
    if amount < 128:
        return down[:, :amount] == line
    return jnp.concatenate([down] * (amount // 128), axis=1) == line


def norm(values, gain_vec, shift_vec):
    centred = values - jnp.mean(values, axis=-1, keepdims=True)
    scale = lax.rsqrt(jnp.mean(centred * centred, axis=-1, keepdims=True) + EPS)
    unit = centred * scale
    return unit, scale, unit * gain_vec + shift_vec


def norm_back(unit, scale, gain_vec, grad):
    pulled = grad * gain_vec
    inner = jnp.mean(pulled * unit, axis=-1, keepdims=True)
    return scale * (pulled - jnp.mean(pulled, axis=-1, keepdims=True) - unit * inner)


def per_device(
    plan, tokens_in, segment_ids, attn_gain, attn_shift, qkv_weight, qkv_bias, out_weight, out_bias, mlp_gain, mlp_shift,
    up_weight, up_bias, down_weight, down_bias, cotangent,
):
    n, width = plan.mp, tokens_in.shape[2]
    ff_local = up_weight.shape[1]
    heads_local = qkv_bias.shape[1] // HEAD_DIM
    parts = qkv_bias.reshape(2, heads_local, HEAD_DIM)
    bias_three = jnp.stack([parts[0], jnp.zeros_like(parts[0]), parts[1]], axis=1).reshape(1, -1)
    vectors = [v.reshape(1, width) for v in (attn_gain, attn_shift, out_bias, mlp_gain, mlp_shift)]
    tok3, cot3, seg, wq, wo, wu, wd, proj, attn, hidden, normed_two, act_low, gelu_slope = forward(
        plan, tokens_in, cotangent, segment_ids, (bias_three, up_bias.reshape(1, ff_local)),
        (qkv_weight, out_weight, up_weight, down_weight), vectors,
    )
    block_out, tokens_low, down_grad, up_grad, rest_grad, sums = backward(
        plan, (wq, wo, wu, wd), tok3, cot3, seg, proj, attn, hidden, normed_two, act_low, gelu_slope,
        [v.reshape(1, width) for v in (attn_gain, attn_shift, mlp_gain, down_bias)],
    )
    local, three = out_weight.shape[0], qkv_weight.shape[1]
    rest_grad = rest_grad.reshape(4, (local + three) // 4, width)
    qkv_grad = rest_grad[:, : three // 4].reshape(three, width).T
    out_grad = rest_grad[:, three // 4 :].reshape(local, width)
    six = jnp.swapaxes(sums[:, :6, : width // n], 0, 1).reshape(6, width)
    mine = lax.dynamic_index_in_dim(sums, lax.axis_index("mp"), 0, keepdims=False)
    lines = [-(-size // 128) for size in (ff_local, three)]
    up_bias_grad = mine[8 : 8 + lines[0]].reshape(-1)[:ff_local]
    bias_sums = mine[8 + lines[0] : 8 + sum(lines)].reshape(-1)[:three].reshape(heads_local, 3, HEAD_DIM)
    qkv_bias_grad = jnp.stack([bias_sums[:, 0], bias_sums[:, 2]]).reshape(2, local)
    return (
        block_out, tokens_low.astype(F32), six[0], six[1], qkv_grad, qkv_bias_grad, out_grad, six[2], six[3], six[4],
        up_grad.T, up_bias_grad, down_grad, six[5],
    )


def solution(mesh):
    dp, mp = mesh.shape["dp"], mesh.shape["mp"]
    rows_spec = P("dp", "mp", None)
    in_specs = (
        rows_spec, P("dp", None), P(), P(), P(None, "mp"), P(None, "mp"), P("mp", None), P(), P(), P(),
        P(None, "mp"), P("mp"), P("mp", None), P(), rows_spec,
    )
    out_specs = (
        rows_spec, rows_spec, P(), P(), P(None, "mp"), P(None, "mp"), P("mp", None), P(), P(), P(),
        P(None, "mp"), P("mp"), P("mp", None), P(),
    )

    def run(tokens_in, segment_ids, *rest):
        rows_all, seq_len, _ = tokens_in.shape
        plan = Plan(dp, mp, rows_all // dp, seq_len // mp, seq_len)
        return jax.shard_map(
            functools.partial(per_device, plan), mesh=mesh, in_specs=in_specs, out_specs=out_specs, check_vma=False
        )(tokens_in, segment_ids, *rest)

    return run
```

```python
import functools
import itertools
import math

import jax
import jax.numpy as jnp
from jax import lax
from jax.experimental import pallas as pl
from jax.experimental.pallas import tpu as pltpu
from jax.sharding import PartitionSpec as P

HEAD_DIM = 64
EPS = 1e-06
MASKED = -1000000000.0
MESH = pl.DeviceIdType.MESH
BF = jnp.bfloat16
F32 = jnp.float32
ACROSS = (((1,), (1,)), ((), ()))
DOWN = (((0,), (0,)), ((), ()))


WIDE_FIRST, WIDE_PACE = 1, 4
BLOCKS_MID, BLOCKS_OVER = 8, 4


class Plan:
    def __init__(self, dp, mp, rows_dev, tok_local, seq_len):
        self.dp, self.mp, self.rows_dev, self.tok, self.seq = dp, mp, rows_dev, tok_local, seq_len
        self.share = mp // math.gcd(rows_dev, mp)
        self.group_rows = rows_dev * self.share // mp
        self.own = self.group_rows // self.share
        if self.share % 2 or dp % self.share or dp % 4 or self.group_rows != self.own * self.share + 1:
            raise ValueError("unsupported sizes")
        self.groups = mp // self.share
        self.part = seq_len // self.share
        self.rows = self.own + 1
        self.hops = mp // 2
        self.all = dp * mp

    def ring_at(self, p):
        p = lax.rem(p, self.mp)
        back = lax.div(p, self.mp // 2)
        return 2 * p * (1 - back) + (2 * self.mp - 1 - 2 * p) * back


class Place:
    def __init__(self, plan):
        d, m = lax.axis_index("dp"), lax.axis_index("mp")
        odd = lax.rem(m, 2)
        self.d, self.m = d, m
        self.p = lax.div(m, 2) * (1 - odd) + (plan.mp - 1 - lax.div(m, 2)) * odd
        self.core = lax.rem(d, 2)
        self.sib = d + 1 - 2 * self.core
        self.y = lax.rem(lax.div(d, 2), 2)
        self.other = d + 2 - 4 * self.y
        self.k = lax.rem(d, plan.share)
        self.base = d - self.k
        self.quarter = 2 * self.y + self.core
        self.neighbour = (plan.ring_at(self.p + 1), plan.ring_at(self.p + plan.mp - 1))

    def away(self, plan, way, s):
        return plan.ring_at(self.p + plan.mp - s if way == 0 else self.p + s)


def greet(plan, at, everyone):
    barrier = pltpu.get_barrier_semaphore()
    span = plan.dp if everyone else max(plan.share, 4)
    base = lax.div(at.d, span) * span

    def one(i, carry):
        e, q = base + lax.div(i, plan.mp), lax.rem(i, plan.mp)

        @pl.when(jnp.logical_or(e != at.d, q != at.m))
        def _():
            pl.semaphore_signal(barrier, inc=1, device_id={"dp": e, "mp": q}, device_id_type=MESH)

        return carry

    lax.fori_loop(0, span * plan.mp, one, 0)
    pl.semaphore_wait(barrier, span * plan.mp - 1)


def remote(src, dst, send, recv, **to):
    return pltpu.make_async_remote_copy(src, dst, send, recv, device_id=to, device_id_type=MESH)


def settle(ref, sem):
    pltpu.make_async_copy(ref, ref, sem).wait()


def piece(ref, quarter, half=None):
    rows, cols = ref.shape[0] // 4, ref.shape[1]
    first = quarter * rows
    if half is None:
        return ref.at[pl.ds(pl.multiple_of(first, rows), rows)]
    if cols % 256 == 0:
        return ref.at[pl.ds(pl.multiple_of(first, rows), rows), pl.ds(half * (cols // 2), cols // 2)]
    return ref.at[pl.ds(pl.multiple_of(first + half * (rows // 2), rows // 2), rows // 2)]


def half_of(ref, half):
    rows, cols = ref.shape
    if cols % 256 == 0:
        return ref.at[:, pl.ds(half * (cols // 2), cols // 2)]
    return ref.at[pl.ds(half * (rows // 2), rows // 2)]


class Gatherer:
    def __init__(self, plan, at, shards, full, sems):
        self.plan, self.at, self.shards, self.full = plan, at, shards, full
        self.own_sem, self.ring_send, self.ring_recv, self.y_send, self.y_recv, self.sib_send, self.sib_recv = sems

    def _half(self, way, s):
        return way if s == self.plan.hops - 1 else None

    def ring(self, w, way, s):
        at, origin = self.at, self.at.away(self.plan, way, s)
        half = self._half(way, s)
        dst = piece(self.full[w].at[origin], at.quarter, half)
        src = piece(self.shards[w], at.quarter, half) if s == 0 else dst
        return remote(src, dst, self.ring_send.at[w, way], self.ring_recv.at[w, way, s], mp=at.neighbour[way])

    def cross(self, w, way, s):
        at, origin = self.at, self.at.away(self.plan, way, s + 1)
        block = piece(self.full[w].at[origin], at.quarter, self._half(way, s))
        return remote(block, block, self.y_send.at[w], self.y_recv.at[w, way, s], dp=at.other)

    def give(self, w, way, s, mine):
        at, origin = self.at, self.at.away(self.plan, way, s + 1)
        quarter = at.quarter if mine else 2 - 2 * at.y + at.core
        block = piece(self.full[w].at[origin], quarter, self._half(way, s))
        return remote(block, block, self.sib_send.at[w], self.sib_recv.at[w], dp=at.sib)

    def begin(self, w):
        for way in range(2):
            self.ring(w, way, 0).start()
        pltpu.make_async_copy(self.shards[w], self.full[w].at[self.at.m], self.own_sem.at[w]).start()

    def step(self, w, s):
        for way in range(2):
            self.ring(w, way, s).wait_recv()
            if s < self.plan.hops - 1:
                self.ring(w, way, s + 1).start()
            self.cross(w, way, s).start()
            self.give(w, way, s, True).start()

    def follow(self, w, s):
        for way in range(2):
            self.cross(w, way, s).wait_recv()
            self.give(w, way, s, False).start()

    def arrived(self, w):
        n, rows = self.plan.mp, self.shards[w].shape[0]
        settle(self.full[w].at[pl.ds(0, n - 1), pl.ds(0, rows // 2)], self.sib_recv.at[w])
        settle(self.shards[w], self.own_sem.at[w])

    def finish(self, w):
        n, rows = self.plan.mp, self.shards[w].shape[0]
        settle(self.full[w].at[pl.ds(0, n - 1), pl.ds(0, rows // 2)], self.sib_send.at[w])
        settle(self.full[w].at[pl.ds(0, n - 1), pl.ds(0, rows // 4)], self.y_send.at[w])
        for way in range(2):
            settle(self.full[w].at[pl.ds(0, self.plan.hops - 1), pl.ds(0, rows // 4)], self.ring_send.at[w, way])
            settle(piece(self.full[w].at[0], 0, way), self.ring_send.at[w, way])


def gatherer_sems(plan, count):
    dma = pltpu.SemaphoreType.DMA
    return [
        dma((count,)), dma((count, 2)), dma((count, 2, plan.hops)), dma((count,)), dma((count, 2, plan.hops)),
        dma((count,)), dma((count,)),
    ]


class RowsIn:
    def __init__(self, plan, at, src, dst, send, recv, whole_shared):
        self.plan, self.at, self.src, self.dst, self.send, self.recv = plan, at, src, dst, send, recv
        self.whole_shared = whole_shared

    def copies(self):
        plan, at = self.plan, self.at
        mine = pl.ds(pl.multiple_of(at.m * plan.tok, plan.tok), plan.tok)
        for j in range(plan.groups):
            q = at.k * plan.groups + j
            first = j * plan.group_rows
            for e in range(plan.share):
                here = jnp.logical_and(at.k == e, at.m == q)
                holds = True if self.whole_shared else lax.div(at.m * plan.tok, plan.part) == e
                to = lax.rem(at.m * plan.tok + plan.seq - e * plan.part, plan.seq)
                to = pl.ds(pl.multiple_of(to, plan.tok), plan.tok)
                yield here, True, q, e, j, 0, self.src.at[pl.ds(first + plan.own * e, plan.own)], self.dst.at[
                    pl.ds(0, plan.own), mine
                ]
                yield here, holds, q, e, j, 1, self.src.at[first + plan.own * plan.share], self.dst.at[plan.own, to]

    def start(self, only=None):
        for here, wanted, q, e, j, what, src, dst in self.copies():
            if only is not None and only != j:
                continue

            @pl.when(jnp.logical_and(here, wanted))
            def _():
                pltpu.make_async_copy(src, dst, self.recv.at[what]).start()

            @pl.when(jnp.logical_and(jnp.logical_not(here), wanted))
            def _():
                remote(src, dst, self.send.at[j, e, what], self.recv.at[what], dp=self.at.base + e, mp=q).start()

    def arrived(self):
        plan = self.plan
        settle(self.dst.at[pl.ds(0, plan.own)], self.recv.at[0])
        extent = plan.seq if self.whole_shared else plan.part
        settle(self.dst.at[plan.own, pl.ds(0, extent)], self.recv.at[1])

    def finish(self):
        for here, wanted, q, e, j, what, src, dst in self.copies():

            @pl.when(jnp.logical_and(jnp.logical_not(here), wanted))
            def _():
                settle(src, self.send.at[j, e, what])


def run(count, body, *tables):
    def one(j, carry):
        def take(k):
            for when, thunks in sorted(tables[k].items()):

                @pl.when(j == when)
                def _():
                    for thunk in thunks:
                        thunk()

        body(j, take)
        return carry

    lax.fori_loop(0, count, one, 0)


def spread_over(count, thunks, first=0):
    table = {}
    for i, thunk in enumerate(thunks):
        table.setdefault(first + i * (count - first) // len(thunks), []).append(thunk)
    return table


def norm_rows(values, gain_vec, shift_vec):
    unit, _, normed = norm(values, gain_vec, shift_vec)
    return normed


def forward_kernel(
    plan, heads, tok, cot, seg, bq, bu, w0, w1, w2, w3, gain_one, shift_one, out_bias, gain_two, shift_two,
    tok_o, cot3, seg_o, g0, g1, g2, g3, proj_o, attn_o, hid_o, two_o, act_o, der_o,
    tok_v, one_v, wq_v, proj_v, attn_v, wo_v, hid_v, two_v, wu_v, act_v, der_v, seg_v, columns, bq_v, bu_v,
    tok_send, tok_recv, cot_send, cot_recv, seg_send, seg_recv, bias_send, bias_recv, load_sem, save_sem, act_sem, *sems,
):
    n, share, own, part, seq = plan.mp, plan.share, plan.own, plan.part, plan.seq
    held = own * seq + part
    at = Place(plan)
    gat = Gatherer(plan, at, (w0, w1, w2, w3), (g0, g1, g2, g3), sems)
    tokens = RowsIn(plan, at, tok, tok_v, tok_send, tok_recv, True)
    cots = RowsIn(plan, at, cot, cot3, cot_send, cot_recv, False)
    hops = plan.hops
    greet(plan, at, False)

    gat.begin(0)
    gat.begin(2)
    tokens.start(0)
    biases = ((bq, bq_v, 0), (bu, bu_v, 1))
    for src, dst, i in biases:
        pltpu.make_async_copy(src, dst.at[at.m], bias_recv.at[i]).start()
        for s in range(1, n):
            remote(src, dst.at[at.m], bias_send.at[i], bias_recv.at[i], mp=lax.rem(at.m + s, n)).start()
    pltpu.make_async_copy(seg, seg_v.at[at.k], seg_recv.at[0]).start()
    for e in range(1, share):
        remote(seg, seg_v.at[at.k], seg_send.at[0], seg_recv.at[0], dp=at.base + lax.rem(at.k + e, share)).start()
    part_of = functools.partial
    hop = [[part_of(gat.step, w, s) for s in range(hops)] for w in range(4)]
    after = [[part_of(gat.follow, w, s) for s in range(hops)] for w in range(4)]
    begin = [part_of(gat.begin, w) for w in range(4)]
    token = [part_of(tokens.start, j) for j in range(plan.groups)]
    between = {0: [begin[3], hop[2][0]] + token[1:2], 1: token[2:3] + [hop[2][1], after[2][0]], 2: token[3:] + [hop[3][0]]}
    between[hops - 1] = between.get(hops - 1, []) + [hop[2][2], after[2][1], begin[1]]
    for s in range(hops):
        hop[0][s]()
        if s:
            after[0][s - 1]()
        for thunk in between.get(s, []):
            thunk()
    after[0][hops - 1]()
    tokens.arrived()
    save_tok = pltpu.make_async_copy(tok_v, tok_o, save_sem.at[0])
    save_tok.start()
    gain, shift = gain_one[...], shift_one[...]

    @pl.loop(0, plan.rows * share)
    def _(b):
        r, first = lax.div(b, share), pl.multiple_of(lax.rem(b, share) * part, part)
        values = tok_v[r, pl.ds(first, part)].astype(F32)
        one_v[pl.ds(pl.multiple_of(b * part, part), part)] = norm_rows(values, gain, shift).astype(BF)

    settle(seg_v, seg_recv.at[0])
    labels = []
    for r in range(plan.rows):
        row = at.m * plan.group_rows + (own * at.k + r if r < own else own * share)
        line = seg_v[lax.div(row, plan.rows_dev), pl.ds(lax.rem(row, plan.rows_dev), 1)]
        if r == own:
            turned = line
            for e in range(1, share):
                moved = jnp.concatenate([line[:, e * part :], line[:, : e * part]], axis=1)
                turned = jnp.where(at.k == e, moved, turned)
            line = turned
        seg_o[pl.ds(r, 1)] = line
    label_columns(seg_o, plan.rows, columns)
    for src, dst, i in biases:
        settle(dst, bias_recv.at[i])

    gat.arrived(0)
    load_q = pltpu.make_async_copy(g0, wq_v, load_sem.at[0])
    load_q.start()
    load_q.wait()

    def attend_shard(s, take):
        take(0)
        projected = jnp.dot(one_v[...], wq_v[s], preferred_element_type=F32) + bq_v[s]
        proj_v[s] = projected.astype(BF)

        def attend(r, first, amount):
            allowed = same_image(seg_o, columns, r, amount)
            keys = pl.ds(pl.multiple_of(r * seq, seq), seq)
            for h in range(heads):
                col = h * 3 * HEAD_DIM
                query = proj_v[s, pl.ds(first, amount), col : col + HEAD_DIM]
                key = proj_v[s, keys, col + HEAD_DIM : col + 2 * HEAD_DIM]
                value = proj_v[s, keys, col + 2 * HEAD_DIM : col + 3 * HEAD_DIM]
                probs = probs_of(key, query, allowed).astype(BF)
                mixed = lax.dot_general(probs, value, DOWN, preferred_element_type=F32)
                attn_v[s, pl.ds(first, amount), h * HEAD_DIM : (h + 1) * HEAD_DIM] = mixed.astype(BF)

        @pl.loop(0, own)
        def _(r):
            attend(r, pl.multiple_of(r * seq, seq), seq)

        take(1)
        attend(own, own * seq, part)

    rest = []
    for w, done in ((2, 3), (3, 1), (1, 0)):
        steps = [hop[w][s : s + 1] + (after[w][s - 1 : s] if s else []) for s in range(done, hops)]
        rest.append(steps + [after[w][hops - 1 :]])
    rest.append([[part_of(cots.start, j)] for j in range(plan.groups)])
    moves = []
    for at_once in itertools.zip_longest(*rest):
        moves += [thunks for thunks in at_once if thunks]
    tables = ({}, {})
    for j, thunks in spread_over(2 * n, moves).items():
        tables[j % 2][j // 2] = [thunk for some in thunks for thunk in some]
    run(n, attend_shard, *tables)
    save_proj = pltpu.make_async_copy(proj_v, proj_o, save_sem.at[1])
    save_proj.start()
    save_attn = pltpu.make_async_copy(attn_v, attn_o, save_sem.at[2])
    save_attn.start()

    gat.arrived(1)
    load_o = pltpu.make_async_copy(g1, wo_v, load_sem.at[0])
    load_o.start()
    load_o.wait()
    bias, gain, shift = out_bias[...], gain_two[...], shift_two[...]

    def branch(first, amount, values):
        rows = pl.ds(first, amount)
        total = values.astype(F32) + bias
        for s in range(n):
            total = total + jnp.dot(attn_v[s, rows], wo_v[s], preferred_element_type=F32)
        hid_v[rows] = total
        two_v[rows] = norm_rows(total, gain, shift).astype(BF)

    @pl.loop(0, own)
    def _(r):
        branch(pl.multiple_of(r * seq, seq), seq, tok_v[r])

    branch(own * seq, part, tok_v[own, :part])

    save_hid = pltpu.make_async_copy(hid_v, hid_o, save_sem.at[3])
    save_hid.start()
    save_two = pltpu.make_async_copy(two_v, two_o, save_sem.at[4])
    save_two.start()
    gat.arrived(2)
    load_u = pltpu.make_async_copy(g2, wu_v, load_sem.at[0])
    load_u.start()
    load_u.wait()

    def feed_shard(s, take):
        pre = jnp.dot(two_v[...], wu_v[s], preferred_element_type=F32) + bu_v[s]
        below = 0.5 * (1.0 + lax.erf(pre * math.sqrt(0.5)))
        density = jnp.exp(-0.5 * pre * pre) * (1.0 / math.sqrt(2.0 * math.pi))
        act_v[s] = (pre * below).astype(BF)
        der_v[s] = below + pre * density

        pltpu.make_async_copy(act_v.at[s], act_o.at[s], act_sem.at[0]).start()
        pltpu.make_async_copy(der_v.at[s], der_o.at[s], act_sem.at[1]).start()

    run(n, feed_shard)
    gat.arrived(3)
    for w in range(4):
        gat.finish(w)
    tokens.finish()
    cots.arrived()
    cots.finish()
    for src, dst, i in biases:
        settle(dst.at[pl.ds(0, n - 1)], bias_send.at[i])
    settle(seg_v.at[pl.ds(0, share - 1)], seg_send.at[0])
    for save in (save_tok, save_proj, save_attn, save_hid, save_two):
        save.wait()
    settle(act_v, act_sem.at[0])
    settle(der_v, act_sem.at[1])


def forward(plan, tokens_in, cotangent, segment_ids, biases, weights, vectors):
    n, share = plan.mp, plan.share
    width = tokens_in.shape[2]
    held, every = plan.own * plan.seq + plan.part, plan.rows * plan.seq
    any_space = pl.BlockSpec(memory_space=pl.ANY)
    in_vmem = pl.BlockSpec(memory_space=pltpu.VMEM)
    dma = pltpu.SemaphoreType.DMA
    rows = ((plan.rows, plan.seq, width), BF)
    heads = weights[1].shape[0] // HEAD_DIM
    local, three, ff = weights[1].shape[0], weights[0].shape[1], weights[2].shape[1]
    full = [((n,) + w.shape, BF) for w in weights]
    proj, attn = ((n, every, three), BF), ((n, held, local), BF)
    hid, two = ((held, width), F32), ((held, width), BF)
    act, der = ((n, held, ff), BF), ((n, held, ff), F32)
    outs = [rows, rows, ((plan.rows, plan.seq), jnp.int32), *full, proj, attn, hid, two, act, der]
    return pl.pallas_call(
        functools.partial(forward_kernel, plan, heads),
        out_shape=[jax.ShapeDtypeStruct(*o) for o in outs],
        in_specs=[any_space] * 9 + [in_vmem] * 5,
        out_specs=[any_space] * 2 + [in_vmem] + [any_space] * 10,
        scratch_shapes=[
            pltpu.VMEM(*rows), pltpu.VMEM((every, width), BF), pltpu.VMEM(*full[0]), pltpu.VMEM(*proj),
            pltpu.VMEM(*attn), pltpu.VMEM(*full[1]), pltpu.VMEM(*hid), pltpu.VMEM(*two), pltpu.VMEM(*full[2]),
            pltpu.VMEM(*act), pltpu.VMEM(*der), pltpu.VMEM((share,) + segment_ids.shape, jnp.int32),
            pltpu.VMEM((plan.rows, plan.seq, 128), F32),
            *[pltpu.VMEM((n,) + b.shape, F32) for b in biases],
            dma((plan.groups, share, 2)), dma((2,)), dma((plan.groups, share, 2)), dma((2,)), dma((1,)), dma((1,)),
            dma((2,)), dma((2,)), dma((1,)), dma((5,)), dma((2,)), *gatherer_sems(plan, 4),
        ],
        compiler_params=pltpu.CompilerParams(
            collective_id=0, has_side_effects=True, vmem_limit_bytes=58 << 20
        ),
        name="forward",
    )(tokens_in, cotangent, segment_ids, *biases, *weights, *vectors)


class Reducer:
    def __init__(self, plan, at, stage, loc, sbl, yrc, slot, wide, fin, grp, out, sems):
        self.plan, self.at, self.stage, self.wide = plan, at, stage, wide
        self.loc, self.sbl, self.yrc, self.slot, self.fin, self.grp, self.out = loc, sbl, yrc, slot, fin, grp, out
        (
            self.sib_send, self.sib_recv, self.y_send, self.y_recv, self.ring_send, self.ring_recv,
            self.grp_send, self.grp_recv, self.fin_send, self.fin_recv, self.out_sem, self.credit,
        ) = sems
        hops = plan.hops
        self.order = [(0, hops)] + [(way, dist) for dist in range(hops - 1, 0, -1) for way in range(2)] + [(0, 0)]

    def target(self, i):
        n, hops = self.plan.mp, self.plan.hops
        dist = hops - lax.div(i + 1, 2)
        up = jnp.where(i == 0, 1, lax.rem(i, 2))
        return self.plan.ring_at(self.at.p + dist * up + (n - dist) * (1 - up))

    def give(self, u, yy, i):
        at, t = self.at, self.target(i)
        src = self.stage[u].at[2 * yy + 1 - at.core]
        return remote(src, self.sbl[u].at[yy, t], self.sib_send.at[u], self.sib_recv.at[u, i, yy], dp=at.sib)

    def begin(self, u, i):
        at, t = self.at, self.target(i)
        rows = self.stage[u].shape[1]
        for yy in range(2):
            self.give(u, yy, i).start()
        size = 32 if rows % 32 == 0 else rows
        for yy in range(2):

            @pl.loop(0, rows // size)
            def _(b):
                inner = pl.ds(pl.multiple_of(b * size, size), size)
                self.loc[u][yy, t, inner] = self.stage[u][2 * yy + at.core, inner]

    def given(self, u):
        settle(self.stage[u].at[pl.ds(0, 2)], self.sib_send.at[u])

    def clear(self, u):
        for way in range(2):
            part = half_of(self.slot[u].at[way, 0], 1 - way)
            part[...] = jnp.zeros(part.shape, BF)

    def wide_clear(self):
        for way in range(2):
            for yy in range(2):
                part = half_of(self.wide.at[way, 0, yy], 1 - way)
                part[...] = jnp.zeros(part.shape, BF)

    def add(self, u, yy, t, extra, put):
        rows = self.loc[u].shape[2]
        size = 32 if rows % 32 == 0 else rows

        def block(b):
            inner = pl.ds(pl.multiple_of(b * size, size), size)
            total = self.loc[u][yy, t, inner].astype(F32) + self.sbl[u][yy, t, inner].astype(F32)
            for ref in extra:
                total = total + ref[inner].astype(F32)
            put(inner, total)

        pl.loop(0, rows // size)(block)

    def cross(self, u, i):
        at, t = self.at, self.target(i)
        return remote(self.loc[u].at[1 - at.y, t], self.yrc[u].at[t], self.y_send.at[u], self.y_recv.at[u, i], dp=at.other)

    def first(self, u, i):
        at, t = self.at, self.target(i)
        self.give(u, 1 - at.y, i).wait_recv()

        def put(inner, total):
            self.loc[u][1 - at.y, t, inner] = total.astype(BF)

        self.add(u, 1 - at.y, t, (), put)
        self.cross(u, i).start()

    def hop(self, u, way, s, t):
        src = self.loc[u].at[self.at.y, t]
        dst = self.slot[u].at[way, s]
        if s == 0:
            src, dst = half_of(src, way), half_of(dst, way)
        return remote(
            src, dst, self.ring_send.at[u, way], self.ring_recv.at[u, way, s], mp=self.at.neighbour[way]
        )

    def step(self, u, i):
        at, t = self.at, self.target(i)
        way, dist = self.order[i]
        s = self.plan.hops - dist
        self.give(u, at.y, i).wait_recv()
        self.cross(u, i).wait_recv()
        extra = [self.yrc[u].at[t]]
        ways = (0, 1) if dist in (0, self.plan.hops) else (way,)
        if s > 0:
            for v in ways:
                self.hop(u, v, s - 1, t).wait_recv()
                extra.append(self.slot[u].at[v, s - 1])
        rows = self.loc[u].shape[2]
        quads = self.plan.dp // 4

        def put(inner, total):
            if dist:
                self.loc[u][at.y, t, inner] = total.astype(BF)
            elif quads > 1:
                self.grp[u][lax.div(at.d, 4), inner] = total.astype(BF)
            else:
                to = pl.ds(pl.multiple_of(at.quarter * rows + inner.start, inner.size), inner.size)
                self.fin[u][to] = total.astype(BF)

        self.add(u, at.y, t, extra, put)
        if dist:
            for v in ways:
                self.hop(u, v, s, t).start()
        else:
            for other in range(1, quads):
                self.between(u, other).start()

    def wide_hop(self, u, way, s, t):
        src, dst = self.loc[u].at[:, t], self.wide.at[way, s]
        if s == 0:
            half = self.wide.shape[-1] // 2
            src, dst = (ref.at[:, :, pl.ds(way * half, half)] for ref in (src, dst))
        return remote(
            src, dst, self.ring_send.at[u, way], self.ring_recv.at[u, way, s], mp=self.at.neighbour[way]
        )

    def wide_cross(self, u):
        mine, theirs = self.yrc[u].at[pl.ds(2, 2)], self.yrc[u].at[pl.ds(0, 2)]
        return remote(mine, theirs, self.y_send.at[u], self.y_recv.at[u, 0], dp=self.at.other)

    def wide_step(self, u, i):
        at, t = self.at, self.target(i)
        way, dist = self.order[i]
        s = self.plan.hops - dist
        ways = (0, 1) if dist in (0, self.plan.hops) else (way,)
        for yy in range(2):
            self.give(u, yy, i).wait_recv()
        if s > 0:
            for v in ways:
                self.wide_hop(u, v, s - 1, t).wait_recv()
        for yy in range(2):
            extra = [self.wide.at[v, s - 1, yy] for v in ways] if s > 0 else []

            def put(inner, total):
                if dist:
                    self.loc[u][yy, t, inner] = total.astype(BF)
                else:
                    self.yrc[u][2 + yy, inner] = total.astype(BF)

            self.add(u, yy, t, extra, put)
        if dist:
            for v in ways:
                self.wide_hop(u, v, s, t).start()
        else:
            self.wide_cross(u).start()

    def wide_last(self, u):
        at, quads = self.at, self.plan.dp // 4
        rows = self.loc[u].shape[2]
        self.wide_cross(u).wait_recv()
        for yy in range(2):
            to = pl.ds(pl.multiple_of((2 * yy + at.core) * rows, rows), rows)
            total = self.yrc[u][yy].astype(F32) + self.yrc[u][2 + yy].astype(F32)
            if quads > 1:
                self.grp[u][lax.div(at.d, 4), yy] = total.astype(BF)
            else:
                self.fin[u][to] = total.astype(BF)
        if quads > 1:
            for other in range(1, quads):
                self.between(u, other).start()
            settle(self.grp[u].at[pl.ds(0, quads - 1)], self.grp_recv.at[u])
            for yy in range(2):
                to = pl.ds(pl.multiple_of((2 * yy + at.core) * rows, rows), rows)
                total = self.grp[u][0, yy].astype(F32)
                for other in range(1, quads):
                    total = total + self.grp[u][other, yy].astype(F32)
                self.fin[u][to] = total.astype(BF)
        for what in range(2):
            self.wide_out(u, what).start()

    def wide_out(self, u, what):
        block = piece(self.fin[u], 2 * what + self.at.core)
        return remote(block, block, self.fin_send.at[u, what], self.fin_recv.at[u, what], dp=self.at.sib)

    def wide_sent(self, u):
        hops = self.plan.hops
        settle(self.yrc[u].at[pl.ds(0, 2)], self.y_send.at[u])
        for way in range(2):
            settle(self.wide.at[way, pl.ds(0, hops - 1)], self.ring_send.at[u, way])
            half = self.wide.shape[-1] // 2
            settle(self.wide.at[way, 0, :, :, pl.ds(0, half)], self.ring_send.at[u, way])

    def between(self, u, other):
        at = self.at
        to = lax.rem(at.d + 4 * other, self.plan.dp)
        block = self.grp[u].at[lax.div(at.d, 4)]
        return remote(block, block, self.grp_send.at[u], self.grp_recv.at[u], dp=to)

    def share_out(self, u, what):
        at = self.at
        quarter = at.quarter if what != 1 else 2 - 2 * at.y + at.core
        block = piece(self.fin[u], quarter)
        to = at.other if what == 2 else at.sib
        return remote(block, block, self.fin_send.at[u, what], self.fin_recv.at[u, what], dp=to)

    def last(self, u):
        quads = self.plan.dp // 4
        if quads > 1:
            rows = self.loc[u].shape[2]
            settle(self.grp[u].at[pl.ds(0, quads - 1)], self.grp_recv.at[u])
            total = self.grp[u][0].astype(F32)
            for other in range(1, quads):
                total = total + self.grp[u][other].astype(F32)
            self.fin[u][pl.ds(pl.multiple_of(self.at.quarter * rows, rows), rows)] = total.astype(BF)
        self.share_out(u, 2).start()
        self.share_out(u, 0).start()

    def spread(self, u):
        self.share_out(u, 2).wait_recv()
        self.share_out(u, 1).start()

    def write(self, u, dst, wide=False):
        for what in range(2):
            (self.wide_out if wide else self.share_out)(u, what).wait_recv()
        rows = self.loc[u].shape[2]

        @pl.loop(0, 4)
        def _(q):
            at = pl.ds(pl.multiple_of(q * rows, rows), rows)
            slot = lax.rem(q, 2)

            @pl.when(q > 1)
            def _():
                settle(self.out.at[slot], self.out_sem.at[slot])

            self.out[slot] = self.fin[u][at].astype(F32)
            begun = 0
            for ref in dst:
                size = ref.shape[0] // 4
                pltpu.make_async_copy(
                    self.out.at[slot, pl.ds(begun, size)],
                    ref.at[pl.ds(pl.multiple_of(q * size, size), size)],
                    self.out_sem.at[slot],
                ).start()
                begun += size

        for slot in range(2):
            settle(self.out.at[slot], self.out_sem.at[slot])

    def sent(self, u):
        hops = self.plan.hops
        settle(self.loc[u].at[0], self.y_send.at[u])
        for way in range(2):
            settle(self.slot[u].at[way, pl.ds(0, hops - 1)], self.ring_send.at[u, way])
            settle(half_of(self.slot[u].at[way, 0], way), self.ring_send.at[u, way])

    def release(self, u):
        at = self.at
        self.sent(u)
        for to in ({"dp": at.sib}, {"dp": at.other}, {"mp": at.neighbour[0]}, {"mp": at.neighbour[1]}):
            pl.semaphore_signal(self.credit, inc=1, device_id=to, device_id_type=MESH)

    def claim(self):
        pl.semaphore_wait(self.credit, 4)

    def finish(self, u, wide=False):
        for what in range(2 if wide else 3):
            (self.wide_out if wide else self.share_out)(u, what).wait_send()
        for other in range(1, self.plan.dp // 4):
            self.between(u, other).wait_send()


class RowsOut:
    def __init__(self, plan, at, src, shared, dst, send, recv):
        self.plan, self.at, self.src, self.shared, self.dst, self.send, self.recv = plan, at, src, shared, dst, send, recv
        self.home = at.base + lax.div(at.m, plan.groups)
        self.first = lax.rem(at.m, plan.groups) * plan.group_rows

    def copies(self, what):
        plan, at = self.plan, self.at
        for q in range(plan.mp):
            here = jnp.logical_and(self.home == at.d, at.m == q)
            toks = pl.ds(q * plan.tok, plan.tok)
            if what == 0:
                yield q, here, True, self.src.at[pl.ds(0, plan.own), toks], self.dst.at[
                    pl.ds(self.first + plan.own * at.k, plan.own)
                ]
            else:
                holds = at.k == (q * plan.tok) // plan.part
                yield q, here, holds, self.shared.at[pl.ds((q * plan.tok) % plan.part, plan.tok)], self.dst.at[
                    self.first + plan.own * plan.share
                ]

    def start(self, what, only=None):
        for q, here, wanted, src, dst in self.copies(what):
            if only is not None and only != q:
                continue

            @pl.when(jnp.logical_and(here, wanted))
            def _():
                pltpu.make_async_copy(src, dst, self.recv.at[0]).start()

            @pl.when(jnp.logical_and(jnp.logical_not(here), wanted))
            def _():
                remote(src, dst, self.send.at[q, what], self.recv.at[0], dp=self.home, mp=q).start()

    def finish(self):
        settle(self.dst, self.recv.at[0])
        for what in range(2):
            for q, here, wanted, src, dst in self.copies(what):

                @pl.when(jnp.logical_and(jnp.logical_not(here), wanted))
                def _():
                    settle(src, self.send.at[q, what])


def backward_kernel(
    plan, heads, g0, g1, g2, g3, tok, cot, seg, proj, attn, hid, two, act, der, gain_one, shift_one, gain_two, down_bias,
    blk, tg, o0, o1, o2, o3, vout, *rest,
):
    n, share, own, part, seq = plan.mp, plan.share, plan.own, plan.part, plan.seq
    hops = plan.hops
    held, every = own * seq + part, plan.rows * seq
    width, ff, three, local = hid.shape[1], act.shape[2], proj.shape[2], attn.shape[2]
    (
        stage_a, stage_b, loc_a, loc_b, sbl_a, sbl_b, yrc_a, yrc_b, slot_b, wide_v, fin_a, fin_b, fin_c,
        grp_a, grp_b, grp_c, out_v,
    ) = rest[:17]
    sems, rest = rest[17:29], rest[29:]
    (
        grad_v, low_v, block_v, tgs, tgo, sums, ups, qbs, msg, vrc, vsum,
        load_sem, wgt_sem, blk_send, blk_recv, tg_send, tg_recv, tgs_send, tgs_recv, tgl_sem, v_send, v_recv,
    ) = rest
    at = Place(plan)
    red = Reducer(
        plan, at, (stage_a, stage_b, stage_b), (loc_a, loc_b, loc_b), (sbl_a, sbl_b, sbl_b), (yrc_a, yrc_b, yrc_b),
        (None, slot_b, slot_b), wide_v, (fin_a, fin_b, fin_c), (grp_a, grp_b, grp_c), out_v, sems,
    )
    blocks = RowsOut(plan, at, block_v, block_v.at[own], blk, blk_send, blk_recv)
    greet(plan, at, True)
    part_of = functools.partial
    count = len(red.order)
    first = [[part_of(red.first, u, i) for i in range(count)] for u in range(3)]
    step = [[part_of(red.step, u, i) for i in range(count)] for u in range(3)]
    wide = [part_of(red.wide_step, 0, i) for i in range(count)]
    when_wide = [WIDE_FIRST + i * WIDE_PACE // 4 for i in range(count)]
    red.wide_clear()
    red.clear(1)
    sums[...] = jnp.zeros(sums.shape, F32)
    blocks_held = own * share + 1

    def stream(loads, i):
        def copies(j, slot):
            t = red.target(j)
            for what, (src, dst) in enumerate(loads):
                yield pltpu.make_async_copy(src.at[t], dst.at[slot], wgt_sem.at[what, slot])

        if isinstance(i, int):
            for copy in copies(i, i % 2):
                copy.start()
            return

        @pl.when(i + 1 < n)
        def _():
            for copy in copies(i + 1, lax.rem(i + 1, 2)):
                copy.start()

        for copy in copies(i, lax.rem(i, 2)):
            copy.wait()

    def feed_forward(wd_v, wu_v, act_v, der_v, low_pre, two_v, cot_v, hid_v, sum_v):
        loads = ((g3, wd_v), (g2, wu_v), (act, act_v), (der, der_v))
        stream(loads, 0)
        small = [pltpu.make_async_copy(two, two_v, load_sem.at[0]), pltpu.make_async_copy(hid, hid_v, load_sem.at[1])]
        for r in range(plan.rows):
            extent = seq if r < own else part
            small.append(
                pltpu.make_async_copy(
                    cot.at[r, pl.ds(0, extent)], cot_v.at[pl.ds(r * seq, extent)], load_sem.at[2 + r]
                )
            )
        for copy in small:
            copy.start()
        for copy in small:
            copy.wait()

        @pl.loop(0, blocks_held)
        def _(b):
            rows = pl.ds(pl.multiple_of(b * part, part), part)
            sum_v[rows] = hid_v[rows] + down_bias[...]
            grad_v[rows] = jnp.zeros((part, width), F32)

        def body(i, take):
            take(0)
            stream(loads, i)
            slot = lax.rem(i, 2)
            rows = ff // 4

            @pl.when(i > 0)
            def _():
                red.given(0)
                red.given(1)

            for q in range(4):
                lhs = act_v[slot, :, q * rows : (q + 1) * rows]
                stage_a[q] = lax.dot_general(lhs, cot_v[...], DOWN, preferred_element_type=F32).astype(BF)
            red.begin(0, i)
            take(1)

            act_grad = lax.dot_general(cot_v[...], wd_v[slot], ACROSS, preferred_element_type=F32)
            low = (act_grad * der_v[slot]).astype(BF)
            low_pre[...] = low
            ups[red.target(i)] = jnp.sum(low.astype(F32), axis=0, keepdims=True)
            for q in range(4):
                lhs = low_pre[:, q * rows : (q + 1) * rows]
                stage_b[q] = lax.dot_general(lhs, two_v[...], DOWN, preferred_element_type=F32).astype(BF)
            red.begin(1, i)
            grad_v[...] += lax.dot_general(low_pre[...], wu_v[slot], ACROSS, preferred_element_type=F32)
            sum_v[...] += jnp.dot(act_v[slot], wd_v[slot], preferred_element_type=F32)

        table, middle = {}, {}
        for i in range(count - 1):
            table.setdefault(i + 1, []).append(first[1][i])
        for i in range(count):
            if when_wide[i] < n:
                middle.setdefault(when_wide[i], []).append(wide[i])
        for i in range(count - 2):
            table.setdefault(i + 2, []).append(step[1][i])
        run(n, body, table, middle)
        red.given(0)
        red.given(1)
        first[1][count - 1]()
        step[1][count - 2]()

        @pl.loop(0, blocks_held)
        def _(b):
            r, start = lax.div(b, share), pl.multiple_of(lax.rem(b, share) * part, part)
            rows = pl.ds(pl.multiple_of(b * part, part), part)
            block_v[r, pl.ds(start, part)] = sum_v[rows].astype(BF)
            hidden, grad, cot_f = hid_v[rows], grad_v[rows], cot_v[rows].astype(F32)
            unit, scale, _ = norm(hidden, gain_two[...], 0.0)
            hidden_grad = cot_f + norm_back(unit, scale, gain_two[...], grad)
            grad_v[rows] = hidden_grad
            low_v[rows] = hidden_grad.astype(BF)
            for line, value in ((2, hidden_grad), (3, grad * unit), (4, grad), (5, cot_f)):
                sums[pl.ds(line, 1)] += jnp.sum(value, axis=0, keepdims=True)

        for q in range(n):
            if q < BLOCKS_MID:
                blocks.start(0, q)
                blocks.start(1, q)

    pl.run_scoped(
        feed_forward,
        pltpu.VMEM((2,) + g3.shape[1:], BF), pltpu.VMEM((2,) + g2.shape[1:], BF), pltpu.VMEM((2, held, ff), BF),
        pltpu.VMEM((2, held, ff), F32), pltpu.VMEM((held, ff), BF), pltpu.VMEM((held, width), BF),
        pltpu.VMEM((held, width), BF), pltpu.VMEM((held, width), F32), pltpu.VMEM((held, width), F32),
    )

    def attention(wq_v, wo_v, proj_v, attn_v, head_v, three_v, tok_v, one_v, back_v, out3, columns):
        loads = ((g0, wq_v), (g1, wo_v), (proj, proj_v), (attn, attn_v))
        stream(loads, 0)
        load = pltpu.make_async_copy(tok, tok_v, load_sem.at[0])
        load.start()
        step[1][count - 1]()
        red.last(1)
        red.release(1)
        load.wait()

        @pl.loop(0, plan.rows * share)
        def _(b):
            r, start = lax.div(b, share), pl.multiple_of(lax.rem(b, share) * part, part)
            rows = pl.ds(pl.multiple_of(b * part, part), part)
            values = tok_v[r, pl.ds(start, part)].astype(F32)
            one_v[rows] = norm_rows(values, gain_one[...], shift_one[...]).astype(BF)
            back_v[rows] = jnp.zeros((part, width), F32)

        three_v[...] = jnp.zeros(three_v.shape, BF)
        label_columns(seg, plan.rows, columns)
        red.spread(1)

        def body(i, take):
            take(0)
            stream(loads, i)
            slot = lax.rem(i, 2)

            head_v[...] = lax.dot_general(low_v[...], wo_v[slot], ACROSS, preferred_element_type=F32).astype(BF)

            def attend(r, first, amount):
                allowed = same_image(seg, columns, r, amount)
                keys, queries = pl.ds(pl.multiple_of(r * seq, seq), seq), pl.ds(first, amount)
                for h in range(heads):
                    col = h * 3 * HEAD_DIM
                    query = proj_v[slot, queries, col : col + HEAD_DIM]
                    key = proj_v[slot, keys, col + HEAD_DIM : col + 2 * HEAD_DIM]
                    value = proj_v[slot, keys, col + 2 * HEAD_DIM : col + 3 * HEAD_DIM]
                    head_grad = head_v[queries, h * HEAD_DIM : (h + 1) * HEAD_DIM]
                    full = probs_of(key, query, allowed)
                    value_grad = jnp.dot(full.astype(BF), head_grad, preferred_element_type=F32)
                    probs_grad = lax.dot_general(value, head_grad, ACROSS, preferred_element_type=F32)
                    delta = jnp.sum(probs_grad * full, axis=0, keepdims=True)
                    low = (jnp.where(allowed, full * (probs_grad - delta), 0.0) * HEAD_DIM ** (-0.5)).astype(BF)
                    query_grad = lax.dot_general(low, key, DOWN, preferred_element_type=F32)
                    key_grad = jnp.dot(low, query, preferred_element_type=F32)
                    three_v[queries, col : col + HEAD_DIM] = query_grad.astype(BF)
                    three_v[keys, col + HEAD_DIM : col + 2 * HEAD_DIM] = key_grad.astype(BF)
                    three_v[keys, col + 2 * HEAD_DIM : col + 3 * HEAD_DIM] = value_grad.astype(BF)

            @pl.loop(0, own)
            def _(r):
                attend(r, pl.multiple_of(r * seq, seq), seq)

            take(1)
            attend(own, own * seq, part)

            @pl.when(i > 0)
            def _():
                red.given(2)

            @pl.when(i == 0)
            def _():
                red.claim()

            wide, narrow = three // 4, local // 4
            weight = lax.dot_general(three_v[...], one_v[...], DOWN, preferred_element_type=F32).astype(BF)
            out_weight = lax.dot_general(attn_v[slot], low_v[...], DOWN, preferred_element_type=F32).astype(BF)
            for q in range(4):
                stage_b[q, :wide] = weight[q * wide : (q + 1) * wide]
                stage_b[q, wide:] = out_weight[q * narrow : (q + 1) * narrow]
            red.begin(2, i)

            back_v[...] += lax.dot_general(three_v[...], wq_v[slot], ACROSS, preferred_element_type=F32)
            qbs[red.target(i)] = jnp.sum(three_v[...].astype(F32), axis=0, keepdims=True)

        late = max(when_wide[-1] - n + 1, 1)
        table = {3: [part_of(red.write, 1, (o1,))]}
        table.setdefault(late, []).append(part_of(red.wide_last, 0))
        table.setdefault(min(late + 2, n - 1), []).append(part_of(red.write, 0, (o0,), True))
        for i in range(count):
            if when_wide[i] >= n:
                table.setdefault(when_wide[i] - n, []).insert(0, wide[i])
        for i in range(count - 1):
            table.setdefault(i + 1, []).insert(0, first[2][i])
        middle = {i + 2: [step[2][i]] for i in range(count - 2)}
        for q in range(BLOCKS_MID, n):
            for what in range(2):
                table.setdefault((q - BLOCKS_MID) * BLOCKS_OVER // n, []).append(part_of(blocks.start, what, q))
        run(n, body, table, middle)
        red.given(2)
        first[2][count - 1]()
        step[2][count - 2]()

        @pl.loop(0, plan.rows * share)
        def _(b):
            r, start = lax.div(b, share), pl.multiple_of(lax.rem(b, share) * part, part)
            rows = pl.ds(pl.multiple_of(b * part, part), part)
            unit, scale, _ = norm(tok_v[r, pl.ds(start, part)].astype(F32), gain_one[...], 0.0)
            grad = back_v[rows]
            for line, value in ((0, grad * unit), (1, grad)):
                sums[pl.ds(line, 1)] += jnp.sum(value, axis=0, keepdims=True)
            grad = norm_back(unit, scale, gain_one[...], grad)

            @pl.when(b < blocks_held)
            def _():
                mine = pl.ds(pl.multiple_of(jnp.minimum(b, blocks_held - 1) * part, part), part)
                out3[r, pl.ds(start, part)] = (grad + grad_v[mine]).astype(BF)

            @pl.when(b >= blocks_held)
            def _():
                out3[r, pl.ds(start, part)] = grad.astype(BF)

        tokens = RowsOut(plan, at, out3, tgo, tg, tg_send, tg_recv)
        for e in range(share):
            src = out3.at[own, pl.ds(e * part, part)]
            if e == 0:
                pltpu.make_async_copy(src, tgs.at[0], tgl_sem.at[0]).start()
            else:
                to = at.base + lax.rem(at.k + e, share)
                remote(src, tgs.at[share - e], tgs_send.at[e], tgs_recv.at[share - e], dp=to).start()
        lines = [-(-size // 128) for size in (ff, three)]
        msg[...] = jnp.zeros(msg.shape, F32)
        for q in range(n):
            msg[q, :8, : width // n] = sums[:, q * (width // n) : (q + 1) * (width // n)]
            line = 8
            for ref, size in ((ups, ff), (qbs, three)):
                for first_col in range(0, size, 128):
                    cols = min(128, size - first_col)
                    msg[q, line : line + 1, :cols] = ref[q, :, first_col : first_col + cols]
                    line += 1
        me = at.d * n + at.m

        def one(i, carry):
            to = lax.rem(me + i, plan.all)
            e, q = lax.div(to, n), lax.rem(to, n)
            remote(msg.at[q], vrc.at[me], v_send.at[0], v_recv.at[0], dp=e, mp=q).start()
            return carry

        lax.fori_loop(1, plan.all, one, 0)
        pltpu.make_async_copy(msg.at[at.m], vrc.at[me], v_recv.at[0]).start()
        tokens.start(0)
        for e in range(1, share):
            settle(tgs.at[e], tgs_recv.at[e])
        settle(tgs.at[0], tgl_sem.at[0])
        tgo[...] = sum(tgs[e].astype(F32) for e in range(share)).astype(BF)
        tokens.start(1)
        step[2][count - 1]()
        red.last(2)
        settle(vrc, v_recv.at[0])
        vsum[...] = jnp.sum(vrc[...], axis=0)
        for e in range(1, n):
            remote(vsum, vout.at[at.m], v_send.at[1], v_recv.at[1], mp=lax.rem(at.m + e, n)).start()
        pltpu.make_async_copy(vsum, vout.at[at.m], v_recv.at[1]).start()
        red.spread(2)
        red.write(2, (o2, o3))
        for u in range(3):
            red.finish(u, u == 0)
        red.wide_sent(0)
        red.sent(2)
        for e in range(1, share):
            settle(tgs.at[0], tgs_send.at[e])
        blocks.finish()
        tokens.finish()
        settle(vout, v_recv.at[1])
        settle(vrc.at[pl.ds(0, plan.all - 1)], v_send.at[0])
        settle(vout.at[pl.ds(0, n - 1)], v_send.at[1])

    pl.run_scoped(
        attention,
        pltpu.VMEM((2,) + g0.shape[1:], BF), pltpu.VMEM((2,) + g1.shape[1:], BF), pltpu.VMEM((2, every, three), BF),
        pltpu.VMEM((2, held, local), BF), pltpu.VMEM((held, local), BF), pltpu.VMEM((every, three), BF),
        pltpu.VMEM((plan.rows, seq, width), BF), pltpu.VMEM((every, width), BF), pltpu.VMEM((every, width), F32),
        pltpu.VMEM((plan.rows, seq, width), BF), pltpu.VMEM((plan.rows, seq, 128), F32),
    )


def backward(plan, weights, tok3, cot3, seg, proj, attn, hid, two, act, der, vectors):
    n, share = plan.mp, plan.share
    held, width = hid.shape
    ff, three, local = act.shape[2], proj.shape[2], attn.shape[2]
    heads = local // HEAD_DIM
    quads, quarter = plan.dp // 4, ff // 4
    if local + three != ff:
        raise ValueError("unsupported sizes")
    any_space = pl.BlockSpec(memory_space=pl.ANY)
    in_vmem = pl.BlockSpec(memory_space=pltpu.VMEM)
    dma = pltpu.SemaphoreType.DMA
    rows = jax.ShapeDtypeStruct((plan.rows_dev, plan.tok, width), BF)
    shard = jax.ShapeDtypeStruct((ff, width), F32)
    size = 8 + -(-ff // 128) + -(-three // 128)
    size = -(-size // 8) * 8
    vec = (size, 128)
    return pl.pallas_call(
        functools.partial(backward_kernel, plan, heads),
        out_shape=[
            rows, rows, shard, shard, jax.ShapeDtypeStruct((three, width), F32), jax.ShapeDtypeStruct((local, width), F32),
            jax.ShapeDtypeStruct((n,) + vec, F32),
        ],
        in_specs=[any_space] * 6 + [in_vmem] + [any_space] * 6 + [in_vmem] * 4,
        out_specs=[any_space] * 7,
        scratch_shapes=[
            *[pltpu.VMEM((4, quarter, width), BF)] * 2,
            *[pltpu.VMEM((2, n, quarter, width), BF)] * 4,
            pltpu.VMEM((4, quarter, width), BF),
            pltpu.VMEM((n, quarter, width), BF),
            pltpu.VMEM((2, plan.hops, quarter, width), BF),
            pltpu.VMEM((2, plan.hops, 2, quarter, width), BF),
            *[pltpu.VMEM((ff, width), BF)] * 3,
            pltpu.VMEM((quads, 2) + ((quarter, width) if quads > 1 else (8, 128)), BF),
            *[pltpu.VMEM((quads,) + ((quarter, width) if quads > 1 else (8, 128)), BF)] * 2,
            pltpu.VMEM((2, quarter, width), F32),
            dma((3,)), dma((3, n, 2)), dma((3,)), dma((3, n)), dma((3, 2)), dma((3, 2, plan.hops)), dma((3,)), dma((3,)),
            dma((3, 3)), dma((3, 3)), dma((2,)), pltpu.SemaphoreType.REGULAR,
            pltpu.VMEM((held, width), F32), pltpu.VMEM((held, width), BF), pltpu.VMEM((plan.rows, plan.seq, width), BF),
            pltpu.VMEM((share, plan.part, width), BF), pltpu.VMEM((plan.part, width), BF), pltpu.VMEM((8, width), F32),
            pltpu.VMEM((n, 1, ff), F32), pltpu.VMEM((n, 1, three), F32), pltpu.VMEM((n,) + vec, F32),
            pltpu.VMEM((plan.all,) + vec, F32), pltpu.VMEM(vec, F32),
            dma((2 + plan.rows,)), dma((4, 2)), dma((n, 2)), dma((1,)), dma((n, 2)), dma((1,)), dma((share,)),
            dma((share,)), dma((1,)), dma((2,)), dma((2,)),
        ],
        compiler_params=pltpu.CompilerParams(
            collective_id=1, has_side_effects=True, vmem_limit_bytes=61 << 20
        ),
        name="backward",
    )(*weights, tok3, cot3, seg, proj, attn, hid, two, act, der, *vectors)


def probs_of(key, query, allowed):
    raw = lax.dot_general(key, query, ACROSS, preferred_element_type=F32)
    scores = jnp.where(allowed, raw * HEAD_DIM ** (-0.5), MASKED)
    raised = jnp.exp(scores - jnp.max(scores, axis=0, keepdims=True))
    return raised * (1.0 / jnp.sum(raised, axis=0, keepdims=True))


def label_columns(labels, rows, columns):
    for r in range(rows):
        line = labels[pl.ds(r, 1)].astype(F32)
        columns[r] = jnp.transpose(jnp.broadcast_to(line, (128, line.shape[1])))


def same_image(labels, columns, r, amount):
    line = labels[pl.ds(r, 1)].astype(F32)[:, :amount]
    down = columns[r]
    if amount < 128:
        return down[:, :amount] == line
    return jnp.concatenate([down] * (amount // 128), axis=1) == line


def norm(values, gain_vec, shift_vec):
    centred = values - jnp.mean(values, axis=-1, keepdims=True)
    scale = lax.rsqrt(jnp.mean(centred * centred, axis=-1, keepdims=True) + EPS)
    unit = centred * scale
    return unit, scale, unit * gain_vec + shift_vec


def norm_back(unit, scale, gain_vec, grad):
    pulled = grad * gain_vec
    inner = jnp.mean(pulled * unit, axis=-1, keepdims=True)
    return scale * (pulled - jnp.mean(pulled, axis=-1, keepdims=True) - unit * inner)


def per_device(
    plan, tokens_in, segment_ids, attn_gain, attn_shift, qkv_weight, qkv_bias, out_weight, out_bias, mlp_gain, mlp_shift,
    up_weight, up_bias, down_weight, down_bias, cotangent,
):
    n, width = plan.mp, tokens_in.shape[2]
    ff_local = up_weight.shape[1]
    heads_local = qkv_bias.shape[1] // HEAD_DIM
    parts = qkv_bias.reshape(2, heads_local, HEAD_DIM)
    bias_three = jnp.stack([parts[0], jnp.zeros_like(parts[0]), parts[1]], axis=1).reshape(1, -1)
    vectors = [v.reshape(1, width) for v in (attn_gain, attn_shift, out_bias, mlp_gain, mlp_shift)]
    tok3, cot3, seg, wq, wo, wu, wd, proj, attn, hidden, normed_two, act_low, gelu_slope = forward(
        plan, tokens_in, cotangent, segment_ids, (bias_three, up_bias.reshape(1, ff_local)),
        (qkv_weight, out_weight, up_weight, down_weight), vectors,
    )
    block_out, tokens_low, down_grad, up_grad, qkv_grad, out_grad, sums = backward(
        plan, (wq, wo, wu, wd), tok3, cot3, seg, proj, attn, hidden, normed_two, act_low, gelu_slope,
        [v.reshape(1, width) for v in (attn_gain, attn_shift, mlp_gain, down_bias)],
    )
    local, three = out_weight.shape[0], qkv_weight.shape[1]
    six = jnp.swapaxes(sums[:, :6, : width // n], 0, 1).reshape(6, width)
    mine = lax.dynamic_index_in_dim(sums, lax.axis_index("mp"), 0, keepdims=False)
    lines = [-(-size // 128) for size in (ff_local, three)]
    up_bias_grad = mine[8 : 8 + lines[0]].reshape(-1)[:ff_local]
    bias_sums = mine[8 + lines[0] : 8 + sum(lines)].reshape(-1)[:three].reshape(heads_local, 3, HEAD_DIM)
    qkv_bias_grad = jnp.stack([bias_sums[:, 0], bias_sums[:, 2]]).reshape(2, local)
    return (
        block_out, tokens_low.astype(F32), six[0], six[1], qkv_grad.T, qkv_bias_grad, out_grad, six[2], six[3], six[4],
        up_grad.T, up_bias_grad, down_grad, six[5],
    )


def solution(mesh):
    dp, mp = mesh.shape["dp"], mesh.shape["mp"]
    rows_spec = P("dp", "mp", None)
    in_specs = (
        rows_spec, P("dp", None), P(), P(), P(None, "mp"), P(None, "mp"), P("mp", None), P(), P(), P(),
        P(None, "mp"), P("mp"), P("mp", None), P(), rows_spec,
    )
    out_specs = (
        rows_spec, rows_spec, P(), P(), P(None, "mp"), P(None, "mp"), P("mp", None), P(), P(), P(),
        P(None, "mp"), P("mp"), P("mp", None), P(),
    )

    def run(tokens_in, segment_ids, *rest):
        rows_all, seq_len, _ = tokens_in.shape
        plan = Plan(dp, mp, rows_all // dp, seq_len // mp, seq_len)
        return jax.shard_map(
            functools.partial(per_device, plan), mesh=mesh, in_specs=in_specs, out_specs=out_specs, check_vma=False
        )(tokens_in, segment_ids, *rest)

    return run
```

```python
import functools
import itertools
import math

import jax
import jax.numpy as jnp
from jax import lax
from jax.experimental import pallas as pl
from jax.experimental.pallas import tpu as pltpu
from jax.sharding import PartitionSpec as P

HEAD_DIM = 64
EPS = 1e-06
MASKED = -1000000000.0
MESH = pl.DeviceIdType.MESH
BF = jnp.bfloat16
F32 = jnp.float32
ACROSS = (((1,), (1,)), ((), ()))
DOWN = (((0,), (0,)), ((), ()))


WIDE_FIRST, WIDE_PACE = 1, 4
BLOCKS_MID, BLOCKS_OVER = 8, 4


class Plan:
    def __init__(self, dp, mp, rows_dev, tok_local, seq_len):
        self.dp, self.mp, self.rows_dev, self.tok, self.seq = dp, mp, rows_dev, tok_local, seq_len
        self.share = mp // math.gcd(rows_dev, mp)
        self.group_rows = rows_dev * self.share // mp
        self.own = self.group_rows // self.share
        if self.share % 2 or dp % self.share or dp % 4 or self.group_rows != self.own * self.share + 1:
            raise ValueError("unsupported sizes")
        self.groups = mp // self.share
        self.part = seq_len // self.share
        self.rows = self.own + 1
        self.hops = mp // 2
        self.all = dp * mp

    def ring_at(self, p):
        p = lax.rem(p, self.mp)
        back = lax.div(p, self.mp // 2)
        return 2 * p * (1 - back) + (2 * self.mp - 1 - 2 * p) * back


class Place:
    def __init__(self, plan):
        d, m = lax.axis_index("dp"), lax.axis_index("mp")
        odd = lax.rem(m, 2)
        self.d, self.m = d, m
        self.p = lax.div(m, 2) * (1 - odd) + (plan.mp - 1 - lax.div(m, 2)) * odd
        self.core = lax.rem(d, 2)
        self.sib = d + 1 - 2 * self.core
        self.y = lax.rem(lax.div(d, 2), 2)
        self.other = d + 2 - 4 * self.y
        self.k = lax.rem(d, plan.share)
        self.base = d - self.k
        self.quarter = 2 * self.y + self.core
        self.neighbour = (plan.ring_at(self.p + 1), plan.ring_at(self.p + plan.mp - 1))

    def away(self, plan, way, s):
        return plan.ring_at(self.p + plan.mp - s if way == 0 else self.p + s)


def greet(plan, at, everyone):
    barrier = pltpu.get_barrier_semaphore()
    span = plan.dp if everyone else max(plan.share, 4)
    base = lax.div(at.d, span) * span

    def one(i, carry):
        e, q = base + lax.div(i, plan.mp), lax.rem(i, plan.mp)

        @pl.when(jnp.logical_or(e != at.d, q != at.m))
        def _():
            pl.semaphore_signal(barrier, inc=1, device_id={"dp": e, "mp": q}, device_id_type=MESH)

        return carry

    lax.fori_loop(0, span * plan.mp, one, 0)


def meet(plan, everyone):
    span = plan.dp if everyone else max(plan.share, 4)
    pl.semaphore_wait(pltpu.get_barrier_semaphore(), span * plan.mp - 1)


def remote(src, dst, send, recv, **to):
    return pltpu.make_async_remote_copy(src, dst, send, recv, device_id=to, device_id_type=MESH)


def settle(ref, sem):
    pltpu.make_async_copy(ref, ref, sem).wait()


def piece(ref, quarter, half=None):
    rows, cols = ref.shape[0] // 4, ref.shape[1]
    first = quarter * rows
    if half is None:
        return ref.at[pl.ds(pl.multiple_of(first, rows), rows)]
    if cols % 256 == 0:
        return ref.at[pl.ds(pl.multiple_of(first, rows), rows), pl.ds(half * (cols // 2), cols // 2)]
    return ref.at[pl.ds(pl.multiple_of(first + half * (rows // 2), rows // 2), rows // 2)]


def half_of(ref, half):
    rows, cols = ref.shape
    if cols % 256 == 0:
        return ref.at[:, pl.ds(half * (cols // 2), cols // 2)]
    return ref.at[pl.ds(half * (rows // 2), rows // 2)]


class Gatherer:
    def __init__(self, plan, at, shards, full, sems):
        self.plan, self.at, self.shards, self.full = plan, at, shards, full
        self.own_sem, self.ring_send, self.ring_recv, self.y_send, self.y_recv, self.sib_send, self.sib_recv = sems

    def _half(self, way, s):
        return way if s == self.plan.hops - 1 else None

    def ring(self, w, way, s):
        at, origin = self.at, self.at.away(self.plan, way, s)
        half = self._half(way, s)
        dst = piece(self.full[w].at[origin], at.quarter, half)
        src = piece(self.shards[w], at.quarter, half) if s == 0 else dst
        return remote(src, dst, self.ring_send.at[w, way], self.ring_recv.at[w, way, s], mp=at.neighbour[way])

    def cross(self, w, way, s):
        at, origin = self.at, self.at.away(self.plan, way, s + 1)
        block = piece(self.full[w].at[origin], at.quarter, self._half(way, s))
        return remote(block, block, self.y_send.at[w], self.y_recv.at[w, way, s], dp=at.other)

    def give(self, w, way, s, mine):
        at, origin = self.at, self.at.away(self.plan, way, s + 1)
        quarter = at.quarter if mine else 2 - 2 * at.y + at.core
        block = piece(self.full[w].at[origin], quarter, self._half(way, s))
        return remote(block, block, self.sib_send.at[w], self.sib_recv.at[w], dp=at.sib)

    def begin(self, w):
        for way in range(2):
            self.ring(w, way, 0).start()
        pltpu.make_async_copy(self.shards[w], self.full[w].at[self.at.m], self.own_sem.at[w]).start()

    def step(self, w, s):
        for way in range(2):
            self.ring(w, way, s).wait_recv()
            if s < self.plan.hops - 1:
                self.ring(w, way, s + 1).start()
            self.cross(w, way, s).start()
            self.give(w, way, s, True).start()

    def follow(self, w, s):
        for way in range(2):
            self.cross(w, way, s).wait_recv()
            self.give(w, way, s, False).start()

    def arrived(self, w):
        n, rows = self.plan.mp, self.shards[w].shape[0]
        settle(self.full[w].at[pl.ds(0, n - 1), pl.ds(0, rows // 2)], self.sib_recv.at[w])
        settle(self.shards[w], self.own_sem.at[w])

    def finish(self, w):
        n, rows = self.plan.mp, self.shards[w].shape[0]
        settle(self.full[w].at[pl.ds(0, n - 1), pl.ds(0, rows // 2)], self.sib_send.at[w])
        settle(self.full[w].at[pl.ds(0, n - 1), pl.ds(0, rows // 4)], self.y_send.at[w])
        for way in range(2):
            settle(self.full[w].at[pl.ds(0, self.plan.hops - 1), pl.ds(0, rows // 4)], self.ring_send.at[w, way])
            settle(piece(self.full[w].at[0], 0, way), self.ring_send.at[w, way])


def gatherer_sems(plan, count):
    dma = pltpu.SemaphoreType.DMA
    return [
        dma((count,)), dma((count, 2)), dma((count, 2, plan.hops)), dma((count,)), dma((count, 2, plan.hops)),
        dma((count,)), dma((count,)),
    ]


class RowsIn:
    def __init__(self, plan, at, src, dst, send, recv):
        self.plan, self.at, self.src, self.dst, self.send, self.recv = plan, at, src, dst, send, recv

    def copies(self):
        plan, at = self.plan, self.at
        mine = pl.ds(pl.multiple_of(at.m * plan.tok, plan.tok), plan.tok)
        for j in range(plan.groups):
            q = at.k * plan.groups + j
            first = j * plan.group_rows
            for e in range(plan.share):
                here = jnp.logical_and(at.k == e, at.m == q)
                holds = lax.div(at.m * plan.tok, plan.part) == e
                to = lax.rem(at.m * plan.tok + plan.seq - e * plan.part, plan.seq)
                to = pl.ds(pl.multiple_of(to, plan.tok), plan.tok)
                yield here, True, q, e, j, 0, self.src.at[pl.ds(first + plan.own * e, plan.own)], self.dst.at[
                    pl.ds(0, plan.own), mine
                ]
                yield here, holds, q, e, j, 1, self.src.at[first + plan.own * plan.share], self.dst.at[plan.own, to]

    def start(self, only=None):
        for here, wanted, q, e, j, what, src, dst in self.copies():
            if only is not None and only != j:
                continue

            @pl.when(jnp.logical_and(here, wanted))
            def _():
                pltpu.make_async_copy(src, dst, self.recv.at[what]).start()

            @pl.when(jnp.logical_and(jnp.logical_not(here), wanted))
            def _():
                remote(src, dst, self.send.at[j, e, what], self.recv.at[what], dp=self.at.base + e, mp=q).start()

    def arrived(self):
        plan = self.plan
        settle(self.dst.at[pl.ds(0, plan.own)], self.recv.at[0])
        settle(self.dst.at[plan.own, pl.ds(0, plan.part)], self.recv.at[1])

    def finish(self):
        for here, wanted, q, e, j, what, src, dst in self.copies():

            @pl.when(jnp.logical_and(jnp.logical_not(here), wanted))
            def _():
                settle(src, self.send.at[j, e, what])


def run(count, body, *tables):
    def one(j, carry):
        def take(k):
            for when, thunks in sorted(tables[k].items()):

                @pl.when(j == when)
                def _():
                    for thunk in thunks:
                        thunk()

        body(j, take)
        return carry

    lax.fori_loop(0, count, one, 0)


def spread_over(count, thunks, first=0):
    table = {}
    for i, thunk in enumerate(thunks):
        table.setdefault(first + i * (count - first) // len(thunks), []).append(thunk)
    return table


def norm_rows(values, gain_vec, shift_vec):
    unit, _, normed = norm(values, gain_vec, shift_vec)
    return normed


def forward_kernel(
    plan, heads, tok, cot, seg, bq, bu, w0, w1, w2, w3, gain_one, shift_one, out_bias, gain_two, shift_two,
    tok_o, cot3, seg_o, g0, g1, g2, g3, proj_o, attn_o, hid_o, two_o, act_o, der_o,
    tok_v, one_v, wq_v, proj_v, attn_v, wo_v, hid_v, two_v, wu_v, act_v, der_v, seg_v, columns, bq_v, bu_v,
    tok_send, tok_recv, cot_send, cot_recv, seg_send, seg_recv, bias_send, bias_recv, part_send, part_recv, load_sem, save_sem, act_sem, *sems,
):
    n, share, own, part, seq = plan.mp, plan.share, plan.own, plan.part, plan.seq
    held = own * seq + part
    at = Place(plan)
    gat = Gatherer(plan, at, (w0, w1, w2, w3), (g0, g1, g2, g3), sems)
    tokens = RowsIn(plan, at, tok, tok_v, tok_send, tok_recv)
    cots = RowsIn(plan, at, cot, cot3, cot_send, cot_recv)
    hops = plan.hops
    greet(plan, at, False)
    meet(plan, False)

    gat.begin(0)
    gat.begin(2)
    tokens.start(0)
    biases = ((bq, bq_v, 0), (bu, bu_v, 1))
    for src, dst, i in biases:
        pltpu.make_async_copy(src, dst.at[at.m], bias_recv.at[i]).start()
        for s in range(1, n):
            remote(src, dst.at[at.m], bias_send.at[i], bias_recv.at[i], mp=lax.rem(at.m + s, n)).start()
    pltpu.make_async_copy(seg, seg_v.at[at.k], seg_recv.at[0]).start()
    for e in range(1, share):
        remote(seg, seg_v.at[at.k], seg_send.at[0], seg_recv.at[0], dp=at.base + lax.rem(at.k + e, share)).start()
    part_of = functools.partial
    hop = [[part_of(gat.step, w, s) for s in range(hops)] for w in range(4)]
    after = [[part_of(gat.follow, w, s) for s in range(hops)] for w in range(4)]
    begin = [part_of(gat.begin, w) for w in range(4)]
    token = [part_of(tokens.start, j) for j in range(plan.groups)]
    between = {0: [begin[3], hop[2][0]] + token[1:2], 1: token[2:3] + [hop[2][1], after[2][0]], 2: token[3:] + [hop[3][0]]}
    between[hops - 1] = between.get(hops - 1, []) + [hop[2][2], after[2][1], begin[1]]
    for s in range(hops):
        hop[0][s]()
        if s:
            after[0][s - 1]()
        for thunk in between.get(s, []):
            thunk()
    after[0][hops - 1]()
    tokens.arrived()
    mine = tok_v.at[own, pl.ds(0, part)]
    for e in range(1, share):
        remote(
            mine, tok_v.at[own, pl.ds((share - e) * part, part)], part_send.at[0], part_recv.at[0],
            dp=at.base + lax.rem(at.k + e, share),
        ).start()
    others = tok_v.at[own, pl.ds(part, (share - 1) * part)]
    settle(others, part_recv.at[0])
    save_tok = pltpu.make_async_copy(tok_v, tok_o, save_sem.at[0])
    save_tok.start()
    gain, shift = gain_one[...], shift_one[...]

    @pl.loop(0, plan.rows * share)
    def _(b):
        r, first = lax.div(b, share), pl.multiple_of(lax.rem(b, share) * part, part)
        values = tok_v[r, pl.ds(first, part)].astype(F32)
        one_v[pl.ds(pl.multiple_of(b * part, part), part)] = norm_rows(values, gain, shift).astype(BF)

    settle(seg_v, seg_recv.at[0])
    labels = []
    for r in range(plan.rows):
        row = at.m * plan.group_rows + (own * at.k + r if r < own else own * share)
        line = seg_v[lax.div(row, plan.rows_dev), pl.ds(lax.rem(row, plan.rows_dev), 1)]
        if r == own:
            turned = line
            for e in range(1, share):
                moved = jnp.concatenate([line[:, e * part :], line[:, : e * part]], axis=1)
                turned = jnp.where(at.k == e, moved, turned)
            line = turned
        seg_o[pl.ds(r, 1)] = line
    label_columns(seg_o, plan.rows, columns)
    for src, dst, i in biases:
        settle(dst, bias_recv.at[i])

    gat.arrived(0)
    load_q = pltpu.make_async_copy(g0, wq_v, load_sem.at[0])
    load_q.start()
    load_q.wait()

    def attend_shard(s, take):
        take(0)
        projected = jnp.dot(one_v[...], wq_v[s], preferred_element_type=F32) + bq_v[s]
        proj_v[s] = projected.astype(BF)
        take(1)

        def attend(r, first, amount):
            allowed = same_image(seg_o, columns, r, amount)
            keys = pl.ds(pl.multiple_of(r * seq, seq), seq)
            for h in range(heads):
                col = h * 3 * HEAD_DIM
                query = proj_v[s, pl.ds(first, amount), col : col + HEAD_DIM]
                key = proj_v[s, keys, col + HEAD_DIM : col + 2 * HEAD_DIM]
                value = proj_v[s, keys, col + 2 * HEAD_DIM : col + 3 * HEAD_DIM]
                probs = probs_of(key, query, allowed).astype(BF)
                mixed = lax.dot_general(probs, value, DOWN, preferred_element_type=F32)
                attn_v[s, pl.ds(first, amount), h * HEAD_DIM : (h + 1) * HEAD_DIM] = mixed.astype(BF)

        for r in range(own):
            attend(r, r * seq, seq)
            take(2 + r)
        attend(own, own * seq, part)

    rest = []
    for w, done in ((2, 3), (3, 1), (1, 0)):
        steps = [hop[w][s : s + 1] + (after[w][s - 1 : s] if s else []) for s in range(done, hops)]
        rest.append(steps + [after[w][hops - 1 :]])
    rest.append([[part_of(cots.start, j)] for j in range(plan.groups)])
    moves = []
    for at_once in itertools.zip_longest(*rest):
        moves += [thunks for thunks in at_once if thunks]
    points = 2 + own
    tables = [{} for _ in range(points)]
    for j, thunks in spread_over(points * n, moves).items():
        tables[j % points][j // points] = [thunk for some in thunks for thunk in some]
    run(n, attend_shard, *tables)
    save_proj = pltpu.make_async_copy(proj_v, proj_o, save_sem.at[1])
    save_proj.start()
    save_attn = pltpu.make_async_copy(attn_v, attn_o, save_sem.at[2])
    save_attn.start()

    gat.arrived(1)
    load_o = pltpu.make_async_copy(g1, wo_v, load_sem.at[0])
    load_o.start()
    load_o.wait()
    bias, gain, shift = out_bias[...], gain_two[...], shift_two[...]

    def branch(first, amount, values):
        rows = pl.ds(first, amount)
        total = values.astype(F32) + bias
        for s in range(n):
            total = total + jnp.dot(attn_v[s, rows], wo_v[s], preferred_element_type=F32)
        hid_v[rows] = total
        two_v[rows] = norm_rows(total, gain, shift).astype(BF)

    @pl.loop(0, own)
    def _(r):
        branch(pl.multiple_of(r * seq, seq), seq, tok_v[r])

    branch(own * seq, part, tok_v[own, :part])

    save_hid = pltpu.make_async_copy(hid_v, hid_o, save_sem.at[3])
    save_hid.start()
    save_two = pltpu.make_async_copy(two_v, two_o, save_sem.at[4])
    save_two.start()
    gat.arrived(2)
    load_u = pltpu.make_async_copy(g2, wu_v, load_sem.at[0])
    load_u.start()
    load_u.wait()

    def feed_shard(s, take):
        pre = jnp.dot(two_v[...], wu_v[s], preferred_element_type=F32) + bu_v[s]
        below = 0.5 * (1.0 + lax.erf(pre * math.sqrt(0.5)))
        density = jnp.exp(-0.5 * pre * pre) * (1.0 / math.sqrt(2.0 * math.pi))
        act_v[s] = (pre * below).astype(BF)
        der_v[s] = below + pre * density

        pltpu.make_async_copy(act_v.at[s], act_o.at[s], act_sem.at[0]).start()
        pltpu.make_async_copy(der_v.at[s], der_o.at[s], act_sem.at[1]).start()

    run(n, feed_shard)
    gat.arrived(3)
    for w in range(4):
        gat.finish(w)
    tokens.finish()
    settle(others, part_send.at[0])
    cots.arrived()
    cots.finish()
    for src, dst, i in biases:
        settle(dst.at[pl.ds(0, n - 1)], bias_send.at[i])
    settle(seg_v.at[pl.ds(0, share - 1)], seg_send.at[0])
    for save in (save_tok, save_proj, save_attn, save_hid, save_two):
        save.wait()
    settle(act_v, act_sem.at[0])
    settle(der_v, act_sem.at[1])


def forward(plan, tokens_in, cotangent, segment_ids, biases, weights, vectors):
    n, share = plan.mp, plan.share
    width = tokens_in.shape[2]
    held, every = plan.own * plan.seq + plan.part, plan.rows * plan.seq
    any_space = pl.BlockSpec(memory_space=pl.ANY)
    in_vmem = pl.BlockSpec(memory_space=pltpu.VMEM)
    dma = pltpu.SemaphoreType.DMA
    rows = ((plan.rows, plan.seq, width), BF)
    heads = weights[1].shape[0] // HEAD_DIM
    local, three, ff = weights[1].shape[0], weights[0].shape[1], weights[2].shape[1]
    full = [((n,) + w.shape, BF) for w in weights]
    proj, attn = ((n, every, three), BF), ((n, held, local), BF)
    hid, two = ((held, width), F32), ((held, width), BF)
    act, der = ((n, held, ff), BF), ((n, held, ff), F32)
    outs = [rows, rows, ((plan.rows, plan.seq), jnp.int32), *full, proj, attn, hid, two, act, der]
    return pl.pallas_call(
        functools.partial(forward_kernel, plan, heads),
        out_shape=[jax.ShapeDtypeStruct(*o) for o in outs],
        in_specs=[any_space] * 9 + [in_vmem] * 5,
        out_specs=[any_space] * 2 + [in_vmem] + [any_space] * 10,
        scratch_shapes=[
            pltpu.VMEM(*rows), pltpu.VMEM((every, width), BF), pltpu.VMEM(*full[0]), pltpu.VMEM(*proj),
            pltpu.VMEM(*attn), pltpu.VMEM(*full[1]), pltpu.VMEM(*hid), pltpu.VMEM(*two), pltpu.VMEM(*full[2]),
            pltpu.VMEM(*act), pltpu.VMEM(*der), pltpu.VMEM((share,) + segment_ids.shape, jnp.int32),
            pltpu.VMEM((plan.rows, plan.seq, 128), F32),
            *[pltpu.VMEM((n,) + b.shape, F32) for b in biases],
            dma((plan.groups, share, 2)), dma((2,)), dma((plan.groups, share, 2)), dma((2,)), dma((1,)), dma((1,)),
            dma((2,)), dma((2,)), dma((1,)), dma((1,)), dma((1,)), dma((5,)), dma((2,)), *gatherer_sems(plan, 4),
        ],
        compiler_params=pltpu.CompilerParams(
            collective_id=0, has_side_effects=True, vmem_limit_bytes=58 << 20
        ),
        name="forward",
    )(tokens_in, cotangent, segment_ids, *biases, *weights, *vectors)


class Reducer:
    def __init__(self, plan, at, stage, loc, sbl, yrc, slot, wide, fin, grp, out, sems):
        self.plan, self.at, self.stage, self.wide = plan, at, stage, wide
        self.loc, self.sbl, self.yrc, self.slot, self.fin, self.grp, self.out = loc, sbl, yrc, slot, fin, grp, out
        (
            self.sib_send, self.sib_recv, self.y_send, self.y_recv, self.ring_send, self.ring_recv,
            self.grp_send, self.grp_recv, self.fin_send, self.fin_recv, self.out_sem, self.credit,
        ) = sems
        hops = plan.hops
        self.order = [(0, hops)] + [(way, dist) for dist in range(hops - 1, 0, -1) for way in range(2)] + [(0, 0)]

    def target(self, i):
        n, hops = self.plan.mp, self.plan.hops
        dist = hops - lax.div(i + 1, 2)
        up = jnp.where(i == 0, 1, lax.rem(i, 2))
        return self.plan.ring_at(self.at.p + dist * up + (n - dist) * (1 - up))

    def give(self, u, yy, i):
        at, t = self.at, self.target(i)
        src = self.stage[u].at[2 * yy + 1 - at.core]
        return remote(src, self.sbl[u].at[yy, t], self.sib_send.at[u], self.sib_recv.at[u, i, yy], dp=at.sib)

    def begin(self, u, i):
        at, t = self.at, self.target(i)
        rows = self.stage[u].shape[1]
        for yy in range(2):
            self.give(u, yy, i).start()
        size = 32 if rows % 32 == 0 else rows
        for yy in range(2):

            @pl.loop(0, rows // size)
            def _(b):
                inner = pl.ds(pl.multiple_of(b * size, size), size)
                self.loc[u][yy, t, inner] = self.stage[u][2 * yy + at.core, inner]

    def given(self, u):
        settle(self.stage[u].at[pl.ds(0, 2)], self.sib_send.at[u])

    def clear(self, u):
        for way in range(2):
            part = half_of(self.slot[u].at[way, 0], 1 - way)
            part[...] = jnp.zeros(part.shape, BF)

    def wide_clear(self):
        for way in range(2):
            for yy in range(2):
                part = half_of(self.wide.at[way, 0, yy], 1 - way)
                part[...] = jnp.zeros(part.shape, BF)

    def add(self, u, yy, t, extra, put):
        rows = self.loc[u].shape[2]
        size = 32 if rows % 32 == 0 else rows

        def block(b):
            inner = pl.ds(pl.multiple_of(b * size, size), size)
            total = self.loc[u][yy, t, inner].astype(F32) + self.sbl[u][yy, t, inner].astype(F32)
            for ref in extra:
                total = total + ref[inner].astype(F32)
            put(inner, total)

        pl.loop(0, rows // size)(block)

    def cross(self, u, i):
        at, t = self.at, self.target(i)
        return remote(self.loc[u].at[1 - at.y, t], self.yrc[u].at[t], self.y_send.at[u], self.y_recv.at[u, i], dp=at.other)

    def first(self, u, i):
        at, t = self.at, self.target(i)
        self.give(u, 1 - at.y, i).wait_recv()

        def put(inner, total):
            self.loc[u][1 - at.y, t, inner] = total.astype(BF)

        self.add(u, 1 - at.y, t, (), put)
        self.cross(u, i).start()

    def hop(self, u, way, s, t):
        src = self.loc[u].at[self.at.y, t]
        dst = self.slot[u].at[way, s]
        if s == 0:
            src, dst = half_of(src, way), half_of(dst, way)
        return remote(
            src, dst, self.ring_send.at[u, way], self.ring_recv.at[u, way, s], mp=self.at.neighbour[way]
        )

    def step(self, u, i):
        at, t = self.at, self.target(i)
        way, dist = self.order[i]
        s = self.plan.hops - dist
        self.give(u, at.y, i).wait_recv()
        self.cross(u, i).wait_recv()
        extra = [self.yrc[u].at[t]]
        ways = (0, 1) if dist in (0, self.plan.hops) else (way,)
        if s > 0:
            for v in ways:
                self.hop(u, v, s - 1, t).wait_recv()
                extra.append(self.slot[u].at[v, s - 1])
        rows = self.loc[u].shape[2]
        quads = self.plan.dp // 4

        def put(inner, total):
            if dist:
                self.loc[u][at.y, t, inner] = total.astype(BF)
            elif quads > 1:
                self.grp[u][lax.div(at.d, 4), inner] = total.astype(BF)
            else:
                to = pl.ds(pl.multiple_of(at.quarter * rows + inner.start, inner.size), inner.size)
                self.fin[u][to] = total.astype(BF)

        self.add(u, at.y, t, extra, put)
        if dist:
            for v in ways:
                self.hop(u, v, s, t).start()
        else:
            for other in range(1, quads):
                self.between(u, other).start()

    def wide_hop(self, u, way, s, t):
        src, dst = self.loc[u].at[:, t], self.wide.at[way, s]
        if s == 0:
            half = self.wide.shape[-1] // 2
            src, dst = (ref.at[:, :, pl.ds(way * half, half)] for ref in (src, dst))
        return remote(
            src, dst, self.ring_send.at[u, way], self.ring_recv.at[u, way, s], mp=self.at.neighbour[way]
        )

    def wide_cross(self, u):
        mine, theirs = self.yrc[u].at[pl.ds(2, 2)], self.yrc[u].at[pl.ds(0, 2)]
        return remote(mine, theirs, self.y_send.at[u], self.y_recv.at[u, 0], dp=self.at.other)

    def wide_step(self, u, i):
        at, t = self.at, self.target(i)
        way, dist = self.order[i]
        s = self.plan.hops - dist
        ways = (0, 1) if dist in (0, self.plan.hops) else (way,)
        for yy in range(2):
            self.give(u, yy, i).wait_recv()
        if s > 0:
            for v in ways:
                self.wide_hop(u, v, s - 1, t).wait_recv()
        for yy in range(2):
            extra = [self.wide.at[v, s - 1, yy] for v in ways] if s > 0 else []

            def put(inner, total):
                if dist:
                    self.loc[u][yy, t, inner] = total.astype(BF)
                else:
                    self.yrc[u][2 + yy, inner] = total.astype(BF)

            self.add(u, yy, t, extra, put)
        if dist:
            for v in ways:
                self.wide_hop(u, v, s, t).start()
        else:
            self.wide_cross(u).start()

    def wide_last(self, u):
        at, quads = self.at, self.plan.dp // 4
        rows = self.loc[u].shape[2]
        self.wide_cross(u).wait_recv()
        for yy in range(2):
            to = pl.ds(pl.multiple_of((2 * yy + at.core) * rows, rows), rows)
            total = self.yrc[u][yy].astype(F32) + self.yrc[u][2 + yy].astype(F32)
            if quads > 1:
                self.grp[u][lax.div(at.d, 4), yy] = total.astype(BF)
            else:
                self.fin[u][to] = total.astype(BF)
        if quads > 1:
            for other in range(1, quads):
                self.between(u, other).start()
            settle(self.grp[u].at[pl.ds(0, quads - 1)], self.grp_recv.at[u])
            for yy in range(2):
                to = pl.ds(pl.multiple_of((2 * yy + at.core) * rows, rows), rows)
                total = self.grp[u][0, yy].astype(F32)
                for other in range(1, quads):
                    total = total + self.grp[u][other, yy].astype(F32)
                self.fin[u][to] = total.astype(BF)
        for what in range(2):
            self.wide_out(u, what).start()

    def wide_out(self, u, what):
        block = piece(self.fin[u], 2 * what + self.at.core)
        return remote(block, block, self.fin_send.at[u, what], self.fin_recv.at[u, what], dp=self.at.sib)

    def wide_sent(self, u):
        hops = self.plan.hops
        settle(self.yrc[u].at[pl.ds(0, 2)], self.y_send.at[u])
        for way in range(2):
            settle(self.wide.at[way, pl.ds(0, hops - 1)], self.ring_send.at[u, way])
            half = self.wide.shape[-1] // 2
            settle(self.wide.at[way, 0, :, :, pl.ds(0, half)], self.ring_send.at[u, way])

    def between(self, u, other):
        at = self.at
        to = lax.rem(at.d + 4 * other, self.plan.dp)
        block = self.grp[u].at[lax.div(at.d, 4)]
        return remote(block, block, self.grp_send.at[u], self.grp_recv.at[u], dp=to)

    def share_out(self, u, what):
        at = self.at
        quarter = at.quarter if what != 1 else 2 - 2 * at.y + at.core
        block = piece(self.fin[u], quarter)
        to = at.other if what == 2 else at.sib
        return remote(block, block, self.fin_send.at[u, what], self.fin_recv.at[u, what], dp=to)

    def last(self, u):
        quads = self.plan.dp // 4
        if quads > 1:
            rows = self.loc[u].shape[2]
            settle(self.grp[u].at[pl.ds(0, quads - 1)], self.grp_recv.at[u])
            total = self.grp[u][0].astype(F32)
            for other in range(1, quads):
                total = total + self.grp[u][other].astype(F32)
            self.fin[u][pl.ds(pl.multiple_of(self.at.quarter * rows, rows), rows)] = total.astype(BF)
        self.share_out(u, 2).start()
        self.share_out(u, 0).start()

    def spread(self, u):
        self.share_out(u, 2).wait_recv()
        self.share_out(u, 1).start()

    def write(self, u, dst, wide=False):
        for what in range(2):
            (self.wide_out if wide else self.share_out)(u, what).wait_recv()
        rows = self.loc[u].shape[2]

        @pl.loop(0, 4)
        def _(q):
            at = pl.ds(pl.multiple_of(q * rows, rows), rows)
            slot = lax.rem(q, 2)

            @pl.when(q > 1)
            def _():
                settle(self.out.at[slot], self.out_sem.at[slot])

            self.out[slot] = self.fin[u][at].astype(F32)
            begun = 0
            for ref in dst:
                size = ref.shape[0] // 4
                pltpu.make_async_copy(
                    self.out.at[slot, pl.ds(begun, size)],
                    ref.at[pl.ds(pl.multiple_of(q * size, size), size)],
                    self.out_sem.at[slot],
                ).start()
                begun += size

        for slot in range(2):
            settle(self.out.at[slot], self.out_sem.at[slot])

    def sent(self, u):
        hops = self.plan.hops
        settle(self.loc[u].at[0], self.y_send.at[u])
        for way in range(2):
            settle(self.slot[u].at[way, pl.ds(0, hops - 1)], self.ring_send.at[u, way])
            settle(half_of(self.slot[u].at[way, 0], way), self.ring_send.at[u, way])

    def release(self, u):
        at = self.at
        self.sent(u)
        for to in ({"dp": at.sib}, {"dp": at.other}, {"mp": at.neighbour[0]}, {"mp": at.neighbour[1]}):
            pl.semaphore_signal(self.credit, inc=1, device_id=to, device_id_type=MESH)

    def claim(self):
        pl.semaphore_wait(self.credit, 4)

    def finish(self, u, wide=False):
        for what in range(2 if wide else 3):
            (self.wide_out if wide else self.share_out)(u, what).wait_send()
        for other in range(1, self.plan.dp // 4):
            self.between(u, other).wait_send()


class RowsOut:
    def __init__(self, plan, at, src, shared, dst, send, recv):
        self.plan, self.at, self.src, self.shared, self.dst, self.send, self.recv = plan, at, src, shared, dst, send, recv
        self.home = at.base + lax.div(at.m, plan.groups)
        self.first = lax.rem(at.m, plan.groups) * plan.group_rows

    def copies(self, what):
        plan, at = self.plan, self.at
        for q in range(plan.mp):
            here = jnp.logical_and(self.home == at.d, at.m == q)
            toks = pl.ds(q * plan.tok, plan.tok)
            if what == 0:
                yield q, here, True, self.src.at[pl.ds(0, plan.own), toks], self.dst.at[
                    pl.ds(self.first + plan.own * at.k, plan.own)
                ]
            else:
                holds = at.k == (q * plan.tok) // plan.part
                yield q, here, holds, self.shared.at[pl.ds((q * plan.tok) % plan.part, plan.tok)], self.dst.at[
                    self.first + plan.own * plan.share
                ]

    def start(self, what, only=None):
        for q, here, wanted, src, dst in self.copies(what):
            if only is not None and only != q:
                continue

            @pl.when(jnp.logical_and(here, wanted))
            def _():
                pltpu.make_async_copy(src, dst, self.recv.at[0]).start()

            @pl.when(jnp.logical_and(jnp.logical_not(here), wanted))
            def _():
                remote(src, dst, self.send.at[q, what], self.recv.at[0], dp=self.home, mp=q).start()

    def finish(self):
        settle(self.dst, self.recv.at[0])
        for what in range(2):
            for q, here, wanted, src, dst in self.copies(what):

                @pl.when(jnp.logical_and(jnp.logical_not(here), wanted))
                def _():
                    settle(src, self.send.at[q, what])


def backward_kernel(
    plan, heads, g0, g1, g2, g3, tok, cot, seg, proj, attn, hid, two, act, der, gain_one, shift_one, gain_two, down_bias,
    blk, tg, o0, o1, o2, o3, vout, *rest,
):
    n, share, own, part, seq = plan.mp, plan.share, plan.own, plan.part, plan.seq
    hops = plan.hops
    held, every = own * seq + part, plan.rows * seq
    width, ff, three, local = hid.shape[1], act.shape[2], proj.shape[2], attn.shape[2]
    (
        stage_a, stage_b, loc_a, loc_b, sbl_a, sbl_b, yrc_a, yrc_b, slot_b, wide_v, fin_a, fin_b, fin_c,
        grp_a, grp_b, grp_c, out_v,
    ) = rest[:17]
    sems, rest = rest[17:29], rest[29:]
    (
        grad_v, low_v, block_v, tgs, tgo, sums, ups, qbs, msg, vrc, vsum,
        load_sem, wgt_sem, blk_send, blk_recv, tg_send, tg_recv, tgs_send, tgs_recv, tgl_sem, v_send, v_recv,
    ) = rest
    at = Place(plan)
    red = Reducer(
        plan, at, (stage_a, stage_b, stage_b), (loc_a, loc_b, loc_b), (sbl_a, sbl_b, sbl_b), (yrc_a, yrc_b, yrc_b),
        (None, slot_b, slot_b), wide_v, (fin_a, fin_b, fin_c), (grp_a, grp_b, grp_c), out_v, sems,
    )
    blocks = RowsOut(plan, at, block_v, block_v.at[own], blk, blk_send, blk_recv)
    greet(plan, at, True)
    part_of = functools.partial
    count = len(red.order)
    first = [[part_of(red.first, u, i) for i in range(count)] for u in range(3)]
    step = [[part_of(red.step, u, i) for i in range(count)] for u in range(3)]
    wide = [part_of(red.wide_step, 0, i) for i in range(count)]
    when_wide = [WIDE_FIRST + i * WIDE_PACE // 4 for i in range(count)]
    red.wide_clear()
    red.clear(1)
    sums[...] = jnp.zeros(sums.shape, F32)
    blocks_held = own * share + 1

    def stream(loads, i):
        def copies(j, slot):
            t = red.target(j)
            for what, (src, dst) in enumerate(loads):
                yield pltpu.make_async_copy(src.at[t], dst.at[slot], wgt_sem.at[what, slot])

        if isinstance(i, int):
            for copy in copies(i, i % 2):
                copy.start()
            return

        @pl.when(i + 1 < n)
        def _():
            for copy in copies(i + 1, lax.rem(i + 1, 2)):
                copy.start()

        for copy in copies(i, lax.rem(i, 2)):
            copy.wait()

    def feed_forward(wd_v, wu_v, act_v, der_v, low_pre, two_v, cot_v, hid_v, sum_v):
        loads = ((g3, wd_v), (g2, wu_v), (act, act_v), (der, der_v))
        stream(loads, 0)
        small = [pltpu.make_async_copy(two, two_v, load_sem.at[0]), pltpu.make_async_copy(hid, hid_v, load_sem.at[1])]
        for r in range(plan.rows):
            extent = seq if r < own else part
            small.append(
                pltpu.make_async_copy(
                    cot.at[r, pl.ds(0, extent)], cot_v.at[pl.ds(r * seq, extent)], load_sem.at[2 + r]
                )
            )
        for copy in small:
            copy.start()
        for copy in small:
            copy.wait()

        @pl.loop(0, blocks_held)
        def _(b):
            rows = pl.ds(pl.multiple_of(b * part, part), part)
            sum_v[rows] = hid_v[rows] + down_bias[...]
            grad_v[rows] = jnp.zeros((part, width), F32)

        meet(plan, True)

        def body(i, take):
            take(0)
            stream(loads, i)
            slot = lax.rem(i, 2)
            rows = ff // 4

            @pl.when(i > 0)
            def _():
                red.given(0)
                red.given(1)

            for q in range(4):
                lhs = act_v[slot, :, q * rows : (q + 1) * rows]
                stage_a[q] = lax.dot_general(lhs, cot_v[...], DOWN, preferred_element_type=F32).astype(BF)
            red.begin(0, i)
            take(1)

            act_grad = lax.dot_general(cot_v[...], wd_v[slot], ACROSS, preferred_element_type=F32)
            low = (act_grad * der_v[slot]).astype(BF)
            low_pre[...] = low
            ups[red.target(i)] = jnp.sum(low.astype(F32), axis=0, keepdims=True)
            for q in range(4):
                lhs = low_pre[:, q * rows : (q + 1) * rows]
                stage_b[q] = lax.dot_general(lhs, two_v[...], DOWN, preferred_element_type=F32).astype(BF)
            red.begin(1, i)
            grad_v[...] += lax.dot_general(low_pre[...], wu_v[slot], ACROSS, preferred_element_type=F32)
            sum_v[...] += jnp.dot(act_v[slot], wd_v[slot], preferred_element_type=F32)

        table, middle = {}, {}
        for i in range(count - 1):
            table.setdefault(i + 1, []).append(first[1][i])
        for i in range(count):
            if when_wide[i] < n:
                middle.setdefault(when_wide[i], []).append(wide[i])
        for i in range(count - 2):
            table.setdefault(i + 2, []).append(step[1][i])
        run(n, body, table, middle)
        red.given(0)
        red.given(1)
        first[1][count - 1]()
        step[1][count - 2]()

        @pl.loop(0, blocks_held)
        def _(b):
            r, start = lax.div(b, share), pl.multiple_of(lax.rem(b, share) * part, part)
            rows = pl.ds(pl.multiple_of(b * part, part), part)
            block_v[r, pl.ds(start, part)] = sum_v[rows].astype(BF)
            hidden, grad, cot_f = hid_v[rows], grad_v[rows], cot_v[rows].astype(F32)
            unit, scale, _ = norm(hidden, gain_two[...], 0.0)
            hidden_grad = cot_f + norm_back(unit, scale, gain_two[...], grad)
            grad_v[rows] = hidden_grad
            low_v[rows] = hidden_grad.astype(BF)
            for line, value in ((2, hidden_grad), (3, grad * unit), (4, grad), (5, cot_f)):
                sums[pl.ds(line, 1)] += jnp.sum(value, axis=0, keepdims=True)

        for q in range(n):
            if q < BLOCKS_MID:
                blocks.start(0, q)
                blocks.start(1, q)

    pl.run_scoped(
        feed_forward,
        pltpu.VMEM((2,) + g3.shape[1:], BF), pltpu.VMEM((2,) + g2.shape[1:], BF), pltpu.VMEM((2, held, ff), BF),
        pltpu.VMEM((2, held, ff), F32), pltpu.VMEM((held, ff), BF), pltpu.VMEM((held, width), BF),
        pltpu.VMEM((held, width), BF), pltpu.VMEM((held, width), F32), pltpu.VMEM((held, width), F32),
    )

    def attention(wq_v, wo_v, proj_v, attn_v, head_v, three_v, tok_v, one_v, back_v, out3, columns):
        loads = ((g0, wq_v), (g1, wo_v), (proj, proj_v), (attn, attn_v))
        stream(loads, 0)
        load = pltpu.make_async_copy(tok, tok_v, load_sem.at[0])
        load.start()
        step[1][count - 1]()
        red.last(1)
        red.release(1)
        load.wait()

        @pl.loop(0, plan.rows * share)
        def _(b):
            r, start = lax.div(b, share), pl.multiple_of(lax.rem(b, share) * part, part)
            rows = pl.ds(pl.multiple_of(b * part, part), part)
            values = tok_v[r, pl.ds(start, part)].astype(F32)
            one_v[rows] = norm_rows(values, gain_one[...], shift_one[...]).astype(BF)
            back_v[rows] = jnp.zeros((part, width), F32)

        three_v[...] = jnp.zeros(three_v.shape, BF)
        label_columns(seg, plan.rows, columns)
        red.spread(1)

        def body(i, take):
            take(0)
            stream(loads, i)
            slot = lax.rem(i, 2)

            head_v[...] = lax.dot_general(low_v[...], wo_v[slot], ACROSS, preferred_element_type=F32).astype(BF)

            def attend(r, first, amount):
                allowed = same_image(seg, columns, r, amount)
                keys, queries = pl.ds(pl.multiple_of(r * seq, seq), seq), pl.ds(first, amount)
                for h in range(heads):
                    col = h * 3 * HEAD_DIM
                    query = proj_v[slot, queries, col : col + HEAD_DIM]
                    key = proj_v[slot, keys, col + HEAD_DIM : col + 2 * HEAD_DIM]
                    value = proj_v[slot, keys, col + 2 * HEAD_DIM : col + 3 * HEAD_DIM]
                    head_grad = head_v[queries, h * HEAD_DIM : (h + 1) * HEAD_DIM]
                    full = probs_of(key, query, allowed)
                    value_grad = jnp.dot(full.astype(BF), head_grad, preferred_element_type=F32)
                    probs_grad = lax.dot_general(value, head_grad, ACROSS, preferred_element_type=F32)
                    delta = jnp.sum(probs_grad * full, axis=0, keepdims=True)
                    low = (jnp.where(allowed, full * (probs_grad - delta), 0.0) * HEAD_DIM ** (-0.5)).astype(BF)
                    query_grad = lax.dot_general(low, key, DOWN, preferred_element_type=F32)
                    key_grad = jnp.dot(low, query, preferred_element_type=F32)
                    three_v[queries, col : col + HEAD_DIM] = query_grad.astype(BF)
                    three_v[keys, col + HEAD_DIM : col + 2 * HEAD_DIM] = key_grad.astype(BF)
                    three_v[keys, col + 2 * HEAD_DIM : col + 3 * HEAD_DIM] = value_grad.astype(BF)

            for r in range(own):
                attend(r, r * seq, seq)
                take(1 + r)
            attend(own, own * seq, part)

            @pl.when(i > 0)
            def _():
                red.given(2)

            @pl.when(i == 0)
            def _():
                red.claim()

            wide, narrow = three // 4, local // 4
            weight = lax.dot_general(three_v[...], one_v[...], DOWN, preferred_element_type=F32).astype(BF)
            out_weight = lax.dot_general(attn_v[slot], low_v[...], DOWN, preferred_element_type=F32).astype(BF)
            for q in range(4):
                stage_b[q, :wide] = weight[q * wide : (q + 1) * wide]
                stage_b[q, wide:] = out_weight[q * narrow : (q + 1) * narrow]
            red.begin(2, i)

            back_v[...] += lax.dot_general(three_v[...], wq_v[slot], ACROSS, preferred_element_type=F32)
            qbs[red.target(i)] = jnp.sum(three_v[...].astype(F32), axis=0, keepdims=True)

        late = max(when_wide[-1] - n + 1, 1)
        table = {3: [part_of(red.write, 1, (o1,))]}
        table.setdefault(late, []).append(part_of(red.wide_last, 0))
        table.setdefault(min(late + 2, n - 1), []).append(part_of(red.write, 0, (o0,), True))
        for i in range(count):
            if when_wide[i] >= n:
                table.setdefault(when_wide[i] - n, []).insert(0, wide[i])
        for i in range(count - 1):
            table.setdefault(i + 1, []).insert(0, first[2][i])
        middle = {i + 2: [step[2][i]] for i in range(count - 2)}
        for q in range(BLOCKS_MID, n):
            for what in range(2):
                table.setdefault((q - BLOCKS_MID) * BLOCKS_OVER // n, []).append(part_of(blocks.start, what, q))
        run(n, body, table, *[{}] * (own - 1), middle)
        red.given(2)
        first[2][count - 1]()
        step[2][count - 2]()

        def norm_block(b):
            r, start = lax.div(b, share), pl.multiple_of(lax.rem(b, share) * part, part)
            rows = pl.ds(pl.multiple_of(b * part, part), part)
            unit, scale, _ = norm(tok_v[r, pl.ds(start, part)].astype(F32), gain_one[...], 0.0)
            grad = back_v[rows]
            for line, value in ((0, grad * unit), (1, grad)):
                sums[pl.ds(line, 1)] += jnp.sum(value, axis=0, keepdims=True)
            grad = norm_back(unit, scale, gain_one[...], grad)

            @pl.when(b < blocks_held)
            def _():
                mine = pl.ds(pl.multiple_of(jnp.minimum(b, blocks_held - 1) * part, part), part)
                out3[r, pl.ds(start, part)] = (grad + grad_v[mine]).astype(BF)

            @pl.when(b >= blocks_held)
            def _():
                out3[r, pl.ds(start, part)] = grad.astype(BF)

        pl.loop(own * share, plan.rows * share)(norm_block)

        tokens = RowsOut(plan, at, out3, tgo, tg, tg_send, tg_recv)
        for e in range(share):
            src = out3.at[own, pl.ds(e * part, part)]
            if e == 0:
                pltpu.make_async_copy(src, tgs.at[0], tgl_sem.at[0]).start()
            else:
                to = at.base + lax.rem(at.k + e, share)
                remote(src, tgs.at[share - e], tgs_send.at[e], tgs_recv.at[share - e], dp=to).start()

        pl.loop(0, own * share)(norm_block)

        lines = [-(-size // 128) for size in (ff, three)]
        msg[...] = jnp.zeros(msg.shape, F32)
        for q in range(n):
            msg[q, :8, : width // n] = sums[:, q * (width // n) : (q + 1) * (width // n)]
            line = 8
            for ref, size in ((ups, ff), (qbs, three)):
                for first_col in range(0, size, 128):
                    cols = min(128, size - first_col)
                    msg[q, line : line + 1, :cols] = ref[q, :, first_col : first_col + cols]
                    line += 1
        me = at.d * n + at.m

        def one(i, carry):
            to = lax.rem(me + i, plan.all)
            e, q = lax.div(to, n), lax.rem(to, n)
            remote(msg.at[q], vrc.at[me], v_send.at[0], v_recv.at[0], dp=e, mp=q).start()
            return carry

        lax.fori_loop(1, plan.all, one, 0)
        pltpu.make_async_copy(msg.at[at.m], vrc.at[me], v_recv.at[0]).start()
        tokens.start(0)
        for e in range(1, share):
            settle(tgs.at[e], tgs_recv.at[e])
        settle(tgs.at[0], tgl_sem.at[0])
        tgo[...] = sum(tgs[e].astype(F32) for e in range(share)).astype(BF)
        tokens.start(1)
        step[2][count - 1]()
        red.last(2)
        settle(vrc, v_recv.at[0])
        vsum[...] = jnp.sum(vrc[...], axis=0)
        for e in range(1, n):
            remote(vsum, vout.at[at.m], v_send.at[1], v_recv.at[1], mp=lax.rem(at.m + e, n)).start()
        pltpu.make_async_copy(vsum, vout.at[at.m], v_recv.at[1]).start()
        red.spread(2)
        red.write(2, (o2, o3))
        for u in range(3):
            red.finish(u, u == 0)
        red.wide_sent(0)
        red.sent(2)
        for e in range(1, share):
            settle(tgs.at[0], tgs_send.at[e])
        blocks.finish()
        tokens.finish()
        settle(vout, v_recv.at[1])
        settle(vrc.at[pl.ds(0, plan.all - 1)], v_send.at[0])
        settle(vout.at[pl.ds(0, n - 1)], v_send.at[1])

    pl.run_scoped(
        attention,
        pltpu.VMEM((2,) + g0.shape[1:], BF), pltpu.VMEM((2,) + g1.shape[1:], BF), pltpu.VMEM((2, every, three), BF),
        pltpu.VMEM((2, held, local), BF), pltpu.VMEM((held, local), BF), pltpu.VMEM((every, three), BF),
        pltpu.VMEM((plan.rows, seq, width), BF), pltpu.VMEM((every, width), BF), pltpu.VMEM((every, width), F32),
        pltpu.VMEM((plan.rows, seq, width), BF), pltpu.VMEM((plan.rows, seq, 128), F32),
    )


def backward(plan, weights, tok3, cot3, seg, proj, attn, hid, two, act, der, vectors):
    n, share = plan.mp, plan.share
    held, width = hid.shape
    ff, three, local = act.shape[2], proj.shape[2], attn.shape[2]
    heads = local // HEAD_DIM
    quads, quarter = plan.dp // 4, ff // 4
    if local + three != ff:
        raise ValueError("unsupported sizes")
    any_space = pl.BlockSpec(memory_space=pl.ANY)
    in_vmem = pl.BlockSpec(memory_space=pltpu.VMEM)
    dma = pltpu.SemaphoreType.DMA
    rows = jax.ShapeDtypeStruct((plan.rows_dev, plan.tok, width), BF)
    shard = jax.ShapeDtypeStruct((ff, width), F32)
    size = 8 + -(-ff // 128) + -(-three // 128)
    size = -(-size // 8) * 8
    vec = (size, 128)
    return pl.pallas_call(
        functools.partial(backward_kernel, plan, heads),
        out_shape=[
            rows, rows, shard, shard, jax.ShapeDtypeStruct((three, width), F32), jax.ShapeDtypeStruct((local, width), F32),
            jax.ShapeDtypeStruct((n,) + vec, F32),
        ],
        in_specs=[any_space] * 6 + [in_vmem] + [any_space] * 6 + [in_vmem] * 4,
        out_specs=[any_space] * 7,
        scratch_shapes=[
            *[pltpu.VMEM((4, quarter, width), BF)] * 2,
            *[pltpu.VMEM((2, n, quarter, width), BF)] * 4,
            pltpu.VMEM((4, quarter, width), BF),
            pltpu.VMEM((n, quarter, width), BF),
            pltpu.VMEM((2, plan.hops, quarter, width), BF),
            pltpu.VMEM((2, plan.hops, 2, quarter, width), BF),
            *[pltpu.VMEM((ff, width), BF)] * 3,
            pltpu.VMEM((quads, 2) + ((quarter, width) if quads > 1 else (8, 128)), BF),
            *[pltpu.VMEM((quads,) + ((quarter, width) if quads > 1 else (8, 128)), BF)] * 2,
            pltpu.VMEM((2, quarter, width), F32),
            dma((3,)), dma((3, n, 2)), dma((3,)), dma((3, n)), dma((3, 2)), dma((3, 2, plan.hops)), dma((3,)), dma((3,)),
            dma((3, 3)), dma((3, 3)), dma((2,)), pltpu.SemaphoreType.REGULAR,
            pltpu.VMEM((held, width), F32), pltpu.VMEM((held, width), BF), pltpu.VMEM((plan.rows, plan.seq, width), BF),
            pltpu.VMEM((share, plan.part, width), BF), pltpu.VMEM((plan.part, width), BF), pltpu.VMEM((8, width), F32),
            pltpu.VMEM((n, 1, ff), F32), pltpu.VMEM((n, 1, three), F32), pltpu.VMEM((n,) + vec, F32),
            pltpu.VMEM((plan.all,) + vec, F32), pltpu.VMEM(vec, F32),
            dma((2 + plan.rows,)), dma((4, 2)), dma((n, 2)), dma((1,)), dma((n, 2)), dma((1,)), dma((share,)),
            dma((share,)), dma((1,)), dma((2,)), dma((2,)),
        ],
        compiler_params=pltpu.CompilerParams(
            collective_id=1, has_side_effects=True, vmem_limit_bytes=61 << 20
        ),
        name="backward",
    )(*weights, tok3, cot3, seg, proj, attn, hid, two, act, der, *vectors)


def probs_of(key, query, allowed):
    raw = lax.dot_general(key, query, ACROSS, preferred_element_type=F32)
    scores = jnp.where(allowed, raw * HEAD_DIM ** (-0.5), MASKED)
    raised = jnp.exp(scores - jnp.max(scores, axis=0, keepdims=True))
    return raised * (1.0 / jnp.sum(raised, axis=0, keepdims=True))


def label_columns(labels, rows, columns):
    for r in range(rows):
        line = labels[pl.ds(r, 1)].astype(F32)
        columns[r] = jnp.transpose(jnp.broadcast_to(line, (128, line.shape[1])))


def same_image(labels, columns, r, amount):
    line = labels[pl.ds(r, 1)].astype(F32)[:, :amount]
    down = columns[r]
    if amount < 128:
        return down[:, :amount] == line
    return jnp.concatenate([down] * (amount // 128), axis=1) == line


def norm(values, gain_vec, shift_vec):
    centred = values - jnp.mean(values, axis=-1, keepdims=True)
    scale = lax.rsqrt(jnp.mean(centred * centred, axis=-1, keepdims=True) + EPS)
    unit = centred * scale
    return unit, scale, unit * gain_vec + shift_vec


def norm_back(unit, scale, gain_vec, grad):
    pulled = grad * gain_vec
    inner = jnp.mean(pulled * unit, axis=-1, keepdims=True)
    return scale * (pulled - jnp.mean(pulled, axis=-1, keepdims=True) - unit * inner)


def per_device(
    plan, tokens_in, segment_ids, attn_gain, attn_shift, qkv_weight, qkv_bias, out_weight, out_bias, mlp_gain, mlp_shift,
    up_weight, up_bias, down_weight, down_bias, cotangent,
):
    n, width = plan.mp, tokens_in.shape[2]
    ff_local = up_weight.shape[1]
    heads_local = qkv_bias.shape[1] // HEAD_DIM
    parts = qkv_bias.reshape(2, heads_local, HEAD_DIM)
    bias_three = jnp.stack([parts[0], jnp.zeros_like(parts[0]), parts[1]], axis=1).reshape(1, -1)
    vectors = [v.reshape(1, width) for v in (attn_gain, attn_shift, out_bias, mlp_gain, mlp_shift)]
    tok3, cot3, seg, wq, wo, wu, wd, proj, attn, hidden, normed_two, act_low, gelu_slope = forward(
        plan, tokens_in, cotangent, segment_ids, (bias_three, up_bias.reshape(1, ff_local)),
        (qkv_weight, out_weight, up_weight, down_weight), vectors,
    )
    block_out, tokens_low, down_grad, up_grad, qkv_grad, out_grad, sums = backward(
        plan, (wq, wo, wu, wd), tok3, cot3, seg, proj, attn, hidden, normed_two, act_low, gelu_slope,
        [v.reshape(1, width) for v in (attn_gain, attn_shift, mlp_gain, down_bias)],
    )
    local, three = out_weight.shape[0], qkv_weight.shape[1]
    six = jnp.swapaxes(sums[:, :6, : width // n], 0, 1).reshape(6, width)
    mine = lax.dynamic_index_in_dim(sums, lax.axis_index("mp"), 0, keepdims=False)
    lines = [-(-size // 128) for size in (ff_local, three)]
    up_bias_grad = mine[8 : 8 + lines[0]].reshape(-1)[:ff_local]
    bias_sums = mine[8 + lines[0] : 8 + sum(lines)].reshape(-1)[:three].reshape(heads_local, 3, HEAD_DIM)
    qkv_bias_grad = jnp.stack([bias_sums[:, 0], bias_sums[:, 2]]).reshape(2, local)
    return (
        block_out, tokens_low.astype(F32), six[0], six[1], qkv_grad.T, qkv_bias_grad, out_grad, six[2], six[3], six[4],
        up_grad.T, up_bias_grad, down_grad, six[5],
    )


def solution(mesh):
    dp, mp = mesh.shape["dp"], mesh.shape["mp"]
    rows_spec = P("dp", "mp", None)
    in_specs = (
        rows_spec, P("dp", None), P(), P(), P(None, "mp"), P(None, "mp"), P("mp", None), P(), P(), P(),
        P(None, "mp"), P("mp"), P("mp", None), P(), rows_spec,
    )
    out_specs = (
        rows_spec, rows_spec, P(), P(), P(None, "mp"), P(None, "mp"), P("mp", None), P(), P(), P(),
        P(None, "mp"), P("mp"), P("mp", None), P(),
    )

    def run(tokens_in, segment_ids, *rest):
        rows_all, seq_len, _ = tokens_in.shape
        plan = Plan(dp, mp, rows_all // dp, seq_len // mp, seq_len)
        return jax.shard_map(
            functools.partial(per_device, plan), mesh=mesh, in_specs=in_specs, out_specs=out_specs, check_vma=False
        )(tokens_in, segment_ids, *rest)

    return run
```

```python
import functools
import itertools
import math

import jax
import jax.numpy as jnp
from jax import lax
from jax.experimental import pallas as pl
from jax.experimental.pallas import tpu as pltpu
from jax.sharding import PartitionSpec as P

HEAD_DIM = 64
EPS = 1e-06
MASKED = -1000000000.0
MESH = pl.DeviceIdType.MESH
BF = jnp.bfloat16
F32 = jnp.float32
ACROSS = (((1,), (1,)), ((), ()))
DOWN = (((0,), (0,)), ((), ()))


WIDE_FIRST, WIDE_PACE = 1, 4
BLOCKS_MID, BLOCKS_OVER = 8, 4


class Plan:
    def __init__(self, dp, mp, rows_dev, tok_local, seq_len):
        self.dp, self.mp, self.rows_dev, self.tok, self.seq = dp, mp, rows_dev, tok_local, seq_len
        self.share = mp // math.gcd(rows_dev, mp)
        self.group_rows = rows_dev * self.share // mp
        self.own = self.group_rows // self.share
        if self.share % 2 or dp % self.share or dp % 4 or self.group_rows != self.own * self.share + 1:
            raise ValueError("unsupported sizes")
        self.groups = mp // self.share
        self.part = seq_len // self.share
        self.rows = self.own + 1
        self.hops = mp // 2
        self.all = dp * mp

    def ring_at(self, p):
        p = lax.rem(p, self.mp)
        back = lax.div(p, self.mp // 2)
        return 2 * p * (1 - back) + (2 * self.mp - 1 - 2 * p) * back


class Place:
    def __init__(self, plan):
        d, m = lax.axis_index("dp"), lax.axis_index("mp")
        odd = lax.rem(m, 2)
        self.d, self.m = d, m
        self.p = lax.div(m, 2) * (1 - odd) + (plan.mp - 1 - lax.div(m, 2)) * odd
        self.core = lax.rem(d, 2)
        self.sib = d + 1 - 2 * self.core
        self.y = lax.rem(lax.div(d, 2), 2)
        self.other = d + 2 - 4 * self.y
        self.k = lax.rem(d, plan.share)
        self.base = d - self.k
        self.quarter = 2 * self.y + self.core
        self.neighbour = (plan.ring_at(self.p + 1), plan.ring_at(self.p + plan.mp - 1))

    def away(self, plan, way, s):
        return plan.ring_at(self.p + plan.mp - s if way == 0 else self.p + s)


def greet(plan, at, everyone):
    barrier = pltpu.get_barrier_semaphore()
    span = plan.dp if everyone else max(plan.share, 4)
    base = lax.div(at.d, span) * span

    def one(i, carry):
        e, q = base + lax.div(i, plan.mp), lax.rem(i, plan.mp)

        @pl.when(jnp.logical_or(e != at.d, q != at.m))
        def _():
            pl.semaphore_signal(barrier, inc=1, device_id={"dp": e, "mp": q}, device_id_type=MESH)

        return carry

    lax.fori_loop(0, span * plan.mp, one, 0)


def meet(plan, everyone):
    span = plan.dp if everyone else max(plan.share, 4)
    pl.semaphore_wait(pltpu.get_barrier_semaphore(), span * plan.mp - 1)


def remote(src, dst, send, recv, **to):
    return pltpu.make_async_remote_copy(src, dst, send, recv, device_id=to, device_id_type=MESH)


def settle(ref, sem):
    pltpu.make_async_copy(ref, ref, sem).wait()


def piece(ref, quarter, half=None):
    rows, cols = ref.shape[0] // 4, ref.shape[1]
    first = quarter * rows
    if half is None:
        return ref.at[pl.ds(pl.multiple_of(first, rows), rows)]
    if cols % 256 == 0:
        return ref.at[pl.ds(pl.multiple_of(first, rows), rows), pl.ds(half * (cols // 2), cols // 2)]
    return ref.at[pl.ds(pl.multiple_of(first + half * (rows // 2), rows // 2), rows // 2)]


def half_of(ref, half):
    rows, cols = ref.shape
    if cols % 256 == 0:
        return ref.at[:, pl.ds(half * (cols // 2), cols // 2)]
    return ref.at[pl.ds(half * (rows // 2), rows // 2)]


class Gatherer:
    def __init__(self, plan, at, shards, full, sems):
        self.plan, self.at, self.shards, self.full = plan, at, shards, full
        self.own_sem, self.ring_send, self.ring_recv, self.y_send, self.y_recv, self.sib_send, self.sib_recv = sems

    def _half(self, way, s):
        return way if s == self.plan.hops - 1 else None

    def ring(self, w, way, s):
        at, origin = self.at, self.at.away(self.plan, way, s)
        half = self._half(way, s)
        dst = piece(self.full[w].at[origin], at.quarter, half)
        src = piece(self.shards[w], at.quarter, half) if s == 0 else dst
        return remote(src, dst, self.ring_send.at[w, way], self.ring_recv.at[w, way, s], mp=at.neighbour[way])

    def cross(self, w, way, s):
        at, origin = self.at, self.at.away(self.plan, way, s + 1)
        block = piece(self.full[w].at[origin], at.quarter, self._half(way, s))
        return remote(block, block, self.y_send.at[w], self.y_recv.at[w, way, s], dp=at.other)

    def give(self, w, way, s, mine):
        at, origin = self.at, self.at.away(self.plan, way, s + 1)
        quarter = at.quarter if mine else 2 - 2 * at.y + at.core
        block = piece(self.full[w].at[origin], quarter, self._half(way, s))
        return remote(block, block, self.sib_send.at[w], self.sib_recv.at[w], dp=at.sib)

    def begin(self, w):
        for way in range(2):
            self.ring(w, way, 0).start()
        pltpu.make_async_copy(self.shards[w], self.full[w].at[self.at.m], self.own_sem.at[w]).start()

    def step(self, w, s):
        for way in range(2):
            self.ring(w, way, s).wait_recv()
            if s < self.plan.hops - 1:
                self.ring(w, way, s + 1).start()
            self.cross(w, way, s).start()
            self.give(w, way, s, True).start()

    def follow(self, w, s):
        for way in range(2):
            self.cross(w, way, s).wait_recv()
            self.give(w, way, s, False).start()

    def arrived(self, w):
        n, rows = self.plan.mp, self.shards[w].shape[0]
        settle(self.full[w].at[pl.ds(0, n - 1), pl.ds(0, rows // 2)], self.sib_recv.at[w])
        settle(self.shards[w], self.own_sem.at[w])

    def finish(self, w):
        n, rows = self.plan.mp, self.shards[w].shape[0]
        settle(self.full[w].at[pl.ds(0, n - 1), pl.ds(0, rows // 2)], self.sib_send.at[w])
        settle(self.full[w].at[pl.ds(0, n - 1), pl.ds(0, rows // 4)], self.y_send.at[w])
        for way in range(2):
            settle(self.full[w].at[pl.ds(0, self.plan.hops - 1), pl.ds(0, rows // 4)], self.ring_send.at[w, way])
            settle(piece(self.full[w].at[0], 0, way), self.ring_send.at[w, way])


def gatherer_sems(plan, count):
    dma = pltpu.SemaphoreType.DMA
    return [
        dma((count,)), dma((count, 2)), dma((count, 2, plan.hops)), dma((count,)), dma((count, 2, plan.hops)),
        dma((count,)), dma((count,)),
    ]


class RowsIn:
    def __init__(self, plan, at, src, dst, send, recv):
        self.plan, self.at, self.src, self.dst, self.send, self.recv = plan, at, src, dst, send, recv

    def copies(self):
        plan, at = self.plan, self.at
        mine = pl.ds(pl.multiple_of(at.m * plan.tok, plan.tok), plan.tok)
        for j in range(plan.groups):
            q = at.k * plan.groups + j
            first = j * plan.group_rows
            for e in range(plan.share):
                here = jnp.logical_and(at.k == e, at.m == q)
                holds = lax.div(at.m * plan.tok, plan.part) == e
                to = lax.rem(at.m * plan.tok + plan.seq - e * plan.part, plan.seq)
                to = pl.ds(pl.multiple_of(to, plan.tok), plan.tok)
                yield here, True, q, e, j, 0, self.src.at[pl.ds(first + plan.own * e, plan.own)], self.dst.at[
                    pl.ds(0, plan.own), mine
                ]
                yield here, holds, q, e, j, 1, self.src.at[first + plan.own * plan.share], self.dst.at[plan.own, to]

    def start(self, only=None):
        for here, wanted, q, e, j, what, src, dst in self.copies():
            if only is not None and only != j:
                continue

            @pl.when(jnp.logical_and(here, wanted))
            def _():
                pltpu.make_async_copy(src, dst, self.recv.at[what]).start()

            @pl.when(jnp.logical_and(jnp.logical_not(here), wanted))
            def _():
                remote(src, dst, self.send.at[j, e, what], self.recv.at[what], dp=self.at.base + e, mp=q).start()

    def arrived(self):
        plan = self.plan
        settle(self.dst.at[pl.ds(0, plan.own)], self.recv.at[0])
        settle(self.dst.at[plan.own, pl.ds(0, plan.part)], self.recv.at[1])

    def finish(self):
        for here, wanted, q, e, j, what, src, dst in self.copies():

            @pl.when(jnp.logical_and(jnp.logical_not(here), wanted))
            def _():
                settle(src, self.send.at[j, e, what])


def run(count, body, *tables):
    def one(j, carry):
        def take(k):
            for when, thunks in sorted(tables[k].items()):

                @pl.when(j == when)
                def _():
                    for thunk in thunks:
                        thunk()

        body(j, take)
        return carry

    lax.fori_loop(0, count, one, 0)


def spread_over(count, thunks, first=0):
    table = {}
    for i, thunk in enumerate(thunks):
        table.setdefault(first + i * (count - first) // len(thunks), []).append(thunk)
    return table


def norm_rows(values, gain_vec, shift_vec):
    unit, _, normed = norm(values, gain_vec, shift_vec)
    return normed


def forward_kernel(
    plan, heads, tok, cot, seg, bq, bu, w0, w1, w2, w3, gain_one, shift_one, out_bias, gain_two, shift_two,
    tok_o, cot3, seg_o, g0, g1, g2, g3, proj_o, attn_o, hid_o, two_o, act_o, der_o,
    tok_v, one_v, wq_v, proj_v, attn_v, wo_v, hid_v, two_v, wu_v, act_v, der_v, seg_v, columns, bq_v, bu_v,
    tok_send, tok_recv, cot_send, cot_recv, seg_send, seg_recv, bias_send, bias_recv, part_send, part_recv, load_sem, save_sem, act_sem, *sems,
):
    n, share, own, part, seq = plan.mp, plan.share, plan.own, plan.part, plan.seq
    held = own * seq + part
    at = Place(plan)
    gat = Gatherer(plan, at, (w0, w1, w2, w3), (g0, g1, g2, g3), sems)
    tokens = RowsIn(plan, at, tok, tok_v, tok_send, tok_recv)
    cots = RowsIn(plan, at, cot, cot3, cot_send, cot_recv)
    hops = plan.hops
    greet(plan, at, False)
    meet(plan, False)

    gat.begin(0)
    gat.begin(2)
    tokens.start(0)
    biases = ((bq, bq_v, 0), (bu, bu_v, 1))
    for src, dst, i in biases:
        pltpu.make_async_copy(src, dst.at[at.m], bias_recv.at[i]).start()
        for s in range(1, n):
            remote(src, dst.at[at.m], bias_send.at[i], bias_recv.at[i], mp=lax.rem(at.m + s, n)).start()
    pltpu.make_async_copy(seg, seg_v.at[at.k], seg_recv.at[0]).start()
    for e in range(1, share):
        remote(seg, seg_v.at[at.k], seg_send.at[0], seg_recv.at[0], dp=at.base + lax.rem(at.k + e, share)).start()
    part_of = functools.partial
    hop = [[part_of(gat.step, w, s) for s in range(hops)] for w in range(4)]
    after = [[part_of(gat.follow, w, s) for s in range(hops)] for w in range(4)]
    begin = [part_of(gat.begin, w) for w in range(4)]
    token = [part_of(tokens.start, j) for j in range(plan.groups)]
    between = {0: [begin[3], hop[2][0]] + token[1:2], 1: token[2:3] + [hop[2][1], after[2][0]], 2: token[3:] + [hop[3][0]]}
    between[hops - 1] = between.get(hops - 1, []) + [hop[2][2], after[2][1], begin[1]]
    for s in range(hops):
        hop[0][s]()
        if s:
            after[0][s - 1]()
        for thunk in between.get(s, []):
            thunk()
    after[0][hops - 1]()
    tokens.arrived()
    mine = tok_v.at[own, pl.ds(0, part)]
    for e in range(1, share):
        remote(
            mine, tok_v.at[own, pl.ds((share - e) * part, part)], part_send.at[0], part_recv.at[0],
            dp=at.base + lax.rem(at.k + e, share),
        ).start()
    others = tok_v.at[own, pl.ds(part, (share - 1) * part)]
    settle(others, part_recv.at[0])
    save_tok = pltpu.make_async_copy(tok_v, tok_o, save_sem.at[0])
    save_tok.start()
    gain, shift = gain_one[...], shift_one[...]

    @pl.loop(0, plan.rows * share)
    def _(b):
        r, first = lax.div(b, share), pl.multiple_of(lax.rem(b, share) * part, part)
        values = tok_v[r, pl.ds(first, part)].astype(F32)
        one_v[pl.ds(pl.multiple_of(b * part, part), part)] = norm_rows(values, gain, shift).astype(BF)

    settle(seg_v, seg_recv.at[0])
    labels = []
    for r in range(plan.rows):
        row = at.m * plan.group_rows + (own * at.k + r if r < own else own * share)
        line = seg_v[lax.div(row, plan.rows_dev), pl.ds(lax.rem(row, plan.rows_dev), 1)]
        if r == own:
            turned = line
            for e in range(1, share):
                moved = jnp.concatenate([line[:, e * part :], line[:, : e * part]], axis=1)
                turned = jnp.where(at.k == e, moved, turned)
            line = turned
        seg_o[pl.ds(r, 1)] = line
    label_columns(seg_o, plan.rows, columns)
    for src, dst, i in biases:
        settle(dst, bias_recv.at[i])

    gat.arrived(0)
    load_q = pltpu.make_async_copy(g0, wq_v, load_sem.at[0])
    load_q.start()
    load_q.wait()

    def attend_shard(s, take):
        take(0)
        projected = jnp.dot(one_v[...], wq_v[s], preferred_element_type=F32) + bq_v[s]
        proj_v[s] = projected.astype(BF)
        take(1)

        def attend(r, first, amount):
            allowed = same_image(seg_o, columns, r, amount)
            keys = pl.ds(pl.multiple_of(r * seq, seq), seq)
            for h in range(heads):
                col = h * 3 * HEAD_DIM
                query = proj_v[s, pl.ds(first, amount), col : col + HEAD_DIM]
                key = proj_v[s, keys, col + HEAD_DIM : col + 2 * HEAD_DIM]
                value = proj_v[s, keys, col + 2 * HEAD_DIM : col + 3 * HEAD_DIM]
                probs = probs_of(key, query, allowed).astype(BF)
                mixed = lax.dot_general(probs, value, DOWN, preferred_element_type=F32)
                attn_v[s, pl.ds(first, amount), h * HEAD_DIM : (h + 1) * HEAD_DIM] = mixed.astype(BF)

        for r in range(own):
            attend(r, r * seq, seq)
            take(2 + r)
        attend(own, own * seq, part)

    rest = []
    for w, done in ((2, 3), (3, 1), (1, 0)):
        steps = [hop[w][s : s + 1] + (after[w][s - 1 : s] if s else []) for s in range(done, hops)]
        rest.append(steps + [after[w][hops - 1 :]])
    rest.append([[part_of(cots.start, j)] for j in range(plan.groups)])
    moves = []
    for at_once in itertools.zip_longest(*rest):
        moves += [thunks for thunks in at_once if thunks]
    points = 2 + own
    tables = [{} for _ in range(points)]
    for j, thunks in spread_over(points * n, moves).items():
        tables[j % points][j // points] = [thunk for some in thunks for thunk in some]
    run(n, attend_shard, *tables)
    save_proj = pltpu.make_async_copy(proj_v, proj_o, save_sem.at[1])
    save_proj.start()
    save_attn = pltpu.make_async_copy(attn_v, attn_o, save_sem.at[2])
    save_attn.start()

    gat.arrived(1)
    load_o = pltpu.make_async_copy(g1, wo_v, load_sem.at[0])
    load_o.start()
    load_o.wait()
    bias, gain, shift = out_bias[...], gain_two[...], shift_two[...]

    def branch(first, amount, values):
        rows = pl.ds(first, amount)
        total = values.astype(F32) + bias
        for s in range(n):
            total = total + jnp.dot(attn_v[s, rows], wo_v[s], preferred_element_type=F32)
        hid_v[rows] = total
        two_v[rows] = norm_rows(total, gain, shift).astype(BF)

    @pl.loop(0, own)
    def _(r):
        branch(pl.multiple_of(r * seq, seq), seq, tok_v[r])

    branch(own * seq, part, tok_v[own, :part])

    save_hid = pltpu.make_async_copy(hid_v, hid_o, save_sem.at[3])
    save_hid.start()
    save_two = pltpu.make_async_copy(two_v, two_o, save_sem.at[4])
    save_two.start()
    gat.arrived(2)
    load_u = pltpu.make_async_copy(g2, wu_v, load_sem.at[0])
    load_u.start()
    load_u.wait()

    def feed_shard(s, take):
        pre = jnp.dot(two_v[...], wu_v[s], preferred_element_type=F32) + bu_v[s]
        below = 0.5 * (1.0 + lax.erf(pre * math.sqrt(0.5)))
        density = jnp.exp(-0.5 * pre * pre) * (1.0 / math.sqrt(2.0 * math.pi))
        act_v[s] = (pre * below).astype(BF)
        der_v[s] = below + pre * density

        pltpu.make_async_copy(act_v.at[s], act_o.at[s], act_sem.at[0]).start()
        pltpu.make_async_copy(der_v.at[s], der_o.at[s], act_sem.at[1]).start()

    run(n, feed_shard)
    gat.arrived(3)
    for w in range(4):
        gat.finish(w)
    tokens.finish()
    settle(others, part_send.at[0])
    cots.arrived()
    cots.finish()
    for src, dst, i in biases:
        settle(dst.at[pl.ds(0, n - 1)], bias_send.at[i])
    settle(seg_v.at[pl.ds(0, share - 1)], seg_send.at[0])
    for save in (save_tok, save_proj, save_attn, save_hid, save_two):
        save.wait()
    settle(act_v, act_sem.at[0])
    settle(der_v, act_sem.at[1])


def forward(plan, tokens_in, cotangent, segment_ids, biases, weights, vectors):
    n, share = plan.mp, plan.share
    width = tokens_in.shape[2]
    held, every = plan.own * plan.seq + plan.part, plan.rows * plan.seq
    any_space = pl.BlockSpec(memory_space=pl.ANY)
    in_vmem = pl.BlockSpec(memory_space=pltpu.VMEM)
    dma = pltpu.SemaphoreType.DMA
    rows = ((plan.rows, plan.seq, width), BF)
    heads = weights[1].shape[0] // HEAD_DIM
    local, three, ff = weights[1].shape[0], weights[0].shape[1], weights[2].shape[1]
    full = [((n,) + w.shape, BF) for w in weights]
    proj, attn = ((n, every, three), BF), ((n, held, local), BF)
    hid, two = ((held, width), F32), ((held, width), BF)
    act, der = ((n, held, ff), BF), ((n, held, ff), F32)
    outs = [rows, rows, ((plan.rows, plan.seq), jnp.int32), *full, proj, attn, hid, two, act, der]
    return pl.pallas_call(
        functools.partial(forward_kernel, plan, heads),
        out_shape=[jax.ShapeDtypeStruct(*o) for o in outs],
        in_specs=[any_space] * 9 + [in_vmem] * 5,
        out_specs=[any_space] * 2 + [in_vmem] + [any_space] * 10,
        scratch_shapes=[
            pltpu.VMEM(*rows), pltpu.VMEM((every, width), BF), pltpu.VMEM(*full[0]), pltpu.VMEM(*proj),
            pltpu.VMEM(*attn), pltpu.VMEM(*full[1]), pltpu.VMEM(*hid), pltpu.VMEM(*two), pltpu.VMEM(*full[2]),
            pltpu.VMEM(*act), pltpu.VMEM(*der), pltpu.VMEM((share,) + segment_ids.shape, jnp.int32),
            pltpu.VMEM((plan.rows, plan.seq, 128), F32),
            *[pltpu.VMEM((n,) + b.shape, F32) for b in biases],
            dma((plan.groups, share, 2)), dma((2,)), dma((plan.groups, share, 2)), dma((2,)), dma((1,)), dma((1,)),
            dma((2,)), dma((2,)), dma((1,)), dma((1,)), dma((1,)), dma((5,)), dma((2,)), *gatherer_sems(plan, 4),
        ],
        compiler_params=pltpu.CompilerParams(
            collective_id=0, has_side_effects=True, vmem_limit_bytes=58 << 20
        ),
        name="forward",
    )(tokens_in, cotangent, segment_ids, *biases, *weights, *vectors)


class Reducer:
    def __init__(self, plan, at, stage, loc, sbl, yrc, slot, wide, fin, grp, out, sems):
        self.plan, self.at, self.stage, self.wide = plan, at, stage, wide
        self.loc, self.sbl, self.yrc, self.slot, self.fin, self.grp, self.out = loc, sbl, yrc, slot, fin, grp, out
        (
            self.sib_send, self.sib_recv, self.y_send, self.y_recv, self.ring_send, self.ring_recv,
            self.grp_send, self.grp_recv, self.fin_send, self.fin_recv, self.out_sem, self.credit,
        ) = sems
        hops = plan.hops
        self.order = [(0, hops)] + [(way, dist) for dist in range(hops - 1, 0, -1) for way in range(2)] + [(0, 0)]

    def target(self, i):
        n, hops = self.plan.mp, self.plan.hops
        dist = hops - lax.div(i + 1, 2)
        up = jnp.where(i == 0, 1, lax.rem(i, 2))
        return self.plan.ring_at(self.at.p + dist * up + (n - dist) * (1 - up))

    def give(self, u, yy, i):
        at, t = self.at, self.target(i)
        src = self.stage[u].at[2 * yy + 1 - at.core]
        return remote(src, self.sbl[u].at[yy, t], self.sib_send.at[u], self.sib_recv.at[u, i, yy], dp=at.sib)

    def begin(self, u, i):
        at, t = self.at, self.target(i)
        rows = self.stage[u].shape[1]
        for yy in range(2):
            self.give(u, yy, i).start()
        size = 32 if rows % 32 == 0 else rows
        for yy in range(2):

            @pl.loop(0, rows // size)
            def _(b):
                inner = pl.ds(pl.multiple_of(b * size, size), size)
                self.loc[u][yy, t, inner] = self.stage[u][2 * yy + at.core, inner]

    def given(self, u):
        settle(self.stage[u].at[pl.ds(0, 2)], self.sib_send.at[u])

    def clear(self, u):
        for way in range(2):
            part = half_of(self.slot[u].at[way, 0], 1 - way)
            part[...] = jnp.zeros(part.shape, BF)

    def wide_clear(self):
        for way in range(2):
            for yy in range(2):
                part = half_of(self.wide.at[way, 0, yy], 1 - way)
                part[...] = jnp.zeros(part.shape, BF)

    def add(self, u, yy, t, extra, put):
        rows = self.loc[u].shape[2]
        size = 32 if rows % 32 == 0 else rows

        def block(b):
            inner = pl.ds(pl.multiple_of(b * size, size), size)
            total = self.loc[u][yy, t, inner].astype(F32) + self.sbl[u][yy, t, inner].astype(F32)
            for ref in extra:
                total = total + ref[inner].astype(F32)
            put(inner, total)

        pl.loop(0, rows // size)(block)

    def cross(self, u, i):
        at, t = self.at, self.target(i)
        return remote(self.loc[u].at[1 - at.y, t], self.yrc[u].at[t], self.y_send.at[u], self.y_recv.at[u, i], dp=at.other)

    def first(self, u, i):
        at, t = self.at, self.target(i)
        self.give(u, 1 - at.y, i).wait_recv()

        def put(inner, total):
            self.loc[u][1 - at.y, t, inner] = total.astype(BF)

        self.add(u, 1 - at.y, t, (), put)
        self.cross(u, i).start()

    def hop(self, u, way, s, t):
        src = self.loc[u].at[self.at.y, t]
        dst = self.slot[u].at[way, s]
        if s == 0:
            src, dst = half_of(src, way), half_of(dst, way)
        return remote(
            src, dst, self.ring_send.at[u, way], self.ring_recv.at[u, way, s], mp=self.at.neighbour[way]
        )

    def step(self, u, i):
        at, t = self.at, self.target(i)
        way, dist = self.order[i]
        s = self.plan.hops - dist
        self.give(u, at.y, i).wait_recv()
        self.cross(u, i).wait_recv()
        extra = [self.yrc[u].at[t]]
        ways = (0, 1) if dist in (0, self.plan.hops) else (way,)
        if s > 0:
            for v in ways:
                self.hop(u, v, s - 1, t).wait_recv()
                extra.append(self.slot[u].at[v, s - 1])
        rows = self.loc[u].shape[2]
        quads = self.plan.dp // 4

        def put(inner, total):
            if dist:
                self.loc[u][at.y, t, inner] = total.astype(BF)
            elif quads > 1:
                self.grp[u][lax.div(at.d, 4), inner] = total.astype(BF)
            else:
                to = pl.ds(pl.multiple_of(at.quarter * rows + inner.start, inner.size), inner.size)
                self.fin[u][to] = total.astype(BF)

        self.add(u, at.y, t, extra, put)
        if dist:
            for v in ways:
                self.hop(u, v, s, t).start()
        else:
            for other in range(1, quads):
                self.between(u, other).start()

    def wide_hop(self, u, way, s, t):
        src, dst = self.loc[u].at[:, t], self.wide.at[way, s]
        if s == 0:
            half = self.wide.shape[-1] // 2
            src, dst = (ref.at[:, :, pl.ds(way * half, half)] for ref in (src, dst))
        return remote(
            src, dst, self.ring_send.at[u, way], self.ring_recv.at[u, way, s], mp=self.at.neighbour[way]
        )

    def wide_cross(self, u):
        mine, theirs = self.yrc[u].at[pl.ds(2, 2)], self.yrc[u].at[pl.ds(0, 2)]
        return remote(mine, theirs, self.y_send.at[u], self.y_recv.at[u, 0], dp=self.at.other)

    def wide_step(self, u, i):
        at, t = self.at, self.target(i)
        way, dist = self.order[i]
        s = self.plan.hops - dist
        ways = (0, 1) if dist in (0, self.plan.hops) else (way,)
        for yy in range(2):
            self.give(u, yy, i).wait_recv()
        if s > 0:
            for v in ways:
                self.wide_hop(u, v, s - 1, t).wait_recv()
        for yy in range(2):
            extra = [self.wide.at[v, s - 1, yy] for v in ways] if s > 0 else []

            def put(inner, total):
                if dist:
                    self.loc[u][yy, t, inner] = total.astype(BF)
                else:
                    self.yrc[u][2 + yy, inner] = total.astype(BF)

            self.add(u, yy, t, extra, put)
        if dist:
            for v in ways:
                self.wide_hop(u, v, s, t).start()
        else:
            self.wide_cross(u).start()

    def wide_last(self, u):
        at, quads = self.at, self.plan.dp // 4
        rows = self.loc[u].shape[2]
        self.wide_cross(u).wait_recv()
        for yy in range(2):
            to = pl.ds(pl.multiple_of((2 * yy + at.core) * rows, rows), rows)
            total = self.yrc[u][yy].astype(F32) + self.yrc[u][2 + yy].astype(F32)
            if quads > 1:
                self.grp[u][lax.div(at.d, 4), yy] = total.astype(BF)
            else:
                self.fin[u][to] = total.astype(BF)
        if quads > 1:
            for other in range(1, quads):
                self.between(u, other).start()
            settle(self.grp[u].at[pl.ds(0, quads - 1)], self.grp_recv.at[u])
            for yy in range(2):
                to = pl.ds(pl.multiple_of((2 * yy + at.core) * rows, rows), rows)
                total = self.grp[u][0, yy].astype(F32)
                for other in range(1, quads):
                    total = total + self.grp[u][other, yy].astype(F32)
                self.fin[u][to] = total.astype(BF)
        for what in range(2):
            self.wide_out(u, what).start()

    def wide_out(self, u, what):
        block = piece(self.fin[u], 2 * what + self.at.core)
        return remote(block, block, self.fin_send.at[u, what], self.fin_recv.at[u, what], dp=self.at.sib)

    def wide_sent(self, u):
        hops = self.plan.hops
        settle(self.yrc[u].at[pl.ds(0, 2)], self.y_send.at[u])
        for way in range(2):
            settle(self.wide.at[way, pl.ds(0, hops - 1)], self.ring_send.at[u, way])
            half = self.wide.shape[-1] // 2
            settle(self.wide.at[way, 0, :, :, pl.ds(0, half)], self.ring_send.at[u, way])

    def between(self, u, other):
        at = self.at
        to = lax.rem(at.d + 4 * other, self.plan.dp)
        block = self.grp[u].at[lax.div(at.d, 4)]
        return remote(block, block, self.grp_send.at[u], self.grp_recv.at[u], dp=to)

    def share_out(self, u, what):
        at = self.at
        quarter = at.quarter if what != 1 else 2 - 2 * at.y + at.core
        block = piece(self.fin[u], quarter)
        to = at.other if what == 2 else at.sib
        return remote(block, block, self.fin_send.at[u, what], self.fin_recv.at[u, what], dp=to)

    def last(self, u):
        quads = self.plan.dp // 4
        if quads > 1:
            rows = self.loc[u].shape[2]
            settle(self.grp[u].at[pl.ds(0, quads - 1)], self.grp_recv.at[u])
            total = self.grp[u][0].astype(F32)
            for other in range(1, quads):
                total = total + self.grp[u][other].astype(F32)
            self.fin[u][pl.ds(pl.multiple_of(self.at.quarter * rows, rows), rows)] = total.astype(BF)
        self.share_out(u, 2).start()
        self.share_out(u, 0).start()

    def spread(self, u):
        self.share_out(u, 2).wait_recv()
        self.share_out(u, 1).start()

    def write(self, u, dst, wide=False):
        for what in range(2):
            (self.wide_out if wide else self.share_out)(u, what).wait_recv()
        rows = self.loc[u].shape[2]

        @pl.loop(0, 4)
        def _(q):
            at = pl.ds(pl.multiple_of(q * rows, rows), rows)
            slot = lax.rem(q, 2)

            @pl.when(q > 1)
            def _():
                settle(self.out.at[slot], self.out_sem.at[slot])

            self.out[slot] = self.fin[u][at].astype(F32)
            begun = 0
            for ref in dst:
                size = ref.shape[0] // 4
                pltpu.make_async_copy(
                    self.out.at[slot, pl.ds(begun, size)],
                    ref.at[pl.ds(pl.multiple_of(q * size, size), size)],
                    self.out_sem.at[slot],
                ).start()
                begun += size

        for slot in range(2):
            settle(self.out.at[slot], self.out_sem.at[slot])

    def sent(self, u):
        hops = self.plan.hops
        settle(self.loc[u].at[0], self.y_send.at[u])
        for way in range(2):
            settle(self.slot[u].at[way, pl.ds(0, hops - 1)], self.ring_send.at[u, way])
            settle(half_of(self.slot[u].at[way, 0], way), self.ring_send.at[u, way])

    def release(self, u):
        at = self.at
        self.sent(u)
        for to in ({"dp": at.sib}, {"dp": at.other}, {"mp": at.neighbour[0]}, {"mp": at.neighbour[1]}):
            pl.semaphore_signal(self.credit, inc=1, device_id=to, device_id_type=MESH)

    def claim(self):
        pl.semaphore_wait(self.credit, 4)

    def finish(self, u, wide=False):
        for what in range(2 if wide else 3):
            (self.wide_out if wide else self.share_out)(u, what).wait_send()
        for other in range(1, self.plan.dp // 4):
            self.between(u, other).wait_send()


class RowsOut:
    def __init__(self, plan, at, src, shared, dst, send, recv):
        self.plan, self.at, self.src, self.shared, self.dst, self.send, self.recv = plan, at, src, shared, dst, send, recv
        self.home = at.base + lax.div(at.m, plan.groups)
        self.first = lax.rem(at.m, plan.groups) * plan.group_rows

    def copies(self, what):
        plan, at = self.plan, self.at
        for q in range(plan.mp):
            here = jnp.logical_and(self.home == at.d, at.m == q)
            toks = pl.ds(q * plan.tok, plan.tok)
            if what == 0:
                yield q, here, True, self.src.at[pl.ds(0, plan.own), toks], self.dst.at[
                    pl.ds(self.first + plan.own * at.k, plan.own)
                ]
            else:
                holds = at.k == (q * plan.tok) // plan.part
                yield q, here, holds, self.shared.at[pl.ds((q * plan.tok) % plan.part, plan.tok)], self.dst.at[
                    self.first + plan.own * plan.share
                ]

    def start(self, what, only=None):
        for q, here, wanted, src, dst in self.copies(what):
            if only is not None and only != q:
                continue

            @pl.when(jnp.logical_and(here, wanted))
            def _():
                pltpu.make_async_copy(src, dst, self.recv.at[0]).start()

            @pl.when(jnp.logical_and(jnp.logical_not(here), wanted))
            def _():
                remote(src, dst, self.send.at[q, what], self.recv.at[0], dp=self.home, mp=q).start()

    def finish(self):
        settle(self.dst, self.recv.at[0])
        for what in range(2):
            for q, here, wanted, src, dst in self.copies(what):

                @pl.when(jnp.logical_and(jnp.logical_not(here), wanted))
                def _():
                    settle(src, self.send.at[q, what])


def backward_kernel(
    plan, heads, g0, g1, g2, g3, tok, cot, seg, proj, attn, hid, two, act, der, gain_one, shift_one, gain_two, down_bias,
    blk, tg, o0, o1, o2, o3, vout, *rest,
):
    n, share, own, part, seq = plan.mp, plan.share, plan.own, plan.part, plan.seq
    hops = plan.hops
    held, every = own * seq + part, plan.rows * seq
    width, ff, three, local = hid.shape[1], act.shape[2], proj.shape[2], attn.shape[2]
    (
        stage_a, stage_b, loc_a, loc_b, sbl_a, sbl_b, yrc_a, yrc_b, slot_b, wide_v, fin_a, fin_b, fin_c,
        grp_a, grp_b, grp_c, out_v,
    ) = rest[:17]
    sems, rest = rest[17:29], rest[29:]
    (
        grad_v, low_v, block_v, tgs, tgo, sums, ups, qbs, msg, vrc, vsum,
        load_sem, wgt_sem, blk_send, blk_recv, tg_send, tg_recv, tgs_send, tgs_recv, tgl_sem, v_send, v_recv,
    ) = rest
    at = Place(plan)
    red = Reducer(
        plan, at, (stage_a, stage_b, stage_b), (loc_a, loc_b, loc_b), (sbl_a, sbl_b, sbl_b), (yrc_a, yrc_b, yrc_b),
        (None, slot_b, slot_b), wide_v, (fin_a, fin_b, fin_c), (grp_a, grp_b, grp_c), out_v, sems,
    )
    blocks = RowsOut(plan, at, block_v, block_v.at[own], blk, blk_send, blk_recv)
    greet(plan, at, True)
    part_of = functools.partial
    count = len(red.order)
    first = [[part_of(red.first, u, i) for i in range(count)] for u in range(3)]
    step = [[part_of(red.step, u, i) for i in range(count)] for u in range(3)]
    wide = [part_of(red.wide_step, 0, i) for i in range(count)]
    when_wide = [WIDE_FIRST + i * WIDE_PACE // 4 for i in range(count)]
    red.wide_clear()
    red.clear(1)
    sums[...] = jnp.zeros(sums.shape, F32)
    blocks_held = own * share + 1

    def stream(loads, i):
        def copies(j, slot):
            t = red.target(j)
            for what, (src, dst) in enumerate(loads):
                yield pltpu.make_async_copy(src.at[t], dst.at[slot], wgt_sem.at[what, slot])

        if isinstance(i, int):
            for copy in copies(i, i % 2):
                copy.start()
            return

        @pl.when(i + 1 < n)
        def _():
            for copy in copies(i + 1, lax.rem(i + 1, 2)):
                copy.start()

        for copy in copies(i, lax.rem(i, 2)):
            copy.wait()

    def feed_forward(wd_v, wu_v, act_v, der_v, low_pre, two_v, cot_v, hid_v, sum_v):
        loads = ((g3, wd_v), (g2, wu_v), (act, act_v), (der, der_v))
        stream(loads, 0)
        small = [pltpu.make_async_copy(two, two_v, load_sem.at[0]), pltpu.make_async_copy(hid, hid_v, load_sem.at[1])]
        for r in range(plan.rows):
            extent = seq if r < own else part
            small.append(
                pltpu.make_async_copy(
                    cot.at[r, pl.ds(0, extent)], cot_v.at[pl.ds(r * seq, extent)], load_sem.at[2 + r]
                )
            )
        for copy in small:
            copy.start()
        for copy in small:
            copy.wait()

        @pl.loop(0, blocks_held)
        def _(b):
            rows = pl.ds(pl.multiple_of(b * part, part), part)
            sum_v[rows] = hid_v[rows] + down_bias[...]
            grad_v[rows] = jnp.zeros((part, width), F32)

        meet(plan, True)

        def body(i, take):
            take(0)
            stream(loads, i)
            slot = lax.rem(i, 2)
            rows = ff // 4

            @pl.when(i > 0)
            def _():
                red.given(0)
                red.given(1)

            for q in range(4):
                lhs = act_v[slot, :, q * rows : (q + 1) * rows]
                stage_a[q] = lax.dot_general(lhs, cot_v[...], DOWN, preferred_element_type=F32).astype(BF)
            red.begin(0, i)
            take(1)

            act_grad = lax.dot_general(cot_v[...], wd_v[slot], ACROSS, preferred_element_type=F32)
            low = (act_grad * der_v[slot]).astype(BF)
            low_pre[...] = low
            ups[red.target(i)] = jnp.sum(low.astype(F32), axis=0, keepdims=True)
            for q in range(4):
                lhs = low_pre[:, q * rows : (q + 1) * rows]
                stage_b[q] = lax.dot_general(lhs, two_v[...], DOWN, preferred_element_type=F32).astype(BF)
            red.begin(1, i)
            grad_v[...] += lax.dot_general(low_pre[...], wu_v[slot], ACROSS, preferred_element_type=F32)
            sum_v[...] += jnp.dot(act_v[slot], wd_v[slot], preferred_element_type=F32)

        table, middle = {}, {}
        for i in range(count - 1):
            table.setdefault(i + 1, []).append(first[1][i])
        for i in range(count):
            if when_wide[i] < n:
                middle.setdefault(when_wide[i], []).append(wide[i])
        for i in range(count - 2):
            table.setdefault(i + 2, []).append(step[1][i])
        run(n, body, table, middle)
        red.given(0)
        red.given(1)
        first[1][count - 1]()
        step[1][count - 2]()

        for r in range(plan.rows):
            extent = seq if r < own else part
            block_v[r, pl.ds(0, extent)] = sum_v[pl.ds(r * seq, extent)].astype(BF)
        for q in range(n):
            if q < BLOCKS_MID:
                blocks.start(0, q)
                blocks.start(1, q)

        @pl.loop(0, blocks_held)
        def _(b):
            rows = pl.ds(pl.multiple_of(b * part, part), part)
            hidden, grad, cot_f = hid_v[rows], grad_v[rows], cot_v[rows].astype(F32)
            unit, scale, _ = norm(hidden, gain_two[...], 0.0)
            hidden_grad = cot_f + norm_back(unit, scale, gain_two[...], grad)
            grad_v[rows] = hidden_grad
            low_v[rows] = hidden_grad.astype(BF)
            for line, value in ((2, hidden_grad), (3, grad * unit), (4, grad), (5, cot_f)):
                sums[pl.ds(line, 1)] += jnp.sum(value, axis=0, keepdims=True)


    pl.run_scoped(
        feed_forward,
        pltpu.VMEM((2,) + g3.shape[1:], BF), pltpu.VMEM((2,) + g2.shape[1:], BF), pltpu.VMEM((2, held, ff), BF),
        pltpu.VMEM((2, held, ff), F32), pltpu.VMEM((held, ff), BF), pltpu.VMEM((held, width), BF),
        pltpu.VMEM((held, width), BF), pltpu.VMEM((held, width), F32), pltpu.VMEM((held, width), F32),
    )

    def attention(wq_v, wo_v, proj_v, attn_v, head_v, three_v, tok_v, one_v, back_v, out3, columns):
        loads = ((g0, wq_v), (g1, wo_v), (proj, proj_v), (attn, attn_v))
        stream(loads, 0)
        load = pltpu.make_async_copy(tok, tok_v, load_sem.at[0])
        load.start()
        step[1][count - 1]()
        red.last(1)
        red.release(1)
        load.wait()

        @pl.loop(0, plan.rows * share)
        def _(b):
            r, start = lax.div(b, share), pl.multiple_of(lax.rem(b, share) * part, part)
            rows = pl.ds(pl.multiple_of(b * part, part), part)
            values = tok_v[r, pl.ds(start, part)].astype(F32)
            one_v[rows] = norm_rows(values, gain_one[...], shift_one[...]).astype(BF)
            back_v[rows] = jnp.zeros((part, width), F32)

        three_v[...] = jnp.zeros(three_v.shape, BF)
        label_columns(seg, plan.rows, columns)
        red.spread(1)

        def body(i, take):
            take(0)
            stream(loads, i)
            slot = lax.rem(i, 2)

            head_v[...] = lax.dot_general(low_v[...], wo_v[slot], ACROSS, preferred_element_type=F32).astype(BF)

            def attend(r, first, amount):
                allowed = same_image(seg, columns, r, amount)
                keys, queries = pl.ds(pl.multiple_of(r * seq, seq), seq), pl.ds(first, amount)
                for h in range(heads):
                    col = h * 3 * HEAD_DIM
                    query = proj_v[slot, queries, col : col + HEAD_DIM]
                    key = proj_v[slot, keys, col + HEAD_DIM : col + 2 * HEAD_DIM]
                    value = proj_v[slot, keys, col + 2 * HEAD_DIM : col + 3 * HEAD_DIM]
                    head_grad = head_v[queries, h * HEAD_DIM : (h + 1) * HEAD_DIM]
                    full = probs_of(key, query, allowed)
                    value_grad = jnp.dot(full.astype(BF), head_grad, preferred_element_type=F32)
                    probs_grad = lax.dot_general(value, head_grad, ACROSS, preferred_element_type=F32)
                    delta = jnp.sum(probs_grad * full, axis=0, keepdims=True)
                    low = (jnp.where(allowed, full * (probs_grad - delta), 0.0) * HEAD_DIM ** (-0.5)).astype(BF)
                    query_grad = lax.dot_general(low, key, DOWN, preferred_element_type=F32)
                    key_grad = jnp.dot(low, query, preferred_element_type=F32)
                    three_v[queries, col : col + HEAD_DIM] = query_grad.astype(BF)
                    three_v[keys, col + HEAD_DIM : col + 2 * HEAD_DIM] = key_grad.astype(BF)
                    three_v[keys, col + 2 * HEAD_DIM : col + 3 * HEAD_DIM] = value_grad.astype(BF)

            for r in range(own):
                attend(r, r * seq, seq)
                take(1 + r)
            attend(own, own * seq, part)

            @pl.when(i > 0)
            def _():
                red.given(2)

            @pl.when(i == 0)
            def _():
                red.claim()

            wide, narrow = three // 4, local // 4
            weight = lax.dot_general(three_v[...], one_v[...], DOWN, preferred_element_type=F32).astype(BF)
            out_weight = lax.dot_general(attn_v[slot], low_v[...], DOWN, preferred_element_type=F32).astype(BF)
            for q in range(4):
                stage_b[q, :wide] = weight[q * wide : (q + 1) * wide]
                stage_b[q, wide:] = out_weight[q * narrow : (q + 1) * narrow]
            red.begin(2, i)

            back_v[...] += lax.dot_general(three_v[...], wq_v[slot], ACROSS, preferred_element_type=F32)
            qbs[red.target(i)] = jnp.sum(three_v[...].astype(F32), axis=0, keepdims=True)

        late = max(when_wide[-1] - n + 1, 1)
        table = {3: [part_of(red.write, 1, (o1,))]}
        table.setdefault(late, []).append(part_of(red.wide_last, 0))
        table.setdefault(min(late + 2, n - 1), []).append(part_of(red.write, 0, (o0,), True))
        for i in range(count):
            if when_wide[i] >= n:
                table.setdefault(when_wide[i] - n, []).insert(0, wide[i])
        for i in range(count - 1):
            table.setdefault(i + 1, []).insert(0, first[2][i])
        middle = {i + 2: [step[2][i]] for i in range(count - 2)}
        for q in range(BLOCKS_MID, n):
            for what in range(2):
                table.setdefault((q - BLOCKS_MID) * BLOCKS_OVER // n, []).append(part_of(blocks.start, what, q))
        run(n, body, table, *[{}] * (own - 1), middle)
        red.given(2)
        first[2][count - 1]()
        step[2][count - 2]()

        def norm_block(b):
            r, start = lax.div(b, share), pl.multiple_of(lax.rem(b, share) * part, part)
            rows = pl.ds(pl.multiple_of(b * part, part), part)
            unit, scale, _ = norm(tok_v[r, pl.ds(start, part)].astype(F32), gain_one[...], 0.0)
            grad = back_v[rows]
            for line, value in ((0, grad * unit), (1, grad)):
                sums[pl.ds(line, 1)] += jnp.sum(value, axis=0, keepdims=True)
            grad = norm_back(unit, scale, gain_one[...], grad)

            @pl.when(b < blocks_held)
            def _():
                mine = pl.ds(pl.multiple_of(jnp.minimum(b, blocks_held - 1) * part, part), part)
                out3[r, pl.ds(start, part)] = (grad + grad_v[mine]).astype(BF)

            @pl.when(b >= blocks_held)
            def _():
                out3[r, pl.ds(start, part)] = grad.astype(BF)

        pl.loop(own * share, plan.rows * share)(norm_block)

        tokens = RowsOut(plan, at, out3, tgo, tg, tg_send, tg_recv)
        for e in range(share):
            src = out3.at[own, pl.ds(e * part, part)]
            if e == 0:
                pltpu.make_async_copy(src, tgs.at[0], tgl_sem.at[0]).start()
            else:
                to = at.base + lax.rem(at.k + e, share)
                remote(src, tgs.at[share - e], tgs_send.at[e], tgs_recv.at[share - e], dp=to).start()

        pl.loop(0, own * share)(norm_block)

        lines = [-(-size // 128) for size in (ff, three)]
        msg[...] = jnp.zeros(msg.shape, F32)
        for q in range(n):
            msg[q, :8, : width // n] = sums[:, q * (width // n) : (q + 1) * (width // n)]
            line = 8
            for ref, size in ((ups, ff), (qbs, three)):
                for first_col in range(0, size, 128):
                    cols = min(128, size - first_col)
                    msg[q, line : line + 1, :cols] = ref[q, :, first_col : first_col + cols]
                    line += 1
        me = at.d * n + at.m

        def one(i, carry):
            to = lax.rem(me + i, plan.all)
            e, q = lax.div(to, n), lax.rem(to, n)
            remote(msg.at[q], vrc.at[me], v_send.at[0], v_recv.at[0], dp=e, mp=q).start()
            return carry

        lax.fori_loop(1, plan.all, one, 0)
        pltpu.make_async_copy(msg.at[at.m], vrc.at[me], v_recv.at[0]).start()
        tokens.start(0)
        for e in range(1, share):
            settle(tgs.at[e], tgs_recv.at[e])
        settle(tgs.at[0], tgl_sem.at[0])
        tgo[...] = sum(tgs[e].astype(F32) for e in range(share)).astype(BF)
        tokens.start(1)
        step[2][count - 1]()
        red.last(2)
        settle(vrc, v_recv.at[0])
        vsum[...] = jnp.sum(vrc[...], axis=0)
        for e in range(1, n):
            remote(vsum, vout.at[at.m], v_send.at[1], v_recv.at[1], mp=lax.rem(at.m + e, n)).start()
        pltpu.make_async_copy(vsum, vout.at[at.m], v_recv.at[1]).start()
        red.spread(2)
        red.write(2, (o2, o3))
        for u in range(3):
            red.finish(u, u == 0)
        red.wide_sent(0)
        red.sent(2)
        for e in range(1, share):
            settle(tgs.at[0], tgs_send.at[e])
        blocks.finish()
        tokens.finish()
        settle(vout, v_recv.at[1])
        settle(vrc.at[pl.ds(0, plan.all - 1)], v_send.at[0])
        settle(vout.at[pl.ds(0, n - 1)], v_send.at[1])

    pl.run_scoped(
        attention,
        pltpu.VMEM((2,) + g0.shape[1:], BF), pltpu.VMEM((2,) + g1.shape[1:], BF), pltpu.VMEM((2, every, three), BF),
        pltpu.VMEM((2, held, local), BF), pltpu.VMEM((held, local), BF), pltpu.VMEM((every, three), BF),
        pltpu.VMEM((plan.rows, seq, width), BF), pltpu.VMEM((every, width), BF), pltpu.VMEM((every, width), F32),
        pltpu.VMEM((plan.rows, seq, width), BF), pltpu.VMEM((plan.rows, seq, 128), F32),
    )


def backward(plan, weights, tok3, cot3, seg, proj, attn, hid, two, act, der, vectors):
    n, share = plan.mp, plan.share
    held, width = hid.shape
    ff, three, local = act.shape[2], proj.shape[2], attn.shape[2]
    heads = local // HEAD_DIM
    quads, quarter = plan.dp // 4, ff // 4
    if local + three != ff:
        raise ValueError("unsupported sizes")
    any_space = pl.BlockSpec(memory_space=pl.ANY)
    in_vmem = pl.BlockSpec(memory_space=pltpu.VMEM)
    dma = pltpu.SemaphoreType.DMA
    rows = jax.ShapeDtypeStruct((plan.rows_dev, plan.tok, width), BF)
    shard = jax.ShapeDtypeStruct((ff, width), F32)
    size = 8 + -(-ff // 128) + -(-three // 128)
    size = -(-size // 8) * 8
    vec = (size, 128)
    return pl.pallas_call(
        functools.partial(backward_kernel, plan, heads),
        out_shape=[
            rows, rows, shard, shard, jax.ShapeDtypeStruct((three, width), F32), jax.ShapeDtypeStruct((local, width), F32),
            jax.ShapeDtypeStruct((n,) + vec, F32),
        ],
        in_specs=[any_space] * 6 + [in_vmem] + [any_space] * 6 + [in_vmem] * 4,
        out_specs=[any_space] * 7,
        scratch_shapes=[
            *[pltpu.VMEM((4, quarter, width), BF)] * 2,
            *[pltpu.VMEM((2, n, quarter, width), BF)] * 4,
            pltpu.VMEM((4, quarter, width), BF),
            pltpu.VMEM((n, quarter, width), BF),
            pltpu.VMEM((2, plan.hops, quarter, width), BF),
            pltpu.VMEM((2, plan.hops, 2, quarter, width), BF),
            *[pltpu.VMEM((ff, width), BF)] * 3,
            pltpu.VMEM((quads, 2) + ((quarter, width) if quads > 1 else (8, 128)), BF),
            *[pltpu.VMEM((quads,) + ((quarter, width) if quads > 1 else (8, 128)), BF)] * 2,
            pltpu.VMEM((2, quarter, width), F32),
            dma((3,)), dma((3, n, 2)), dma((3,)), dma((3, n)), dma((3, 2)), dma((3, 2, plan.hops)), dma((3,)), dma((3,)),
            dma((3, 3)), dma((3, 3)), dma((2,)), pltpu.SemaphoreType.REGULAR,
            pltpu.VMEM((held, width), F32), pltpu.VMEM((held, width), BF), pltpu.VMEM((plan.rows, plan.seq, width), BF),
            pltpu.VMEM((share, plan.part, width), BF), pltpu.VMEM((plan.part, width), BF), pltpu.VMEM((8, width), F32),
            pltpu.VMEM((n, 1, ff), F32), pltpu.VMEM((n, 1, three), F32), pltpu.VMEM((n,) + vec, F32),
            pltpu.VMEM((plan.all,) + vec, F32), pltpu.VMEM(vec, F32),
            dma((2 + plan.rows,)), dma((4, 2)), dma((n, 2)), dma((1,)), dma((n, 2)), dma((1,)), dma((share,)),
            dma((share,)), dma((1,)), dma((2,)), dma((2,)),
        ],
        compiler_params=pltpu.CompilerParams(
            collective_id=1, has_side_effects=True, vmem_limit_bytes=61 << 20
        ),
        name="backward",
    )(*weights, tok3, cot3, seg, proj, attn, hid, two, act, der, *vectors)


def probs_of(key, query, allowed):
    raw = lax.dot_general(key, query, ACROSS, preferred_element_type=F32)
    scores = jnp.where(allowed, raw * HEAD_DIM ** (-0.5), MASKED)
    raised = jnp.exp(scores - jnp.max(scores, axis=0, keepdims=True))
    return raised * (1.0 / jnp.sum(raised, axis=0, keepdims=True))


def label_columns(labels, rows, columns):
    for r in range(rows):
        line = labels[pl.ds(r, 1)].astype(F32)
        columns[r] = jnp.transpose(jnp.broadcast_to(line, (128, line.shape[1])))


def same_image(labels, columns, r, amount):
    line = labels[pl.ds(r, 1)].astype(F32)[:, :amount]
    down = columns[r]
    if amount < 128:
        return down[:, :amount] == line
    return jnp.concatenate([down] * (amount // 128), axis=1) == line


def norm(values, gain_vec, shift_vec):
    centred = values - jnp.mean(values, axis=-1, keepdims=True)
    scale = lax.rsqrt(jnp.mean(centred * centred, axis=-1, keepdims=True) + EPS)
    unit = centred * scale
    return unit, scale, unit * gain_vec + shift_vec


def norm_back(unit, scale, gain_vec, grad):
    pulled = grad * gain_vec
    inner = jnp.mean(pulled * unit, axis=-1, keepdims=True)
    return scale * (pulled - jnp.mean(pulled, axis=-1, keepdims=True) - unit * inner)


def per_device(
    plan, tokens_in, segment_ids, attn_gain, attn_shift, qkv_weight, qkv_bias, out_weight, out_bias, mlp_gain, mlp_shift,
    up_weight, up_bias, down_weight, down_bias, cotangent,
):
    n, width = plan.mp, tokens_in.shape[2]
    ff_local = up_weight.shape[1]
    heads_local = qkv_bias.shape[1] // HEAD_DIM
    parts = qkv_bias.reshape(2, heads_local, HEAD_DIM)
    bias_three = jnp.stack([parts[0], jnp.zeros_like(parts[0]), parts[1]], axis=1).reshape(1, -1)
    vectors = [v.reshape(1, width) for v in (attn_gain, attn_shift, out_bias, mlp_gain, mlp_shift)]
    tok3, cot3, seg, wq, wo, wu, wd, proj, attn, hidden, normed_two, act_low, gelu_slope = forward(
        plan, tokens_in, cotangent, segment_ids, (bias_three, up_bias.reshape(1, ff_local)),
        (qkv_weight, out_weight, up_weight, down_weight), vectors,
    )
    block_out, tokens_low, down_grad, up_grad, qkv_grad, out_grad, sums = backward(
        plan, (wq, wo, wu, wd), tok3, cot3, seg, proj, attn, hidden, normed_two, act_low, gelu_slope,
        [v.reshape(1, width) for v in (attn_gain, attn_shift, mlp_gain, down_bias)],
    )
    local, three = out_weight.shape[0], qkv_weight.shape[1]
    six = jnp.swapaxes(sums[:, :6, : width // n], 0, 1).reshape(6, width)
    mine = lax.dynamic_index_in_dim(sums, lax.axis_index("mp"), 0, keepdims=False)
    lines = [-(-size // 128) for size in (ff_local, three)]
    up_bias_grad = mine[8 : 8 + lines[0]].reshape(-1)[:ff_local]
    bias_sums = mine[8 + lines[0] : 8 + sum(lines)].reshape(-1)[:three].reshape(heads_local, 3, HEAD_DIM)
    qkv_bias_grad = jnp.stack([bias_sums[:, 0], bias_sums[:, 2]]).reshape(2, local)
    return (
        block_out, tokens_low.astype(F32), six[0], six[1], qkv_grad.T, qkv_bias_grad, out_grad, six[2], six[3], six[4],
        up_grad.T, up_bias_grad, down_grad, six[5],
    )


def solution(mesh):
    dp, mp = mesh.shape["dp"], mesh.shape["mp"]
    rows_spec = P("dp", "mp", None)
    in_specs = (
        rows_spec, P("dp", None), P(), P(), P(None, "mp"), P(None, "mp"), P("mp", None), P(), P(), P(),
        P(None, "mp"), P("mp"), P("mp", None), P(), rows_spec,
    )
    out_specs = (
        rows_spec, rows_spec, P(), P(), P(None, "mp"), P(None, "mp"), P("mp", None), P(), P(), P(),
        P(None, "mp"), P("mp"), P("mp", None), P(),
    )

    def run(tokens_in, segment_ids, *rest):
        rows_all, seq_len, _ = tokens_in.shape
        plan = Plan(dp, mp, rows_all // dp, seq_len // mp, seq_len)
        return jax.shard_map(
            functools.partial(per_device, plan), mesh=mesh, in_specs=in_specs, out_specs=out_specs, check_vma=False
        )(tokens_in, segment_ids, *rest)

    return run
```
